256 devices in a mesh: sec: 2 (over core), var: 32 (over y, z), trait: 4 (over x).
Axes of the slice: x: 4, y: 4, z: 8, core: 2. Of those that a mesh axis runs over, the one named last changes fastest.
Arguments:
- z_typed: bfloat16 [262144, 512], P(('sec', 'var'), 'trait'), may hold values from -6 to 6
- band_inverse: bfloat16 [2048, 128, 384], P(('sec', 'var')), may hold values from -0.3125 to 0.3125
- ld_untyped: bfloat16 [4096, 128, 512], P(('sec', 'var')), may hold values from -0.375 to 0.375
- trait_mix: bfloat16 [512, 512], replicated, may hold values from -0.25 to 0.25
- win_start: int32 [4096], P(('sec', 'var')), may hold values from 0 to 2047, as said below
- win_count: int32 [4096], P(('sec', 'var')), may hold values from 1 to 4, as said below
Outputs:
- imputed_mixed: bfloat16 [524288, 512], P(('sec', 'var'), 'trait')
The draws below stay inside these ranges and needn't reach their ends.
Inputs may be any that keep to these rules, and one draw needn't show every extreme that they name: Windows follow chromosome order: within the 64 untyped blocks of one index g of sec+var, win_start never falls, and every window lies in typed blocks g * 32 - 32 to (g + 1) * 32 + 31; the first window of each index starts at its lower end (or at 0) and the last one ends at its upper end (or at the chromosome's end). win_start + win_count never exceeds 2048.
All inputs are finite; a program needn't handle non-finite values.
Results may differ from the reference program's by a relative error of at most 0.0057.
Values may be sent and summed in bfloat16 or wider, within the bound.
No kernel may reach another device: no remote copies, remote signals or barrier semaphores. Data moves between devices by JAX's collectives and lax.ppermute only.
A program may use at most 64 MiB of HBM per device.

```python
import jax
import jax.numpy as jnp
from jax import lax

BLK = 128
WIN = 4
TRAITS = 512
TB_DEV = 32
UB_DEV = 64
REACH = 32
VGROUPS = 64
TYPED_BLOCKS = 2048
TYPED_ROWS = 262144
UNTYPED_BLOCKS = 4096


def window_plan(key):
    subkeys = jax.random.split(jax.random.fold_in(key, 7), VGROUPS)
    owners = jnp.arange(VGROUPS, dtype=jnp.int32)
    span = TB_DEV + 2 * REACH - WIN

    def one_owner(owner_key, owner):
        first_key, second_key = jax.random.split(owner_key, 2)
        lowest = owner * TB_DEV - REACH
        offsets = jnp.sort(jax.random.randint(first_key, (UB_DEV,), 0, span + 1))
        offsets = offsets.at[0].set(0).at[UB_DEV - 1].set(span)
        counts = jax.random.randint(second_key, (UB_DEV,), 1, WIN + 1)
        counts = counts.at[0].set(WIN).at[UB_DEV - 1].set(WIN)
        starts = jnp.clip(lowest + offsets, 0, TYPED_BLOCKS - 1)
        counts = jnp.minimum(counts, TYPED_BLOCKS - starts)
        return (starts, counts)
    starts, counts = jax.vmap(one_owner)(subkeys, owners)
    return (starts.reshape(-1).astype(jnp.int32), counts.reshape(-1).astype(jnp.int32))


def draw_win_start(key, part):
    return window_plan(key)[0]


def draw_win_count(key, part):
    return window_plan(key)[1]


def block_levels(own_key, extent, cuts, low, top_value):
    loudness = 1.0
    for axis_at, blocks in cuts:
        heights = jax.random.uniform(jax.random.fold_in(jax.random.fold_in(own_key, 6), axis_at), (blocks,), jnp.float32, low / len(cuts), top_value / len(cuts))
        loudness = loudness * jnp.repeat(jnp.exp(heights), extent[axis_at] // blocks).reshape((-1,) + (1,) * (len(extent) - 1 - axis_at))
    return loudness


def gaussian(key, shape, deviation, limit, shards=(), kind=jnp.bfloat16):
    values = jax.random.normal(key, shape, jnp.float32) * deviation
    if len(shards) > 0:
        values = block_levels(key, shape, shards, -0.22, 0.18) * values
    return jnp.clip(values, min=-limit, max=limit).astype(kind)


def setup_inputs(seed: int = 0) -> dict:
    streams_of = jax.random.split(jax.random.key(seed), 7)
    return {
        "z_typed": gaussian(streams_of[0], (TYPED_ROWS, TRAITS), 1.0, 6.0, ((0, 64), (1, 4))),
        "band_inverse": gaussian(streams_of[1], (TYPED_BLOCKS, BLK, 3 * BLK), (3 * BLK) ** -0.5, 0.3125, ((0, 64),)),
        "ld_untyped": gaussian(streams_of[2], (UNTYPED_BLOCKS, BLK, WIN * BLK), (2 * BLK) ** -0.5, 0.375, ((0, 64),)),
        "trait_mix": gaussian(streams_of[3], (TRAITS, TRAITS), TRAITS ** -0.5, 0.25),
        "win_start": draw_win_start(jax.random.fold_in(streams_of[6], 71), 0),
        "win_count": draw_win_count(jax.random.fold_in(streams_of[6], 71), 0),
    }


def whiten(z_typed, band_inverse):
    blocks = z_typed.shape[0] // BLK
    padded = jnp.pad(z_typed, ((BLK, BLK), (0, 0)))
    stacked = jnp.concatenate([padded[k * BLK:(k + blocks) * BLK].reshape(blocks, BLK, z_typed.shape[1]) for k in range(3)], axis=1)
    return jnp.einsum("bij,bjc->bic", band_inverse.astype(jnp.float32), stacked.astype(jnp.float32)).astype(jnp.bfloat16)


def reference(z_typed, band_inverse, ld_untyped, trait_mix, win_start, win_count):
    whitened = whiten(z_typed, band_inverse)
    mixed = jnp.dot(whitened.reshape(TYPED_ROWS, TRAITS), trait_mix, preferred_element_type=jnp.float32).astype(jnp.bfloat16)
    mixed = mixed.reshape(TYPED_BLOCKS, BLK, TRAITS)
    window_steps = jnp.arange(WIN, dtype=jnp.int32)

    def impute(inputs):
        ld_group, starts, counts = inputs
        wanted = (starts[:, None] + window_steps[None, :]).astype(jnp.int32)
        usable = window_steps[None, :] < counts[:, None]
        picked = mixed[jnp.clip(wanted, 0, TYPED_BLOCKS - 1)]
        picked = jnp.where(usable[:, :, None, None], picked, jnp.zeros_like(picked))
        picked = picked.reshape(picked.shape[0], WIN * BLK, TRAITS)
        return jnp.einsum("uij,ujc->uic", ld_group.astype(jnp.float32), picked.astype(jnp.float32)).astype(jnp.bfloat16)

    grouped = (ld_untyped.reshape(VGROUPS, UB_DEV, BLK, WIN * BLK), win_start.reshape(VGROUPS, UB_DEV), win_count.reshape(VGROUPS, UB_DEV))
    imputed = lax.map(impute, grouped)
    return imputed.reshape(UNTYPED_BLOCKS * BLK, TRAITS)
```

```python
import functools

import jax
import jax.numpy as jnp
import numpy as np
from jax import lax
from jax.experimental import pallas as pl
from jax.experimental.pallas import tpu as pltpu
from jax.sharding import PartitionSpec as P

BLK = 128
WIN = 4
COLS = 128
TB = 32
UB = 64
BF = jnp.bfloat16
F32 = jnp.float32
ROWS = ("sec", "var")
ANY = pl.BlockSpec(memory_space=pl.ANY)
HBM = pl.BlockSpec(memory_space=pltpu.HBM)
SMEM = pl.BlockSpec(memory_space=pltpu.SMEM)
VM = pl.BlockSpec(memory_space=pltpu.VMEM)
PARAMS = pltpu.CompilerParams(vmem_limit_bytes=40 * 1024 * 1024)


def shaped(rows, dtype=BF):
    return jax.ShapeDtypeStruct((rows, COLS), dtype)


def dot(left, right):
    return jnp.dot(left, right, preferred_element_type=F32)


def whiten_mid(place, z, band, mix, w_a, w_b, first, last, mix_a, mix_b, zs, bs, sems):
    zcopy = pltpu.make_async_copy(z.at[pl.ds(7 * BLK, 18 * BLK)], zs, sems.at[0])
    zcopy.start()
    bands = []
    for k in range(4):
        bands.append(
            pltpu.make_async_copy(band.at[pl.ds(8 + 4 * k, 4)], bs.at[pl.ds(4 * k, 4)], sems.at[1 + k])
        )
        bands[-1].start()
    others = [
        pltpu.make_async_copy(z.at[pl.ds(0, BLK)], first, sems.at[5]),
        pltpu.make_async_copy(z.at[pl.ds((TB - 1) * BLK, BLK)], last, sems.at[6]),
    ]
    t, a, b = place[0], place[1], place[2]
    n = 7
    for target, near, far in ((mix_a, a, b), (mix_b, b, a)):
        for i, row in enumerate((t, near)):
            for j, col in enumerate((t, far)):
                source = mix.at[
                    pl.ds(pl.multiple_of(row * COLS, COLS), COLS), pl.ds(pl.multiple_of(col * COLS, COLS), COLS)
                ]
                others.append(
                    pltpu.make_async_copy(
                        source, target.at[pl.ds(i * COLS, COLS), pl.ds(j * COLS, COLS)], sems.at[n]
                    )
                )
                n += 1
    for copy in others:
        copy.start()
    zcopy.wait()
    for k in range(4):
        bands[k].wait()
        for i in range(4 * k, 4 * k + 4):
            rows = dot(bs[i], zs[pl.ds(i * BLK, 3 * BLK), :]).astype(BF)
            if i < 8:
                w_a[pl.ds(i * BLK, BLK), :] = rows
            else:
                w_b[pl.ds((i - 8) * BLK, BLK), :] = rows
    for copy in others:
        copy.wait()


def whiten_edge(place, z, band, from_left, from_right, w_a, w_b, zs, bs, sems):
    copies = [
        pltpu.make_async_copy(z.at[pl.ds(0, 9 * BLK)], zs.at[pl.ds(BLK, 9 * BLK)], sems.at[0]),
        pltpu.make_async_copy(z.at[pl.ds(23 * BLK, 9 * BLK)], zs.at[pl.ds(10 * BLK, 9 * BLK)], sems.at[1]),
    ]
    for k in range(2):
        copies.append(
            pltpu.make_async_copy(band.at[pl.ds(24 * k, 8)], bs.at[pl.ds(8 * k, 8)], sems.at[2 + k])
        )
    for copy in copies:
        copy.start()
    nothing = jnp.zeros((BLK, COLS), BF)
    zs[pl.ds(0, BLK), :] = jnp.where(place[3] == 0, nothing, from_left[...])
    zs[pl.ds(19 * BLK, BLK), :] = jnp.where(place[3] == place[4] - 1, nothing, from_right[...])
    for copy in copies:
        copy.wait()
    for i in range(8):
        w_a[pl.ds(i * BLK, BLK), :] = dot(bs[i], zs[pl.ds(i * BLK, 3 * BLK), :]).astype(BF)
        w_b[pl.ds(i * BLK, BLK), :] = dot(bs[8 + i], zs[pl.ds((10 + i) * BLK, 3 * BLK), :]).astype(BF)


def partial_sums(w_a, got_a, w_b, got_b, mix_a, mix_b, send_a, send_b, own):
    rows = w_a.shape[0]
    for k, (w, got, mix, send) in enumerate(((w_a, got_a, mix_a, send_a), (w_b, got_b, mix_b, send_b))):
        sums = dot(w[...], mix[pl.ds(0, COLS), :]) + dot(got[...], mix[pl.ds(COLS, COLS), :])
        own[pl.ds(k * rows, rows), :] = sums[:, :COLS]
        send[...] = sums[:, COLS:].astype(BF)


def combine(own, got_a, got_b, out):
    rows = got_a.shape[0]
    out[pl.ds(0, rows), :] = (own[pl.ds(0, rows), :] + got_a[...].astype(F32)).astype(BF)
    out[pl.ds(rows, rows), :] = (own[pl.ds(rows, rows), :] + got_b[...].astype(F32)).astype(BF)


GROUP = 8


def impute(place, starts, counts, own1, own2, l1, l2, r1, r2, ld, out, ext, sems):
    step = pl.program_id(0)

    @pl.when(step == 0)
    def _():
        copies = []
        for k, (mid, edge) in enumerate(((l1, l2), (own1, own2), (r1, r2))):
            at = 32 * k * BLK
            copies.append(pltpu.make_async_copy(edge.at[pl.ds(0, 8 * BLK)], ext.at[pl.ds(at, 8 * BLK)], sems.at[3 * k]))
            copies.append(pltpu.make_async_copy(mid, ext.at[pl.ds(at + 8 * BLK, 16 * BLK)], sems.at[3 * k + 1]))
            copies.append(
                pltpu.make_async_copy(
                    edge.at[pl.ds(8 * BLK, 8 * BLK)], ext.at[pl.ds(at + 24 * BLK, 8 * BLK)], sems.at[3 * k + 2]
                )
            )
        for copy in copies:
            copy.start()
        ext[pl.ds(96 * BLK, 3 * BLK), :] = jnp.zeros((3 * BLK, COLS), BF)
        for copy in copies:
            copy.wait()

    lowest = place[3] * TB - TB
    for i in range(GROUP):
        u = step * GROUP + i
        at = jnp.clip(starts[u] - lowest, 0, 95)
        count = counts[u]
        rows = ld[i]
        kept = [rows[:, :BLK]]
        for s in range(1, WIN):
            part = rows[:, s * BLK : (s + 1) * BLK]
            kept.append(jnp.where(s < count, part, jnp.zeros_like(part)))
        window = ext[pl.ds(pl.multiple_of(at * BLK, BLK), WIN * BLK), :]
        out[pl.ds(i * BLK, BLK), :] = dot(jnp.concatenate(kept, axis=1), window).astype(BF)


def on_device(z, band, ld, mix, starts, counts):
    t = lax.axis_index("trait")
    g = lax.axis_index(ROWS)
    owners = lax.axis_size(ROWS)
    lane = lax.iota(jnp.int32, 8)
    place = jnp.where(
        lane == 0, t, jnp.where(lane == 1, t ^ 1, jnp.where(lane == 2, 3 - t, jnp.where(lane == 3, g, owners)))
    ).astype(jnp.int32)
    pair_a = [(i, i ^ 1) for i in range(4)]
    pair_b = [(i, 3 - i) for i in range(4)]
    to_right = [(i, (i + 1) % owners) for i in range(owners)]
    to_left = [((i + 1) % owners, i) for i in range(owners)]

    w1a, w1b, first, last, mix_a, mix_b = pl.pallas_call(
        whiten_mid,
        name="whiten_mid",
        out_shape=(
            shaped(1024),
            shaped(1024),
            shaped(BLK),
            shaped(BLK),
            jax.ShapeDtypeStruct((256, 256), BF),
            jax.ShapeDtypeStruct((256, 256), BF),
        ),
        in_specs=[SMEM, HBM, HBM, HBM],
        out_specs=(VM,) * 6,
        scratch_shapes=[
            pltpu.VMEM((18 * BLK, COLS), BF),
            pltpu.VMEM((16, BLK, 3 * BLK), BF),
            pltpu.SemaphoreType.DMA((15,)),
        ],
        compiler_params=PARAMS,
    )(place, z, band, mix)

    def exchange(w_a, w_b, pairs):
        return lax.ppermute(w_a, "trait", pairs[0]), lax.ppermute(w_b, "trait", pairs[1])

    def mixing(w_a, w_b, got_a, got_b):
        rows = w_a.shape[0]
        return pl.pallas_call(
            partial_sums,
            name="partial_sums",
            out_shape=(shaped(rows), shaped(rows), shaped(2 * rows, F32)),
            in_specs=[VM] * 6,
            out_specs=(VM,) * 3,
            compiler_params=PARAMS,
        )(w_a, got_a, w_b, got_b, mix_a, mix_b)

    def combined(own, got_a, got_b):
        return pl.pallas_call(
            combine,
            name="combine",
            out_shape=shaped(own.shape[0]),
            in_specs=[VM] * 3,
            out_specs=VM,
            compiler_params=PARAMS,
        )(own, got_a, got_b)

    got1a, got1b = exchange(w1a, w1b, (pair_a, pair_b))
    from_left = lax.ppermute(last, ROWS, to_right)
    from_right = lax.ppermute(first, ROWS, to_left)
    send1a, send1b, own1 = mixing(w1a, w1b, got1a, got1b)
    far1a, far1b = exchange(send1a, send1b, (pair_b, pair_a))
    from_left, from_right, send1a = lax.optimization_barrier((from_left, from_right, send1a))
    w2a, w2b = pl.pallas_call(
        whiten_edge,
        name="whiten_edge",
        out_shape=(shaped(1024), shaped(1024)),
        in_specs=[SMEM, HBM, HBM, VM, VM],
        out_specs=(VM,) * 2,
        scratch_shapes=[
            pltpu.VMEM((20 * BLK, COLS), BF),
            pltpu.VMEM((16, BLK, 3 * BLK), BF),
            pltpu.SemaphoreType.DMA((4,)),
        ],
        compiler_params=PARAMS,
    )(place, z, band, from_left, from_right)
    got2a, got2b = exchange(w2a, w2b, (pair_a, pair_b))
    mixed1 = combined(own1, far1a, far1b)
    left1 = lax.ppermute(mixed1, ROWS, to_right)
    right1 = lax.ppermute(mixed1, ROWS, to_left)
    got2a, got2b, mixed1 = lax.optimization_barrier((got2a, got2b, mixed1))
    send2a, send2b, own2 = mixing(w2a, w2b, got2a, got2b)
    far2a, far2b = exchange(send2a, send2b, (pair_b, pair_a))
    mixed2 = combined(own2, far2a, far2b)
    left2 = lax.ppermute(mixed2, ROWS, to_right)
    right2 = lax.ppermute(mixed2, ROWS, to_left)
    return pl.pallas_call(
        impute,
        name="impute",
        grid=(UB // GROUP,),
        out_shape=shaped(UB * BLK),
        in_specs=[SMEM, SMEM, SMEM] + [ANY] * 6 + [pl.BlockSpec((GROUP, BLK, WIN * BLK), lambda i: (i, 0, 0))],
        out_specs=pl.BlockSpec((GROUP * BLK, COLS), lambda i: (i, 0)),
        scratch_shapes=[pltpu.VMEM((99 * BLK, COLS), BF), pltpu.SemaphoreType.DMA((9,))],
        compiler_params=PARAMS,
    )(place, starts, counts, mixed1, mixed2, left1, left2, right1, right2, ld)


def solution(mesh):
    in_specs = (
        P(ROWS, "trait"),
        P(ROWS, None, None),
        P(ROWS, None, None),
        P(),
        P(ROWS),
        P(ROWS),
    )
    return jax.shard_map(on_device, mesh=mesh, in_specs=in_specs, out_specs=P(ROWS, "trait"), check_vma=False)
```

```python
import jax
import jax.numpy as jnp
from jax import lax
from jax.experimental import pallas as pl
from jax.experimental.pallas import tpu as pltpu
from jax.sharding import PartitionSpec as P

BLK = 128
WIN = 4
COLS = 128
TB = 32
UB = 64
EXT = 3 * TB + WIN - 1
UNROLL = 4
BF = jnp.bfloat16
F32 = jnp.float32
ROWS = ("sec", "var")
HBM = pl.BlockSpec(memory_space=pltpu.HBM)
SMEM = pl.BlockSpec(memory_space=pltpu.SMEM)
VM = pl.BlockSpec(memory_space=pltpu.VMEM)
PARAMS = pltpu.CompilerParams(vmem_limit_bytes=40 * 1024 * 1024)
MID = 8
MID_END = 24
HALF1 = (MID_END - MID) // 2
HALF2 = MID - 1


def shaped(blocks, dtype=BF):
    return jax.ShapeDtypeStruct((blocks * BLK, COLS), dtype)


def dot(left, right):
    return jnp.dot(left, right, preferred_element_type=F32)


def at(block, blocks=1):
    start = block * BLK
    return pl.ds(start if isinstance(start, int) else pl.multiple_of(start, BLK), blocks * BLK)


def copy_all(pairs, sems, first=0):
    copies = [pltpu.make_async_copy(a, b, sems.at[first + k]) for k, (a, b) in enumerate(pairs)]
    for copy in copies:
        copy.start()
    return copies


def pieces(blocks):
    return [(k, min(4, blocks - k)) for k in range(0, blocks, 4)]


def whiten_1(place, z, band, mix, w_a, w_b, halo_e, halo_o, mix_a, mix_b, zs, bs, sems):
    zcopy = copy_all([(z.at[at(MID - 1, 2 * HALF1 + 2)], zs)], sems)
    cuts = pieces(2 * HALF1)
    bands = copy_all([(band.at[pl.ds(MID + k, n)], bs.at[pl.ds(k, n)]) for k, n in cuts], sems, 1)
    t, a, b, odd = place[0], place[1], place[2], place[5]
    pairs = [(z.at[at((1 - odd) * (TB - 1))], halo_e), (z.at[at(odd * (TB - 1))], halo_o)]
    for target, near, far in ((mix_a, a, b), (mix_b, b, a)):
        for i, row in enumerate((t, near)):
            for j, col in enumerate((t, far)):
                pairs.append((mix.at[at(row), at(col)], target.at[at(i), at(j)]))
    others = copy_all(pairs, sems, 1 + len(cuts))
    zcopy[0].wait()
    for (k, n), copy in zip(cuts, bands):
        copy.wait()
        for i in range(k, k + n):
            w = w_a if i < HALF1 else w_b
            w[at(i % HALF1), :] = dot(bs[i], zs[at(i, 3), :]).astype(BF)
    for copy in others:
        copy.wait()


def whiten_2(z, band, w_a, w_b, zs, bs, sems):
    zcopies = copy_all(
        [
            (z.at[at(0, HALF2 + 2)], zs.at[at(0, HALF2 + 2)]),
            (z.at[at(MID_END - 1, HALF2 + 2)], zs.at[at(HALF2 + 2, HALF2 + 2)]),
        ],
        sems,
    )
    cuts = [(side, k, n) for side in range(2) for k, n in pieces(HALF2)]
    bands = copy_all(
        [(band.at[pl.ds((1, MID_END)[side] + k, n)], bs.at[pl.ds(side * HALF2 + k, n)]) for side, k, n in cuts], sems, 2
    )
    for (side, k, n), copy in zip(cuts, bands):
        if k == 0:
            zcopies[side].wait()
        copy.wait()
        for i in range(k, k + n):
            rows = dot(bs[side * HALF2 + i], zs[at(side * (HALF2 + 2) + i, 3), :])
            (w_a, w_b)[side][at(i), :] = rows.astype(BF)


def sums(own_rows, got_rows, mix):
    return dot(own_rows, mix[pl.ds(0, COLS), :]) + dot(got_rows, mix[pl.ds(COLS, COLS), :])


def partial_1(w_a, got_a, w_b, got_b, mix_a, mix_b, send_a, send_b, own):
    for k, (w, got, mix, send) in enumerate(((w_a, got_a, mix_a, send_a), (w_b, got_b, mix_b, send_b))):
        both = sums(w[...], got[...], mix)
        own[at(k * HALF1, HALF1), :] = both[:, :COLS]
        send[...] = both[:, COLS:].astype(BF)


def partial_2(
    place, z, band, halo_e, halo_o, w_a, got_a, w_b, got_b, mix_a, mix_b, send_a, send_b, own, zs, bs, sems
):
    copies = copy_all(
        [
            (z.at[at(0, 2)], zs.at[at(1, 2)]),
            (z.at[at(TB - 2, 2)], zs.at[at(3, 2)]),
            (band.at[0], bs.at[0]),
            (band.at[TB - 1], bs.at[1]),
        ],
        sems,
    )
    for k, (w, got, mix, send) in enumerate(((w_a, got_a, mix_a, send_a), (w_b, got_b, mix_b, send_b))):
        both = sums(w[...], got[...], mix)
        own[at(k * HALF2, HALF2), :] = both[:, :COLS]
        send[at(0, HALF2), :] = both[:, COLS:].astype(BF)
    odd = place[5] == 1
    nothing = jnp.zeros((BLK, COLS), BF)
    from_left = jnp.where(odd, halo_e[...], halo_o[...])
    from_right = jnp.where(odd, halo_o[...], halo_e[...])
    zs[at(0), :] = jnp.where(place[3] == 0, nothing, from_left)
    zs[at(5), :] = jnp.where(place[3] == place[4] - 1, nothing, from_right)
    for copy in copies:
        copy.wait()
    send_a[at(HALF2), :] = dot(bs[0], zs[at(0, 3), :]).astype(BF)
    send_b[at(HALF2), :] = dot(bs[1], zs[at(3, 3), :]).astype(BF)


def combine_1(own, far_a, far_b, out):
    for k, far in enumerate((far_a, far_b)):
        out[at(k * HALF1, HALF1), :] = (own[at(k * HALF1, HALF1), :] + far[...].astype(F32)).astype(BF)


def combine_2(own, far_a, far_b, sent_a, sent_b, mix_a, mix_b, out, send_first, send_last, own_edge):
    for k, (far, sent, mix, send) in enumerate(((far_a, sent_a, mix_b, send_first), (far_b, sent_b, mix_a, send_last))):
        both = sums(sent[at(HALF2), :], far[at(HALF2), :], mix)
        own_edge[at(k), :] = both[:, :COLS]
        send[...] = both[:, COLS:].astype(BF)
        out[at(k * HALF2, HALF2), :] = (own[at(k * HALF2, HALF2), :] + far[at(0, HALF2), :].astype(F32)).astype(BF)


def combine_edge(own, far_first, far_last, out):
    for k, far in enumerate((far_first, far_last)):
        out[at(k), :] = (own[at(k), :] + far[...].astype(F32)).astype(BF)


def to_out(u, n, out, staged, sems):
    return pltpu.make_async_copy(staged.at[n], out.at[at(u)], sems.at[n])


def on_list(index, count, starts, counts, lowest, ld, ext, out, staged, sems):
    def several(k, carry):
        for i in range(UNROLL):
            u = index[jnp.minimum(UNROLL * k + i, count - 1)]
            first = jnp.clip(starts[u] - lowest, 0, 3 * TB - 1)
            have = counts[u]
            rows = ld[u]
            kept = [rows[:, :BLK]]
            for s in range(1, WIN):
                part = rows[:, s * BLK : (s + 1) * BLK]
                kept.append(jnp.where(s < have, part, jnp.zeros_like(part)))
            staged[UNROLL * k + i] = dot(jnp.concatenate(kept, axis=1), ext[at(first, WIN), :]).astype(BF)
        for i in range(UNROLL):
            n = UNROLL * k + i

            @pl.when(n < count)
            def _():
                to_out(index[n], n, out, staged, sems).start()

        return carry

    def finish(n, carry):
        to_out(index[n], n, out, staged, sems).wait()
        return carry

    lax.fori_loop(0, (count + UNROLL - 1) // UNROLL, several, 0)
    lax.fori_loop(0, count, finish, 0)


def set_1(ext, base, mid):
    return [(mid, ext.at[at(base + MID, 2 * HALF1)])]


def set_2(ext, base, rest, edge):
    return [
        (edge.at[at(0)], ext.at[at(base)]),
        (rest.at[at(0, HALF2)], ext.at[at(base + 1, HALF2)]),
        (rest.at[at(HALF2, HALF2)], ext.at[at(base + MID_END, HALF2)]),
        (edge.at[at(1)], ext.at[at(base + TB - 1)]),
    ]


def impute_ready(
    place, starts, counts, mid, rest, edge, mid_e, mid_o, ld, ext, late, out, ready, staged, sems, out_sems
):
    base_e = 2 * TB * (1 - place[5])
    base_o = 2 * TB * place[5]
    copies = copy_all(
        set_1(ext, TB, mid) + set_2(ext, TB, rest, edge) + set_1(ext, base_e, mid_e) + set_1(ext, base_o, mid_o), sems
    )
    ext[at(3 * TB, WIN - 1), :] = jnp.zeros(((WIN - 1) * BLK, COLS), BF)
    for k in (0, MID_END, 2 * TB, 2 * TB + MID_END):
        ext[at(k, MID), :] = jnp.zeros((MID * BLK, COLS), BF)
    lowest = place[3] * TB - TB

    def sort(u, sizes):
        now, later = sizes
        first = jnp.clip(starts[u] - lowest, 0, 3 * TB - 1)
        last = first + counts[u] - 1
        waits = first < MID
        for low, high in ((MID_END, TB), (2 * TB, 2 * TB + MID), (2 * TB + MID_END, 3 * TB)):
            waits = waits | ((last >= low) & (first < high))
        waits = waits.astype(jnp.int32)
        ready[now] = u
        late[later] = u
        return now + 1 - waits, later + waits

    now, later = lax.fori_loop(0, UB, sort, (0, 0))
    late[UB + 1] = later
    for copy in copies:
        copy.wait()

    @pl.when(now > 0)
    def _():
        on_list(ready, now, starts, counts, lowest, ld, ext, out, staged, out_sems)


def impute_late(
    place, starts, counts, late, rest_e, rest_o, edge_e, edge_o, ld, before, done, ext, out, staged, sems, out_sems
):
    base_e = 2 * TB * (1 - place[5])
    base_o = 2 * TB * place[5]
    copies = copy_all(set_2(ext, base_e, rest_e, edge_e) + set_2(ext, base_o, rest_o, edge_o), sems)
    count = late[UB + 1]
    for copy in copies:
        copy.wait()

    @pl.when(count > 0)
    def _():
        on_list(late, count, starts, counts, place[3] * TB - TB, ld, ext, out, staged, out_sems)


def call(kernel, outs, ins, args, scratch=(), aliases=None):
    return pl.pallas_call(
        kernel,
        name=kernel.__name__,
        out_shape=tuple(shape for shape, _ in outs),
        in_specs=ins,
        out_specs=tuple(spec for _, spec in outs),
        scratch_shapes=list(scratch),
        input_output_aliases=aliases or {},
        compiler_params=PARAMS,
    )(*args)


def in_vmem(*shapes):
    return [(shape, VM) for shape in shapes]


def on_device(z, band, ld, mix, starts, counts):
    t = lax.axis_index("trait")
    g = lax.axis_index(ROWS)
    owners = lax.axis_size(ROWS)
    lane = lax.iota(jnp.int32, 8)
    place = jnp.zeros((8,), jnp.int32)
    for k, value in enumerate((t, t ^ 1, 3 - t, g, owners, g % 2)):
        place = jnp.where(lane == k, value, place)
    pairs_a = [(i, i ^ 1) for i in range(4)]
    pairs_b = [(i, 3 - i) for i in range(4)]
    pairs_e = [(i, i ^ 1) for i in range(owners)]
    pairs_o = [(i, (i + 1) % owners if i % 2 else (i - 1) % owners) for i in range(owners)]

    def along_trait(x, y, pairs_x, pairs_y):
        return lax.ppermute(x, "trait", pairs_x), lax.ppermute(y, "trait", pairs_y)

    def along_rows(x, y):
        return lax.ppermute(x, ROWS, pairs_e), lax.ppermute(y, ROWS, pairs_o)

    z, band, mix = (pltpu.with_memory_space_constraint(x, pltpu.HBM) for x in (z, band, mix))
    mix_part = jax.ShapeDtypeStruct((2 * COLS, 2 * COLS), BF)
    w1a, w1b, halo_e, halo_o, mix_a, mix_b = call(
        whiten_1,
        in_vmem(shaped(HALF1), shaped(HALF1), shaped(1), shaped(1), mix_part, mix_part),
        [SMEM, HBM, HBM, HBM],
        (place, z, band, mix),
        [
            pltpu.VMEM(((2 * HALF1 + 2) * BLK, COLS), BF),
            pltpu.VMEM((2 * HALF1, BLK, 3 * BLK), BF),
            pltpu.SemaphoreType.DMA((11 + len(pieces(2 * HALF1)),)),
        ],
    )
    got1a, got1b = along_trait(w1a, w1b, pairs_a, pairs_b)
    z, _ = lax.optimization_barrier((z, w1a))
    w2a, w2b = call(
        whiten_2,
        in_vmem(shaped(HALF2), shaped(HALF2)),
        [HBM, HBM],
        (z, band),
        [
            pltpu.VMEM(((2 * HALF2 + 4) * BLK, COLS), BF),
            pltpu.VMEM((2 * HALF2, BLK, 3 * BLK), BF),
            pltpu.SemaphoreType.DMA((2 + 2 * len(pieces(HALF2)),)),
        ],
    )
    got2a, got2b = along_trait(w2a, w2b, pairs_a, pairs_b)
    halo_e, halo_o, _ = lax.optimization_barrier((halo_e, halo_o, w2a))
    halo_e, halo_o = along_rows(halo_e, halo_o)
    send1a, send1b, own1 = call(
        partial_1,
        in_vmem(shaped(HALF1), shaped(HALF1), shaped(2 * HALF1, F32)),
        [VM] * 6,
        (w1a, got1a, w1b, got1b, mix_a, mix_b),
    )
    far1a, far1b = along_trait(send1a, send1b, pairs_b, pairs_a)
    got2a, got2b, halo_e, halo_o, _ = lax.optimization_barrier((got2a, got2b, halo_e, halo_o, send1a))
    send2a, send2b, own2 = call(
        partial_2,
        in_vmem(shaped(HALF2 + 1), shaped(HALF2 + 1), shaped(2 * HALF2, F32)),
        [SMEM, HBM, HBM] + [VM] * 8,
        (place, z, band, halo_e, halo_o, w2a, got2a, w2b, got2b, mix_a, mix_b),
        [
            pltpu.VMEM((6 * BLK, COLS), BF),
            pltpu.VMEM((2, BLK, 3 * BLK), BF),
            pltpu.SemaphoreType.DMA((4,)),
        ],
    )
    far2a, far2b = along_trait(send2a, send2b, pairs_b, pairs_a)
    far1a, far1b, _ = lax.optimization_barrier((far1a, far1b, send2a))
    (mixed1,) = call(combine_1, in_vmem(shaped(2 * HALF1)), [VM] * 3, (own1, far1a, far1b))
    mid_e, mid_o = along_rows(mixed1, mixed1)
    far2a, far2b, _ = lax.optimization_barrier((far2a, far2b, mixed1))
    mixed2, send_first, send_last, own_edge = call(
        combine_2,
        in_vmem(shaped(2 * HALF2), shaped(1), shaped(1), shaped(2, F32)),
        [VM] * 7,
        (own2, far2a, far2b, send2a, send2b, mix_a, mix_b),
    )
    far_first, far_last = along_trait(send_first, send_last, pairs_a, pairs_b)
    rest_e, rest_o = along_rows(mixed2, mixed2)
    (mixed3,) = call(combine_edge, in_vmem(shaped(2)), [VM] * 3, (own_edge, far_first, far_last))
    edge_e, edge_o = along_rows(mixed3, mixed3)
    window_scratch = [
        pltpu.VMEM((UB, BLK, COLS), BF),
        pltpu.SemaphoreType.DMA((8,)),
        pltpu.SemaphoreType.DMA((UB,)),
    ]
    ext, late, done = call(
        impute_ready,
        [(shaped(EXT), VM), (jax.ShapeDtypeStruct((UB + 2,), jnp.int32), SMEM), (shaped(UB), HBM)],
        [SMEM] * 3 + [VM] * 6,
        (place, starts, counts, mixed1, mixed2, mixed3, mid_e, mid_o, ld),
        [pltpu.SMEM((UB + 1,), jnp.int32)] + window_scratch,
    )
    _, out = call(
        impute_late,
        [(shaped(EXT), VM), (shaped(UB), HBM)],
        [SMEM] * 4 + [VM] * 6 + [HBM],
        (place, starts, counts, late, rest_e, rest_o, edge_e, edge_o, ld, ext, done),
        window_scratch,
        {9: 0, 10: 1},
    )
    return out


def solution(mesh):
    in_specs = (
        P(ROWS, "trait"),
        P(ROWS, None, None),
        P(ROWS, None, None),
        P(),
        P(ROWS),
        P(ROWS),
    )
    return jax.shard_map(on_device, mesh=mesh, in_specs=in_specs, out_specs=P(ROWS, "trait"), check_vma=False)
```

```python
import jax
import jax.numpy as jnp
from jax import lax
from jax.experimental import pallas as pl
from jax.experimental.pallas import tpu as pltpu
from jax.sharding import PartitionSpec as P

BLK = 128
WIN = 4
COLS = 128
TB = 32
UB = 64
ZERO = 3 * TB
EXT = ZERO + 1
UNROLL = 8
BF = jnp.bfloat16
F32 = jnp.float32
ROWS = ("sec", "var")
HBM = pl.BlockSpec(memory_space=pltpu.HBM)
SMEM = pl.BlockSpec(memory_space=pltpu.SMEM)
VM = pl.BlockSpec(memory_space=pltpu.VMEM)
PARAMS = pltpu.CompilerParams(vmem_limit_bytes=40 * 1024 * 1024)
MID = 8
MID_END = TB - MID
HALF1 = (MID_END - MID) // 2
HALF2 = MID


def shaped(blocks, dtype=BF):
    return jax.ShapeDtypeStruct((blocks * BLK, COLS), dtype)


def dot(left, right):
    return jnp.dot(left, right, preferred_element_type=F32)


def at(block, blocks=1):
    start = block * BLK
    return pl.ds(start if isinstance(start, int) else pl.multiple_of(start, BLK), blocks * BLK)


def copy_all(pairs, sems, first=0):
    copies = [pltpu.make_async_copy(a, b, sems.at[first + k]) for k, (a, b) in enumerate(pairs)]
    for copy in copies:
        copy.start()
    return copies


def pieces(blocks):
    return [(k, min(4, blocks - k)) for k in range(0, blocks, 4)]


def whiten_1(place, z, band, mix, w_a, w_b, mix_a, mix_b, zs, bs, sems):
    zcopy = copy_all([(z.at[at(MID - 1, 2 * HALF1 + 2)], zs)], sems)
    cuts = pieces(2 * HALF1)
    bands = copy_all([(band.at[pl.ds(MID + k, n)], bs.at[pl.ds(k, n)]) for k, n in cuts], sems, 1)
    t, a, b = place[0], place[1], place[2]
    pairs = [(z.at[at(0)], w_a.at[at(HALF1)]), (z.at[at(TB - 1)], w_b.at[at(HALF1)])]
    for target, near, far in ((mix_a, a, b), (mix_b, b, a)):
        for i, row in enumerate((t, near)):
            for j, col in enumerate((t, far)):
                pairs.append((mix.at[at(row), at(col)], target.at[at(i), at(j)]))
    others = copy_all(pairs, sems, 1 + len(cuts))
    zcopy[0].wait()
    for (k, n), copy in zip(cuts, bands):
        copy.wait()
        for i in range(k, k + n):
            w = w_a if i < HALF1 else w_b
            w[at(i % HALF1), :] = dot(bs[i], zs[at(i, 3), :]).astype(BF)
    for copy in others:
        copy.wait()


def whiten_2(z, band, w_a, w_b, edge_band, zs, bs, sems):
    zcopies = copy_all(
        [
            (z.at[at(0, HALF2 + 1)], zs.at[at(1, HALF2 + 1)]),
            (z.at[at(MID_END - 1, HALF2 + 1)], zs.at[at(HALF2 + 2, HALF2 + 1)]),
        ],
        sems,
    )
    cuts = [(side, k, n) for side in range(2) for k, n in pieces(HALF2)]
    bands = copy_all(
        [(band.at[pl.ds(side * MID_END + k, n)], bs.at[pl.ds(side * HALF2 + k, n)]) for side, k, n in cuts], sems, 2
    )
    zs[at(0), :] = jnp.zeros((BLK, COLS), BF)
    zs[at(2 * HALF2 + 3), :] = jnp.zeros((BLK, COLS), BF)
    for (side, k, n), copy in zip(cuts, bands):
        if k == 0:
            zcopies[side].wait()
        copy.wait()
        for i in range(k, k + n):
            rows = dot(bs[side * HALF2 + i], zs[at(side * (HALF2 + 2) + i, 3), :])
            (w_a, w_b)[side][at(i), :] = rows.astype(BF)
    edge_band[at(0), :] = bs[0, :, pl.ds(0, BLK)]
    edge_band[at(1), :] = bs[2 * HALF2 - 1, :, pl.ds(2 * BLK, BLK)]


def sums(own_rows, got_rows, mix):
    return dot(own_rows, mix[pl.ds(0, COLS), :]) + dot(got_rows, mix[pl.ds(COLS, COLS), :])


def partial(w_a, got_a, w_b, got_b, mix_a, mix_b, send_a, send_b, own):
    rows = w_a.shape[0]
    for k, (w, got, mix, send) in enumerate(((w_a, got_a, mix_a, send_a), (w_b, got_b, mix_b, send_b))):
        both = sums(w[...], got[...], mix)
        own[pl.ds(k * rows, rows), :] = both[:, :COLS]
        send[...] = both[:, COLS:].astype(BF)


def combine_1(place, own, far_a, far_b, out_e, out_o):
    for k, far in enumerate((far_a, far_b)):
        rows = (own[at(k * (HALF1 + 1), HALF1), :] + far[at(0, HALF1), :].astype(F32)).astype(BF)
        out_e[at(k * HALF1, HALF1), :] = rows
        out_o[at(k * HALF1, HALF1), :] = rows
    first = (own[at(HALF1), :] + far_a[at(HALF1), :].astype(F32)).astype(BF)
    last = (own[at(2 * HALF1 + 1), :] + far_b[at(HALF1), :].astype(F32)).astype(BF)
    odd = place[5] == 1
    out_e[at(2 * HALF1), :] = jnp.where(odd, first, last)
    out_o[at(2 * HALF1), :] = jnp.where(odd, last, first)


def combine_2(own, far_a, far_b, out, edge):
    inner = HALF2 - 1
    edge[at(0), :] = own[at(0), :] + far_a[at(0), :].astype(F32)
    out[at(0, inner), :] = (own[at(1, inner), :] + far_a[at(1, inner), :].astype(F32)).astype(BF)
    out[at(inner, inner), :] = (own[at(HALF2, inner), :] + far_b[at(0, inner), :].astype(F32)).astype(BF)
    edge[at(1), :] = own[at(2 * HALF2 - 1), :] + far_b[at(inner), :].astype(F32)


def finish_edge(place, edge, edge_band, got_e, got_o, out):
    odd = place[5] == 1
    nothing = jnp.zeros((BLK, COLS), BF)
    end_e = got_e[at(2 * HALF1), :]
    end_o = got_o[at(2 * HALF1), :]
    from_left = jnp.where(place[3] == 0, nothing, jnp.where(odd, end_e, end_o))
    from_right = jnp.where(place[3] == place[4] - 1, nothing, jnp.where(odd, end_o, end_e))
    for k, rows in enumerate((from_left, from_right)):
        out[at(k), :] = (edge[at(k), :] + dot(edge_band[at(k), :], rows)).astype(BF)


def to_out(u, n, out, staged, sems):
    return pltpu.make_async_copy(staged.at[n], out.at[at(u)], sems.at[n])


def on_list(index, count, starts, counts, lowest, ld, ext, out, staged, sems):
    def several(k, carry):
        for i in range(UNROLL):
            u = index[jnp.minimum(UNROLL * k + i, count - 1)]
            first = jnp.clip(starts[u] - lowest, 0, 3 * TB - 1)
            have = counts[u]
            window = [ext[at(jnp.where(s < have, jnp.minimum(first + s, ZERO), ZERO)), :] for s in range(WIN)]
            staged[UNROLL * k + i] = dot(ld[u], jnp.concatenate(window, axis=0)).astype(BF)
        for i in range(UNROLL):
            n = UNROLL * k + i

            @pl.when(n < count)
            def _():
                to_out(index[n], n, out, staged, sems).start()

        return carry

    def finish(n, carry):
        to_out(index[n], n, out, staged, sems).wait()
        return carry

    lax.fori_loop(0, (count + UNROLL - 1) // UNROLL, several, 0)
    lax.fori_loop(0, count, finish, 0)


def set_1(ext, base, mid):
    return [(mid.at[at(0, 2 * HALF1)], ext.at[at(base + MID, 2 * HALF1)])]


def set_2(ext, base, rest, edge):
    inner = HALF2 - 1
    return [
        (edge.at[at(0)], ext.at[at(base)]),
        (rest.at[at(0, inner)], ext.at[at(base + 1, inner)]),
        (rest.at[at(inner, inner)], ext.at[at(base + MID_END, inner)]),
        (edge.at[at(1)], ext.at[at(base + TB - 1)]),
    ]


def impute_ready(
    place, starts, counts, mid, rest, edge, mid_e, mid_o, ld, ext, late, out, ready, staged, sems, out_sems
):
    base_e = 2 * TB * (1 - place[5])
    base_o = 2 * TB * place[5]
    copies = copy_all(
        set_1(ext, TB, mid) + set_2(ext, TB, rest, edge) + set_1(ext, base_e, mid_e) + set_1(ext, base_o, mid_o), sems
    )
    ext[at(ZERO), :] = jnp.zeros((BLK, COLS), BF)
    lowest = place[3] * TB - TB

    def sort(u, sizes):
        now, later = sizes
        first = jnp.clip(starts[u] - lowest, 0, 3 * TB - 1)
        last = first + counts[u] - 1
        waits = first < MID
        for low, high in ((MID_END, TB), (2 * TB, 2 * TB + MID), (2 * TB + MID_END, 3 * TB)):
            waits = waits | ((last >= low) & (first < high))
        waits = waits.astype(jnp.int32)
        ready[now] = u
        late[later] = u
        return now + 1 - waits, later + waits

    now, later = lax.fori_loop(0, UB, sort, (0, 0))
    late[UB + 1] = later
    for copy in copies:
        copy.wait()

    @pl.when(now > 0)
    def _():
        on_list(ready, now, starts, counts, lowest, ld, ext, out, staged, out_sems)


def impute_late(
    place, starts, counts, late, rest_e, rest_o, edge_e, edge_o, ld, before, done, ext, out, staged, sems, out_sems
):
    base_e = 2 * TB * (1 - place[5])
    base_o = 2 * TB * place[5]
    copies = copy_all(set_2(ext, base_e, rest_e, edge_e) + set_2(ext, base_o, rest_o, edge_o), sems)
    count = late[UB + 1]
    for copy in copies:
        copy.wait()

    @pl.when(count > 0)
    def _():
        on_list(late, count, starts, counts, place[3] * TB - TB, ld, ext, out, staged, out_sems)


def call(kernel, outs, ins, args, scratch=(), aliases=None):
    return pl.pallas_call(
        kernel,
        name=kernel.__name__,
        out_shape=tuple(shape for shape, _ in outs),
        in_specs=ins,
        out_specs=tuple(spec for _, spec in outs),
        scratch_shapes=list(scratch),
        input_output_aliases=aliases or {},
        compiler_params=PARAMS,
    )(*args)


def in_vmem(*shapes):
    return [(shape, VM) for shape in shapes]


def on_device(z, band, ld, mix, starts, counts):
    t = lax.axis_index("trait")
    g = lax.axis_index(ROWS)
    owners = lax.axis_size(ROWS)
    lane = lax.iota(jnp.int32, 8)
    place = jnp.zeros((8,), jnp.int32)
    for k, value in enumerate((t, t ^ 1, 3 - t, g, owners, g % 2)):
        place = jnp.where(lane == k, value, place)
    pairs_a = [(i, i ^ 1) for i in range(4)]
    pairs_b = [(i, 3 - i) for i in range(4)]
    pairs_e = [(i, i ^ 1) for i in range(owners)]
    pairs_o = [(i, (i + 1) % owners if i % 2 else (i - 1) % owners) for i in range(owners)]

    def along_trait(x, y, pairs_x, pairs_y):
        return lax.ppermute(x, "trait", pairs_x), lax.ppermute(y, "trait", pairs_y)

    def along_rows(x, y):
        return lax.ppermute(x, ROWS, pairs_e), lax.ppermute(y, ROWS, pairs_o)

    z, band, mix = (pltpu.with_memory_space_constraint(x, pltpu.HBM) for x in (z, band, mix))
    mix_part = jax.ShapeDtypeStruct((2 * COLS, 2 * COLS), BF)
    w1a, w1b, mix_a, mix_b = call(
        whiten_1,
        in_vmem(shaped(HALF1 + 1), shaped(HALF1 + 1), mix_part, mix_part),
        [SMEM, HBM, HBM, HBM],
        (place, z, band, mix),
        [
            pltpu.VMEM(((2 * HALF1 + 2) * BLK, COLS), BF),
            pltpu.VMEM((2 * HALF1, BLK, 3 * BLK), BF),
            pltpu.SemaphoreType.DMA((11 + len(pieces(2 * HALF1)),)),
        ],
    )
    got1a, got1b = along_trait(w1a, w1b, pairs_a, pairs_b)
    z, _ = lax.optimization_barrier((z, w1a))
    w2a, w2b, edge_band = call(
        whiten_2,
        in_vmem(shaped(HALF2), shaped(HALF2), shaped(2)),
        [HBM, HBM],
        (z, band),
        [
            pltpu.VMEM(((2 * HALF2 + 4) * BLK, COLS), BF),
            pltpu.VMEM((2 * HALF2, BLK, 3 * BLK), BF),
            pltpu.SemaphoreType.DMA((2 + 2 * len(pieces(HALF2)),)),
        ],
    )
    got2a, got2b = along_trait(w2a, w2b, pairs_a, pairs_b)

    def mixing(w_a, got_a, w_b, got_b):
        blocks = w_a.shape[0] // BLK
        outs = in_vmem(shaped(blocks), shaped(blocks), shaped(2 * blocks, F32))
        send_a, send_b, own = call(partial, outs, [VM] * 6, (w_a, got_a, w_b, got_b, mix_a, mix_b))
        return (own, *along_trait(send_a, send_b, pairs_b, pairs_a)), send_a

    (own1, far1a, far1b), after = mixing(w1a, got1a, w1b, got1b)
    got2a, got2b, _ = lax.optimization_barrier((got2a, got2b, after))
    (own2, far2a, far2b), after = mixing(w2a, got2a, w2b, got2b)
    far1a, far1b, _ = lax.optimization_barrier((far1a, far1b, after))
    to_e, to_o = call(
        combine_1,
        in_vmem(shaped(2 * HALF1 + 1), shaped(2 * HALF1 + 1)),
        [SMEM] + [VM] * 3,
        (place, own1, far1a, far1b),
    )
    mid_e, mid_o = along_rows(to_e, to_o)
    far2a, far2b, _ = lax.optimization_barrier((far2a, far2b, to_e))
    mixed2, edge_sums = call(
        combine_2, in_vmem(shaped(2 * HALF2 - 2), shaped(2, F32)), [VM] * 3, (own2, far2a, far2b)
    )
    rest_e, rest_o = along_rows(mixed2, mixed2)
    (mixed3,) = call(
        finish_edge, in_vmem(shaped(2)), [SMEM] + [VM] * 4, (place, edge_sums, edge_band, mid_e, mid_o)
    )
    edge_e, edge_o = along_rows(mixed3, mixed3)
    window_scratch = [
        pltpu.VMEM((UB, BLK, COLS), BF),
        pltpu.SemaphoreType.DMA((8,)),
        pltpu.SemaphoreType.DMA((UB,)),
    ]
    ext, late, done = call(
        impute_ready,
        [(shaped(EXT), VM), (jax.ShapeDtypeStruct((UB + 2,), jnp.int32), SMEM), (shaped(UB), HBM)],
        [SMEM] * 3 + [VM] * 6,
        (place, starts, counts, to_e, mixed2, mixed3, mid_e, mid_o, ld),
        [pltpu.SMEM((UB + 1,), jnp.int32)] + window_scratch,
    )
    _, out = call(
        impute_late,
        [(shaped(EXT), VM), (shaped(UB), HBM)],
        [SMEM] * 4 + [VM] * 6 + [HBM],
        (place, starts, counts, late, rest_e, rest_o, edge_e, edge_o, ld, ext, done),
        window_scratch,
        {9: 0, 10: 1},
    )
    return out


def solution(mesh):
    in_specs = (
        P(ROWS, "trait"),
        P(ROWS, None, None),
        P(ROWS, None, None),
        P(),
        P(ROWS),
        P(ROWS),
    )
    return jax.shard_map(on_device, mesh=mesh, in_specs=in_specs, out_specs=P(ROWS, "trait"), check_vma=False)
```

```python
import jax
import jax.numpy as jnp
from jax import lax
from jax.experimental import pallas as pl
from jax.experimental.pallas import tpu as pltpu
from jax.sharding import PartitionSpec as P

BLK = 128
WIN = 4
COLS = 128
TB = 32
UB = 64
ZERO = 3 * TB
EXT = ZERO + 1
UNROLL = 8
BF = jnp.bfloat16
F32 = jnp.float32
ROWS = ("sec", "var")
HBM = pl.BlockSpec(memory_space=pltpu.HBM)
SMEM = pl.BlockSpec(memory_space=pltpu.SMEM)
VM = pl.BlockSpec(memory_space=pltpu.VMEM)
PARAMS = pltpu.CompilerParams(vmem_limit_bytes=8 * 1024 * 1024)
MID = 8
MID_END = TB - MID
HALF1 = (MID_END - MID) // 2
HALF2 = MID


def shaped(blocks, dtype=BF):
    return jax.ShapeDtypeStruct((blocks * BLK, COLS), dtype)


def dot(left, right):
    return jnp.dot(left, right, preferred_element_type=F32)


def at(block, blocks=1):
    start = block * BLK
    return pl.ds(start if isinstance(start, int) else pl.multiple_of(start, BLK), blocks * BLK)


def copy_all(pairs, sems, first=0):
    copies = [pltpu.make_async_copy(a, b, sems.at[first + k]) for k, (a, b) in enumerate(pairs)]
    for copy in copies:
        copy.start()
    return copies


def pieces(blocks):
    return [(k, min(4, blocks - k)) for k in range(0, blocks, 4)]


def whiten_1(place, z, band, mix, w_a, w_b, mix_a, mix_b, zs, bs, sems):
    zcopy = copy_all([(z.at[at(MID - 1, 2 * HALF1 + 2)], zs)], sems)
    cuts = pieces(2 * HALF1)
    bands = copy_all([(band.at[pl.ds(MID + k, n)], bs.at[pl.ds(k, n)]) for k, n in cuts], sems, 1)
    t, a, b = place[0], place[1], place[2]
    pairs = [(z.at[at(0)], w_a.at[at(HALF1)]), (z.at[at(TB - 1)], w_b.at[at(HALF1)])]
    for target, near, far in ((mix_a, a, b), (mix_b, b, a)):
        for i, row in enumerate((t, near)):
            for j, col in enumerate((t, far)):
                pairs.append((mix.at[at(row), at(col)], target.at[at(i), at(j)]))
    others = copy_all(pairs, sems, 1 + len(cuts))
    zcopy[0].wait()
    for (k, n), copy in zip(cuts, bands):
        copy.wait()
        for i in range(k, k + n):
            w = w_a if i < HALF1 else w_b
            w[at(i % HALF1), :] = dot(bs[i], zs[at(i, 3), :]).astype(BF)
    for copy in others:
        copy.wait()


def whiten_2(z, band, w_a, w_b, edge_band, zs, bs, sems):
    zcopies = copy_all(
        [
            (z.at[at(0, HALF2 + 1)], zs.at[at(1, HALF2 + 1)]),
            (z.at[at(MID_END - 1, HALF2 + 1)], zs.at[at(HALF2 + 2, HALF2 + 1)]),
        ],
        sems,
    )
    cuts = [(side, k, n) for side in range(2) for k, n in pieces(HALF2)]
    bands = copy_all(
        [(band.at[pl.ds(side * MID_END + k, n)], bs.at[pl.ds(side * HALF2 + k, n)]) for side, k, n in cuts], sems, 2
    )
    zs[at(0), :] = jnp.zeros((BLK, COLS), BF)
    zs[at(2 * HALF2 + 3), :] = jnp.zeros((BLK, COLS), BF)
    for (side, k, n), copy in zip(cuts, bands):
        if k == 0:
            zcopies[side].wait()
        copy.wait()
        for i in range(k, k + n):
            rows = dot(bs[side * HALF2 + i], zs[at(side * (HALF2 + 2) + i, 3), :])
            (w_a, w_b)[side][at(i), :] = rows.astype(BF)
    edge_band[at(0), :] = bs[0, :, pl.ds(0, BLK)]
    edge_band[at(1), :] = bs[2 * HALF2 - 1, :, pl.ds(2 * BLK, BLK)]


def sums(own_rows, got_rows, mix):
    return dot(own_rows, mix[pl.ds(0, COLS), :]) + dot(got_rows, mix[pl.ds(COLS, COLS), :])


def partial(w_a, got_a, w_b, got_b, mix_a, mix_b, send_a, send_b, own):
    rows = w_a.shape[0]
    for k, (w, got, mix, send) in enumerate(((w_a, got_a, mix_a, send_a), (w_b, got_b, mix_b, send_b))):
        both = sums(w[...], got[...], mix)
        own[pl.ds(k * rows, rows), :] = both[:, :COLS]
        send[...] = both[:, COLS:].astype(BF)


def combine_1(place, own, far_a, far_b, out_e, out_o):
    for k, far in enumerate((far_a, far_b)):
        rows = (own[at(k * (HALF1 + 1), HALF1), :] + far[at(0, HALF1), :].astype(F32)).astype(BF)
        out_e[at(k * HALF1, HALF1), :] = rows
        out_o[at(k * HALF1, HALF1), :] = rows
    first = (own[at(HALF1), :] + far_a[at(HALF1), :].astype(F32)).astype(BF)
    last = (own[at(2 * HALF1 + 1), :] + far_b[at(HALF1), :].astype(F32)).astype(BF)
    odd = place[5] == 1
    out_e[at(2 * HALF1), :] = jnp.where(odd, first, last)
    out_o[at(2 * HALF1), :] = jnp.where(odd, last, first)


def combine_2(own, far_a, far_b, out, edge):
    inner = HALF2 - 1
    edge[at(0), :] = own[at(0), :] + far_a[at(0), :].astype(F32)
    out[at(0, inner), :] = (own[at(1, inner), :] + far_a[at(1, inner), :].astype(F32)).astype(BF)
    out[at(inner, inner), :] = (own[at(HALF2, inner), :] + far_b[at(0, inner), :].astype(F32)).astype(BF)
    edge[at(1), :] = own[at(2 * HALF2 - 1), :] + far_b[at(inner), :].astype(F32)


def finish_edge(place, edge, edge_band, got_e, got_o, out):
    odd = place[5] == 1
    nothing = jnp.zeros((BLK, COLS), BF)
    end_e = got_e[at(2 * HALF1), :]
    end_o = got_o[at(2 * HALF1), :]
    from_left = jnp.where(place[3] == 0, nothing, jnp.where(odd, end_e, end_o))
    from_right = jnp.where(place[3] == place[4] - 1, nothing, jnp.where(odd, end_o, end_e))
    for k, rows in enumerate((from_left, from_right)):
        out[at(k), :] = (edge[at(k), :] + dot(edge_band[at(k), :], rows)).astype(BF)


def to_out(u, n, out, staged, sems):
    return pltpu.make_async_copy(staged.at[n], out.at[at(u)], sems.at[n])


def on_ranges(ranges, starts, counts, lowest, ld, ext, out, staged, sems):
    total = 0
    parts = []
    for low, high in ranges:
        parts.append((total, low))
        total = total + high - low

    def window_of(n):
        u = n + parts[0][1]
        for before, low in parts[1:]:
            u = jnp.where(n >= before, n - before + low, u)
        return u

    def several(k, carry):
        for i in range(UNROLL):
            u = window_of(jnp.minimum(UNROLL * k + i, total - 1))
            first = jnp.clip(starts[u] - lowest, 0, 3 * TB - 1)
            have = counts[u]
            window = [ext[at(jnp.where(s < have, jnp.minimum(first + s, ZERO), ZERO)), :] for s in range(WIN)]
            staged[UNROLL * k + i] = dot(ld[u], jnp.concatenate(window, axis=0)).astype(BF)
        for i in range(UNROLL):
            n = UNROLL * k + i

            @pl.when(n < total)
            def _():
                to_out(window_of(n), n, out, staged, sems).start()

        return carry

    def finish(n, carry):
        to_out(window_of(n), n, out, staged, sems).wait()
        return carry

    lax.fori_loop(0, (total + UNROLL - 1) // UNROLL, several, 0)
    lax.fori_loop(0, total, finish, 0)


def set_1(ext, base, mid):
    return [(mid.at[at(0, 2 * HALF1)], ext.at[at(base + MID, 2 * HALF1)])]


def set_2(ext, base, rest, edge):
    inner = HALF2 - 1
    return [
        (edge.at[at(0)], ext.at[at(base)]),
        (rest.at[at(0, inner)], ext.at[at(base + 1, inner)]),
        (rest.at[at(inner, inner)], ext.at[at(base + MID_END, inner)]),
        (edge.at[at(1)], ext.at[at(base + TB - 1)]),
    ]


LIMITS = (
    MID,
    MID_END - WIN + 1,
    TB,
    TB + 1,
    2 * TB - WIN,
    2 * TB - WIN + 1,
    2 * TB + MID,
    2 * TB + MID_END - WIN + 1,
)


def impute_own(place, starts, counts, below, mid, rest, ld, ext, ld_here, out, staged, sems, out_sems):
    inner = HALF2 - 1
    quarter = UB // 4
    whole = [(ld.at[pl.ds(k, quarter)], ld_here.at[pl.ds(k, quarter)]) for k in range(0, UB, quarter)]
    loads = copy_all(whole, sems, 4)
    copies = copy_all(
        set_1(ext, TB, mid)
        + [
            (rest.at[at(0, inner)], ext.at[at(TB + 1, inner)]),
            (rest.at[at(inner, inner)], ext.at[at(TB + MID_END, inner)]),
        ],
        sems,
    )
    ext[at(ZERO), :] = jnp.zeros((BLK, COLS), BF)
    for copy in copies + loads:
        copy.wait()
    ranges = [(below[3], below[4])]
    on_ranges(ranges, starts, counts, place[3] * TB - TB, ld_here, ext, out, staged, out_sems)


def impute_near(
    place, starts, counts, below, edge, mid_e, mid_o, ld, before, done, ext, out, staged, sems, out_sems
):
    base_e = 2 * TB * (1 - place[5])
    base_o = 2 * TB * place[5]
    own_edge = [(edge.at[at(0)], ext.at[at(TB)]), (edge.at[at(1)], ext.at[at(2 * TB - 1)])]
    copies = copy_all(own_edge + set_1(ext, base_e, mid_e) + set_1(ext, base_o, mid_o), sems)
    for copy in copies:
        copy.wait()
    ranges = [(below[k], below[k + 1]) for k in (0, 2, 4, 6)]
    on_ranges(ranges, starts, counts, place[3] * TB - TB, ld, ext, out, staged, out_sems)


def impute_far(
    place, starts, counts, below, rest_e, rest_o, edge_e, edge_o, ld, before, done, ext, out, staged, sems, out_sems
):
    base_e = 2 * TB * (1 - place[5])
    base_o = 2 * TB * place[5]
    copies = copy_all(set_2(ext, base_e, rest_e, edge_e) + set_2(ext, base_o, rest_o, edge_o), sems)
    for copy in copies:
        copy.wait()
    ranges = [(0, below[0]), (below[1], below[2]), (below[5], below[6]), (below[7], UB)]
    on_ranges(ranges, starts, counts, place[3] * TB - TB, ld, ext, out, staged, out_sems)


def call(kernel, outs, ins, args, scratch=(), aliases=None):
    return pl.pallas_call(
        kernel,
        name=kernel.__name__,
        out_shape=tuple(shape for shape, _ in outs),
        in_specs=ins,
        out_specs=tuple(spec for _, spec in outs),
        scratch_shapes=list(scratch),
        input_output_aliases=aliases or {},
        compiler_params=PARAMS,
    )(*args)


def in_vmem(*shapes):
    return [(shape, VM) for shape in shapes]


def on_device(z, band, ld, mix, starts, counts):
    t = lax.axis_index("trait")
    g = lax.axis_index(ROWS)
    owners = lax.axis_size(ROWS)
    lane = lax.iota(jnp.int32, 8)
    place = jnp.zeros((8,), jnp.int32)
    for k, value in enumerate((t, t ^ 1, 3 - t, g, owners, g % 2)):
        place = jnp.where(lane == k, value, place)
    pairs_a = [(i, i ^ 1) for i in range(4)]
    pairs_b = [(i, 3 - i) for i in range(4)]
    pairs_e = [(i, i ^ 1) for i in range(owners)]
    pairs_o = [(i, min(i + 1, owners - 1) if i % 2 else max(i - 1, 0)) for i in range(owners)]

    def along_trait(x, y, pairs_x, pairs_y):
        return lax.ppermute(x, "trait", pairs_x), lax.ppermute(y, "trait", pairs_y)

    def along_rows(x, y):
        return lax.ppermute(x, ROWS, pairs_e), lax.ppermute(y, ROWS, pairs_o)

    z, band, mix, ld = (pltpu.with_memory_space_constraint(x, pltpu.HBM) for x in (z, band, mix, ld))
    mix_part = jax.ShapeDtypeStruct((2 * COLS, 2 * COLS), BF)
    w1a, w1b, mix_a, mix_b = call(
        whiten_1,
        in_vmem(shaped(HALF1 + 1), shaped(HALF1 + 1), mix_part, mix_part),
        [SMEM, HBM, HBM, HBM],
        (place, z, band, mix),
        [
            pltpu.VMEM(((2 * HALF1 + 2) * BLK, COLS), BF),
            pltpu.VMEM((2 * HALF1, BLK, 3 * BLK), BF),
            pltpu.SemaphoreType.DMA((11 + len(pieces(2 * HALF1)),)),
        ],
    )
    got1a, got1b = along_trait(w1a, w1b, pairs_a, pairs_b)
    z, _ = lax.optimization_barrier((z, w1a))
    w2a, w2b, edge_band = call(
        whiten_2,
        in_vmem(shaped(HALF2), shaped(HALF2), shaped(2)),
        [HBM, HBM],
        (z, band),
        [
            pltpu.VMEM(((2 * HALF2 + 4) * BLK, COLS), BF),
            pltpu.VMEM((2 * HALF2, BLK, 3 * BLK), BF),
            pltpu.SemaphoreType.DMA((2 + 2 * len(pieces(HALF2)),)),
        ],
    )
    got2a, got2b = along_trait(w2a, w2b, pairs_a, pairs_b)

    def mixing(w_a, got_a, w_b, got_b):
        blocks = w_a.shape[0] // BLK
        outs = in_vmem(shaped(blocks), shaped(blocks), shaped(2 * blocks, F32))
        send_a, send_b, own = call(partial, outs, [VM] * 6, (w_a, got_a, w_b, got_b, mix_a, mix_b))
        return (own, *along_trait(send_a, send_b, pairs_b, pairs_a)), send_a

    (own1, far1a, far1b), after = mixing(w1a, got1a, w1b, got1b)
    got2a, got2b, _ = lax.optimization_barrier((got2a, got2b, after))
    (own2, far2a, far2b), after = mixing(w2a, got2a, w2b, got2b)
    far1a, far1b, _ = lax.optimization_barrier((far1a, far1b, after))
    to_e, to_o = call(
        combine_1,
        in_vmem(shaped(2 * HALF1 + 1), shaped(2 * HALF1 + 1)),
        [SMEM] + [VM] * 3,
        (place, own1, far1a, far1b),
    )
    mid_e, mid_o = along_rows(to_e, to_o)
    far2a, far2b, _ = lax.optimization_barrier((far2a, far2b, to_e))
    mixed2, edge_sums = call(
        combine_2, in_vmem(shaped(2 * HALF2 - 2), shaped(2, F32)), [VM] * 3, (own2, far2a, far2b)
    )
    rest_e, rest_o = along_rows(mixed2, mixed2)
    starts_here = starts - (g * TB - TB)
    below = jnp.sum(starts_here[None, :] < jnp.array(LIMITS, jnp.int32)[:, None], axis=1, dtype=jnp.int32)
    window_scratch = [
        pltpu.VMEM((UB, BLK, COLS), BF),
        pltpu.SemaphoreType.DMA((8,)),
        pltpu.SemaphoreType.DMA((UB,)),
    ]
    outs = [(shaped(EXT), VM), (shaped(UB), HBM)]
    plan = (place, starts, counts, below)
    ext, ld, done = call(
        impute_own,
        [outs[0], (jax.ShapeDtypeStruct(ld.shape, BF), VM), outs[1]],
        [SMEM] * 4 + [VM] * 2 + [HBM],
        (*plan, to_e, mixed2, ld),
        window_scratch,
    )
    mid_e, mid_o, ext = lax.optimization_barrier((mid_e, mid_o, ext))
    (mixed3,) = call(
        finish_edge, in_vmem(shaped(2)), [SMEM] + [VM] * 4, (place, edge_sums, edge_band, mid_e, mid_o)
    )
    edge_e, edge_o = along_rows(mixed3, mixed3)
    ext, done = call(
        impute_near,
        outs,
        [SMEM] * 4 + [VM] * 5 + [HBM],
        (*plan, mixed3, mid_e, mid_o, ld, ext, done),
        window_scratch,
        {8: 0, 9: 1},
    )
    _, out = call(
        impute_far,
        outs,
        [SMEM] * 4 + [VM] * 6 + [HBM],
        (*plan, rest_e, rest_o, edge_e, edge_o, ld, ext, done),
        window_scratch,
        {9: 0, 10: 1},
    )
    return out


def solution(mesh):
    in_specs = (
        P(ROWS, "trait"),
        P(ROWS, None, None),
        P(ROWS, None, None),
        P(),
        P(ROWS),
        P(ROWS),
    )
    return jax.shard_map(on_device, mesh=mesh, in_specs=in_specs, out_specs=P(ROWS, "trait"), check_vma=False)
```

```python
import jax
import jax.numpy as jnp
from jax import lax
from jax.experimental import pallas as pl
from jax.experimental.pallas import tpu as pltpu
from jax.sharding import PartitionSpec as P

BLK = 128
WIN = 4
COLS = 128
TB = 32
UB = 64
ZERO = 3 * TB
EXT = ZERO + 1
UNROLL = 8
BF = jnp.bfloat16
F32 = jnp.float32
ROWS = ("sec", "var")
HBM = pl.BlockSpec(memory_space=pltpu.HBM)
SMEM = pl.BlockSpec(memory_space=pltpu.SMEM)
VM = pl.BlockSpec(memory_space=pltpu.VMEM)
PARAMS = pltpu.CompilerParams(vmem_limit_bytes=16 * 1024 * 1024)
MID = 8
MID_END = TB - MID
HALF1 = (MID_END - MID) // 2
HALF2 = MID


def shaped(blocks, dtype=BF):
    return jax.ShapeDtypeStruct((blocks * BLK, COLS), dtype)


def dot(left, right):
    return jnp.dot(left, right, preferred_element_type=F32)


def at(block, blocks=1):
    start = block * BLK
    return pl.ds(start if isinstance(start, int) else pl.multiple_of(start, BLK), blocks * BLK)


def copy_all(pairs, sems, first=0):
    copies = [pltpu.make_async_copy(a, b, sems.at[first + k]) for k, (a, b) in enumerate(pairs)]
    for copy in copies:
        copy.start()
    return copies


def pieces(blocks):
    return [(k, min(4, blocks - k)) for k in range(0, blocks, 4)]


def whiten_1(place, z, band, mix, w_a, w_b, mix_a, mix_b, zs, bs, sems):
    zcopy = copy_all([(z.at[at(MID - 1, 2 * HALF1 + 2)], zs)], sems)
    cuts = pieces(2 * HALF1)
    bands = copy_all([(band.at[pl.ds(MID + k, n)], bs.at[pl.ds(k, n)]) for k, n in cuts], sems, 1)
    t, a, b = place[0], place[1], place[2]
    pairs = [(z.at[at(0)], w_a.at[at(HALF1)]), (z.at[at(TB - 1)], w_b.at[at(HALF1)])]
    for target, near, far in ((mix_a, a, b), (mix_b, b, a)):
        for i, row in enumerate((t, near)):
            for j, col in enumerate((t, far)):
                pairs.append((mix.at[at(row), at(col)], target.at[at(i), at(j)]))
    others = copy_all(pairs, sems, 1 + len(cuts))
    zcopy[0].wait()
    for (k, n), copy in zip(cuts, bands):
        copy.wait()
        for i in range(k, k + n):
            w = w_a if i < HALF1 else w_b
            w[at(i % HALF1), :] = dot(bs[i], zs[at(i, 3), :]).astype(BF)
    for copy in others:
        copy.wait()


def whiten_2(z, band, w_a, w_b, edge_band, zs, bs, sems):
    zcopies = copy_all(
        [
            (z.at[at(0, HALF2 + 1)], zs.at[at(1, HALF2 + 1)]),
            (z.at[at(MID_END - 1, HALF2 + 1)], zs.at[at(HALF2 + 2, HALF2 + 1)]),
        ],
        sems,
    )
    cuts = [(side, k, n) for side in range(2) for k, n in pieces(HALF2)]
    bands = copy_all(
        [(band.at[pl.ds(side * MID_END + k, n)], bs.at[pl.ds(side * HALF2 + k, n)]) for side, k, n in cuts], sems, 2
    )
    zs[at(0), :] = jnp.zeros((BLK, COLS), BF)
    zs[at(2 * HALF2 + 3), :] = jnp.zeros((BLK, COLS), BF)
    for (side, k, n), copy in zip(cuts, bands):
        if k == 0:
            zcopies[side].wait()
        copy.wait()
        for i in range(k, k + n):
            rows = dot(bs[side * HALF2 + i], zs[at(side * (HALF2 + 2) + i, 3), :])
            (w_a, w_b)[side][at(i), :] = rows.astype(BF)
    edge_band[at(0), :] = bs[0, :, pl.ds(0, BLK)]
    edge_band[at(1), :] = bs[2 * HALF2 - 1, :, pl.ds(2 * BLK, BLK)]


def sums(own_rows, got_rows, mix):
    return dot(own_rows, mix[pl.ds(0, COLS), :]) + dot(got_rows, mix[pl.ds(COLS, COLS), :])


def partial(w_a, got_a, w_b, got_b, mix_a, mix_b, send_a, send_b, own):
    rows = w_a.shape[0]
    for k, (w, got, mix, send) in enumerate(((w_a, got_a, mix_a, send_a), (w_b, got_b, mix_b, send_b))):
        both = sums(w[...], got[...], mix)
        own[pl.ds(k * rows, rows), :] = both[:, :COLS]
        send[...] = both[:, COLS:].astype(BF)


def combine_1(place, own, far_a, far_b, out_e, out_o):
    for k, far in enumerate((far_a, far_b)):
        rows = (own[at(k * (HALF1 + 1), HALF1), :] + far[at(0, HALF1), :].astype(F32)).astype(BF)
        out_e[at(k * HALF1, HALF1), :] = rows
        out_o[at(k * HALF1, HALF1), :] = rows
    first = (own[at(HALF1), :] + far_a[at(HALF1), :].astype(F32)).astype(BF)
    last = (own[at(2 * HALF1 + 1), :] + far_b[at(HALF1), :].astype(F32)).astype(BF)
    odd = place[5] == 1
    out_e[at(2 * HALF1), :] = jnp.where(odd, first, last)
    out_o[at(2 * HALF1), :] = jnp.where(odd, last, first)


def combine_2(own, far_a, far_b, out, edge):
    inner = HALF2 - 1
    edge[at(0), :] = own[at(0), :] + far_a[at(0), :].astype(F32)
    out[at(0, inner), :] = (own[at(1, inner), :] + far_a[at(1, inner), :].astype(F32)).astype(BF)
    out[at(inner, inner), :] = (own[at(HALF2, inner), :] + far_b[at(0, inner), :].astype(F32)).astype(BF)
    edge[at(1), :] = own[at(2 * HALF2 - 1), :] + far_b[at(inner), :].astype(F32)


def finish_edge(place, edge, edge_band, got_e, got_o, out):
    odd = place[5] == 1
    nothing = jnp.zeros((BLK, COLS), BF)
    end_e = got_e[at(2 * HALF1), :]
    end_o = got_o[at(2 * HALF1), :]
    from_left = jnp.where(place[3] == 0, nothing, jnp.where(odd, end_e, end_o))
    from_right = jnp.where(place[3] == place[4] - 1, nothing, jnp.where(odd, end_o, end_e))
    for k, rows in enumerate((from_left, from_right)):
        out[at(k), :] = (edge[at(k), :] + dot(edge_band[at(k), :], rows)).astype(BF)


def to_out(u, n, out, staged, sems):
    return pltpu.make_async_copy(staged.at[n], out.at[at(u)], sems.at[n])


def on_ranges(ranges, starts, counts, lowest, ld, fill, ext, out, ld_here, staged, ld_sems, out_sems):
    total = 0
    parts = []
    for low, high in ranges:
        parts.append((total, low))
        total = total + high - low

    def window_of(n):
        u = n + parts[0][1]
        for before, low in parts[1:]:
            u = jnp.where(n >= before, n - before + low, u)
        return u

    def load(n):
        return pltpu.make_async_copy(ld.at[window_of(n)], ld_here.at[n], ld_sems.at[n])

    def begin(n, carry):
        load(n).start()
        return carry

    def several(k, carry):
        for i in range(UNROLL):
            n = UNROLL * k + i

            @pl.when(n < total)
            def _():
                load(n).wait()

        for i in range(UNROLL):
            n = jnp.minimum(UNROLL * k + i, total - 1)
            u = window_of(n)
            first = jnp.clip(starts[u] - lowest, 0, 3 * TB - 1)
            have = counts[u]
            window = [ext[at(jnp.where(s < have, jnp.minimum(first + s, ZERO), ZERO)), :] for s in range(WIN)]
            staged[UNROLL * k + i] = dot(ld_here[n], jnp.concatenate(window, axis=0)).astype(BF)
        for i in range(UNROLL):
            n = UNROLL * k + i

            @pl.when(n < total)
            def _():
                to_out(window_of(n), n, out, staged, out_sems).start()

        return carry

    def finish(n, carry):
        to_out(window_of(n), n, out, staged, out_sems).wait()
        return carry

    lax.fori_loop(0, total, begin, 0)
    fill()
    lax.fori_loop(0, (total + UNROLL - 1) // UNROLL, several, 0)
    lax.fori_loop(0, total, finish, 0)


def move(ext, block, source, first, blocks):
    ext[at(block, blocks), :] = source[at(first, blocks), :]


LIMITS = (
    MID,
    MID_END - WIN + 1,
    TB,
    TB + 1,
    2 * TB - WIN,
    2 * TB - WIN + 1,
    2 * TB + MID,
    2 * TB + MID_END - WIN + 1,
)


def impute_own(place, starts, counts, below, mid, rest, ld, ext, out, *scratch):
    inner = HALF2 - 1

    def fill():
        move(ext, TB + 1, rest, 0, inner)
        move(ext, TB + MID, mid, 0, 2 * HALF1)
        move(ext, TB + MID_END, rest, inner, inner)
        ext[at(ZERO), :] = jnp.zeros((BLK, COLS), BF)

    on_ranges([(below[3], below[4])], starts, counts, place[3] * TB - TB, ld, fill, ext, out, *scratch)


def impute_near(place, starts, counts, below, edge, mid_e, mid_o, ld, before, done, ext, out, *scratch):
    def fill():
        move(ext, TB, edge, 0, 1)
        move(ext, 2 * TB - 1, edge, 1, 1)
        move(ext, 2 * TB * (1 - place[5]) + MID, mid_e, 0, 2 * HALF1)
        move(ext, 2 * TB * place[5] + MID, mid_o, 0, 2 * HALF1)

    ranges = [(below[k], below[k + 1]) for k in (0, 2, 4, 6)]
    on_ranges(ranges, starts, counts, place[3] * TB - TB, ld, fill, ext, out, *scratch)


def impute_far(place, starts, counts, below, rest_e, rest_o, edge_e, edge_o, ld, before, done, ext, out, *scratch):
    inner = HALF2 - 1

    def fill():
        for base, rest, edge in ((2 * TB * (1 - place[5]), rest_e, edge_e), (2 * TB * place[5], rest_o, edge_o)):
            move(ext, base, edge, 0, 1)
            move(ext, base + 1, rest, 0, inner)
            move(ext, base + MID_END, rest, inner, inner)
            move(ext, base + TB - 1, edge, 1, 1)

    ranges = [(0, below[0]), (below[1], below[2]), (below[5], below[6]), (below[7], UB)]
    on_ranges(ranges, starts, counts, place[3] * TB - TB, ld, fill, ext, out, *scratch)


def call(kernel, outs, ins, args, scratch=(), aliases=None):
    return pl.pallas_call(
        kernel,
        name=kernel.__name__,
        out_shape=tuple(shape for shape, _ in outs),
        in_specs=ins,
        out_specs=tuple(spec for _, spec in outs),
        scratch_shapes=list(scratch),
        input_output_aliases=aliases or {},
        compiler_params=PARAMS,
    )(*args)


def in_vmem(*shapes):
    return [(shape, VM) for shape in shapes]


def on_device(z, band, ld, mix, starts, counts):
    t = lax.axis_index("trait")
    g = lax.axis_index(ROWS)
    owners = lax.axis_size(ROWS)
    lane = lax.iota(jnp.int32, 8)
    place = jnp.zeros((8,), jnp.int32)
    for k, value in enumerate((t, t ^ 1, 3 - t, g, owners, g % 2)):
        place = jnp.where(lane == k, value, place)
    pairs_a = [(i, i ^ 1) for i in range(4)]
    pairs_b = [(i, 3 - i) for i in range(4)]
    pairs_e = [(i, i ^ 1) for i in range(owners)]
    pairs_o = [(i, (i + 1) % owners if i % 2 else (i - 1) % owners) for i in range(owners)]

    def along_trait(x, y, pairs_x, pairs_y):
        return lax.ppermute(x, "trait", pairs_x), lax.ppermute(y, "trait", pairs_y)

    def along_rows(x, y):
        return lax.ppermute(x, ROWS, pairs_e), lax.ppermute(y, ROWS, pairs_o)

    z, band, mix, ld = (pltpu.with_memory_space_constraint(x, pltpu.HBM) for x in (z, band, mix, ld))
    mix_part = jax.ShapeDtypeStruct((2 * COLS, 2 * COLS), BF)
    w1a, w1b, mix_a, mix_b = call(
        whiten_1,
        in_vmem(shaped(HALF1 + 1), shaped(HALF1 + 1), mix_part, mix_part),
        [SMEM, HBM, HBM, HBM],
        (place, z, band, mix),
        [
            pltpu.VMEM(((2 * HALF1 + 2) * BLK, COLS), BF),
            pltpu.VMEM((2 * HALF1, BLK, 3 * BLK), BF),
            pltpu.SemaphoreType.DMA((11 + len(pieces(2 * HALF1)),)),
        ],
    )
    got1a, got1b = along_trait(w1a, w1b, pairs_a, pairs_b)
    z, _ = lax.optimization_barrier((z, w1a))
    w2a, w2b, edge_band = call(
        whiten_2,
        in_vmem(shaped(HALF2), shaped(HALF2), shaped(2)),
        [HBM, HBM],
        (z, band),
        [
            pltpu.VMEM(((2 * HALF2 + 4) * BLK, COLS), BF),
            pltpu.VMEM((2 * HALF2, BLK, 3 * BLK), BF),
            pltpu.SemaphoreType.DMA((2 + 2 * len(pieces(HALF2)),)),
        ],
    )
    got2a, got2b = along_trait(w2a, w2b, pairs_a, pairs_b)

    def mixing(w_a, got_a, w_b, got_b):
        blocks = w_a.shape[0] // BLK
        outs = in_vmem(shaped(blocks), shaped(blocks), shaped(2 * blocks, F32))
        send_a, send_b, own = call(partial, outs, [VM] * 6, (w_a, got_a, w_b, got_b, mix_a, mix_b))
        return (own, *along_trait(send_a, send_b, pairs_b, pairs_a)), send_a

    (own1, far1a, far1b), after = mixing(w1a, got1a, w1b, got1b)
    got2a, got2b, _ = lax.optimization_barrier((got2a, got2b, after))
    (own2, far2a, far2b), after = mixing(w2a, got2a, w2b, got2b)
    far1a, far1b, _ = lax.optimization_barrier((far1a, far1b, after))
    to_e, to_o = call(
        combine_1,
        in_vmem(shaped(2 * HALF1 + 1), shaped(2 * HALF1 + 1)),
        [SMEM] + [VM] * 3,
        (place, own1, far1a, far1b),
    )
    mid_e, mid_o = along_rows(to_e, to_o)
    far2a, far2b, _ = lax.optimization_barrier((far2a, far2b, to_e))
    mixed2, edge_sums = call(
        combine_2, in_vmem(shaped(2 * HALF2 - 2), shaped(2, F32)), [VM] * 3, (own2, far2a, far2b)
    )
    rest_e, rest_o = along_rows(mixed2, mixed2)
    starts_here = starts - (g * TB - TB)
    below = jnp.sum(starts_here[None, :] < jnp.array(LIMITS, jnp.int32)[:, None], axis=1, dtype=jnp.int32)
    window_scratch = [
        pltpu.VMEM((UB, BLK, WIN * BLK), BF),
        pltpu.VMEM((UB, BLK, COLS), BF),
        pltpu.SemaphoreType.DMA((UB,)),
        pltpu.SemaphoreType.DMA((UB,)),
    ]
    outs = [(shaped(EXT), VM), (shaped(UB), HBM)]
    plan = (place, starts, counts, below)
    ext, done = call(impute_own, outs, [SMEM] * 4 + [VM] * 2 + [HBM], (*plan, to_e, mixed2, ld), window_scratch)
    mid_e, mid_o, ext = lax.optimization_barrier((mid_e, mid_o, ext))
    (mixed3,) = call(
        finish_edge, in_vmem(shaped(2)), [SMEM] + [VM] * 4, (place, edge_sums, edge_band, mid_e, mid_o)
    )
    edge_e, edge_o = along_rows(mixed3, mixed3)
    ext, done = call(
        impute_near,
        outs,
        [SMEM] * 4 + [VM] * 3 + [HBM, VM, HBM],
        (*plan, mixed3, mid_e, mid_o, ld, ext, done),
        window_scratch,
        {8: 0, 9: 1},
    )
    _, out = call(
        impute_far,
        outs,
        [SMEM] * 4 + [VM] * 4 + [HBM, VM, HBM],
        (*plan, rest_e, rest_o, edge_e, edge_o, ld, ext, done),
        window_scratch,
        {9: 0, 10: 1},
    )
    return out


def solution(mesh):
    in_specs = (
        P(ROWS, "trait"),
        P(ROWS, None, None),
        P(ROWS, None, None),
        P(),
        P(ROWS),
        P(ROWS),
    )
    return jax.shard_map(on_device, mesh=mesh, in_specs=in_specs, out_specs=P(ROWS, "trait"), check_vma=False)
```

```python
import jax
import jax.numpy as jnp
from jax import lax
from jax.experimental import pallas as pl
from jax.experimental.pallas import tpu as pltpu
from jax.sharding import PartitionSpec as P

BLK = 128
WIN = 4
COLS = 128
TB = 32
UB = 64
ZERO = 3 * TB
EXT = ZERO + 1
UNROLL = 8
BF = jnp.bfloat16
F32 = jnp.float32
ROWS = ("sec", "var")
HBM = pl.BlockSpec(memory_space=pltpu.HBM)
SMEM = pl.BlockSpec(memory_space=pltpu.SMEM)
VM = pl.BlockSpec(memory_space=pltpu.VMEM)
PARAMS = pltpu.CompilerParams(vmem_limit_bytes=16 * 1024 * 1024)
MID = 8
MID_END = TB - MID
HALF1 = (MID_END - MID) // 2
HALF2 = MID


def shaped(blocks, dtype=BF):
    return jax.ShapeDtypeStruct((blocks * BLK, COLS), dtype)


def dot(left, right):
    return jnp.dot(left, right, preferred_element_type=F32)


def at(block, blocks=1):
    start = block * BLK
    return pl.ds(start if isinstance(start, int) else pl.multiple_of(start, BLK), blocks * BLK)


def copy_all(pairs, sems, first=0):
    copies = [pltpu.make_async_copy(a, b, sems.at[first + k]) for k, (a, b) in enumerate(pairs)]
    for copy in copies:
        copy.start()
    return copies


def pieces(blocks):
    return [(k, min(4, blocks - k)) for k in range(0, blocks, 4)]


def whiten_1(place, z, band, mix, w_a, w_b, mix_a, mix_b, zs, bs, sems):
    zcopy = copy_all([(z.at[at(MID - 1, 2 * HALF1 + 2)], zs)], sems)
    cuts = pieces(2 * HALF1)
    bands = copy_all([(band.at[pl.ds(MID + k, n)], bs.at[pl.ds(k, n)]) for k, n in cuts], sems, 1)
    t, a, b = place[0], place[1], place[2]
    pairs = [(z.at[at(0)], w_a.at[at(HALF1)]), (z.at[at(TB - 1)], w_b.at[at(HALF1)])]
    for target, near, far in ((mix_a, a, b), (mix_b, b, a)):
        for i, row in enumerate((t, near)):
            for j, col in enumerate((t, far)):
                pairs.append((mix.at[at(row), at(col)], target.at[at(i), at(j)]))
    others = copy_all(pairs, sems, 1 + len(cuts))
    zcopy[0].wait()
    for (k, n), copy in zip(cuts, bands):
        copy.wait()
        for i in range(k, k + n):
            w = w_a if i < HALF1 else w_b
            w[at(i % HALF1), :] = dot(bs[i], zs[at(i, 3), :]).astype(BF)
    for copy in others:
        copy.wait()


def whiten_2(z, band, w_a, w_b, edge_band, zs, bs, sems):
    zcopies = copy_all(
        [
            (z.at[at(0, HALF2 + 1)], zs.at[at(1, HALF2 + 1)]),
            (z.at[at(MID_END - 1, HALF2 + 1)], zs.at[at(HALF2 + 2, HALF2 + 1)]),
        ],
        sems,
    )
    cuts = [(side, k, n) for side in range(2) for k, n in pieces(HALF2)]
    bands = copy_all(
        [(band.at[pl.ds(side * MID_END + k, n)], bs.at[pl.ds(side * HALF2 + k, n)]) for side, k, n in cuts], sems, 2
    )
    zs[at(0), :] = jnp.zeros((BLK, COLS), BF)
    zs[at(2 * HALF2 + 3), :] = jnp.zeros((BLK, COLS), BF)
    for (side, k, n), copy in zip(cuts, bands):
        if k == 0:
            zcopies[side].wait()
        copy.wait()
        for i in range(k, k + n):
            rows = dot(bs[side * HALF2 + i], zs[at(side * (HALF2 + 2) + i, 3), :])
            (w_a, w_b)[side][at(i), :] = rows.astype(BF)
    edge_band[at(0), :] = bs[0, :, pl.ds(0, BLK)]
    edge_band[at(1), :] = bs[2 * HALF2 - 1, :, pl.ds(2 * BLK, BLK)]


def sums(own_rows, got_rows, mix):
    return dot(own_rows, mix[pl.ds(0, COLS), :]) + dot(got_rows, mix[pl.ds(COLS, COLS), :])


def partial(w_a, got_a, w_b, got_b, mix_a, mix_b, send_a, send_b, own):
    rows = w_a.shape[0]
    for k, (w, got, mix, send) in enumerate(((w_a, got_a, mix_a, send_a), (w_b, got_b, mix_b, send_b))):
        both = sums(w[...], got[...], mix)
        own[pl.ds(k * rows, rows), :] = both[:, :COLS]
        send[...] = both[:, COLS:].astype(BF)


def combine_1(own, far_a, far_b, out):
    for k, far in enumerate((far_a, far_b)):
        rows = (own[at(k * (HALF1 + 1), HALF1 + 1), :] + far[...].astype(F32)).astype(BF)
        out[at(k * HALF1, HALF1), :] = rows[: HALF1 * BLK]
        out[at(2 * HALF1 + k), :] = rows[HALF1 * BLK :]


def combine_2(own, far_a, far_b, out, edge):
    inner = HALF2 - 1
    edge[at(0), :] = own[at(0), :] + far_a[at(0), :].astype(F32)
    out[at(0, inner), :] = (own[at(1, inner), :] + far_a[at(1, inner), :].astype(F32)).astype(BF)
    out[at(inner, inner), :] = (own[at(HALF2, inner), :] + far_b[at(0, inner), :].astype(F32)).astype(BF)
    edge[at(1), :] = own[at(2 * HALF2 - 1), :] + far_b[at(inner), :].astype(F32)


def finish_edge(place, edge, edge_band, got_e, got_o, out):
    odd = place[5] == 1
    nothing = jnp.zeros((BLK, COLS), BF)
    from_left = jnp.where(odd, got_e[at(2 * HALF1 + 1), :], got_o[at(2 * HALF1 + 1), :])
    from_right = jnp.where(odd, got_o[at(2 * HALF1), :], got_e[at(2 * HALF1), :])
    from_left = jnp.where(place[3] == 0, nothing, from_left)
    from_right = jnp.where(place[3] == place[4] - 1, nothing, from_right)
    for k, rows in enumerate((from_left, from_right)):
        out[at(k), :] = (edge[at(k), :] + dot(edge_band[at(k), :], rows)).astype(BF)


def on_ranges(ranges, starts, counts, lowest, ld, ext, out, ready=None):
    total = 0
    parts = []
    for low, high in ranges:
        parts.append((total, low))
        total = total + high - low

    def window_of(n):
        u = n + parts[0][1]
        for before, low in parts[1:]:
            u = jnp.where(n >= before, n - before + low, u)
        return u

    def several(k, carry):
        if ready is not None:
            ready(k)
        for i in range(UNROLL):
            u = window_of(jnp.minimum(UNROLL * k + i, total - 1))
            first = jnp.clip(starts[u] - lowest, 0, 3 * TB - 1)
            have = counts[u]
            window = [ext[at(jnp.where(s < have, jnp.minimum(first + s, ZERO), ZERO)), :] for s in range(WIN)]
            out[at(u), :] = dot(ld[u], jnp.concatenate(window, axis=0)).astype(BF)
        return carry

    lax.fori_loop(0, (total + UNROLL - 1) // UNROLL, several, 0)


def move(ext, block, source, first, blocks):
    ext[at(block, blocks), :] = source[at(first, blocks), :]


LIMITS = (
    MID,
    MID_END - WIN + 1,
    TB,
    TB + 1,
    2 * TB - WIN,
    2 * TB - WIN + 1,
    2 * TB + MID,
    2 * TB + MID_END - WIN + 1,
)


def impute_own(place, starts, counts, below, mid, rest, ld, ext, out, ld_here, sems):
    inner = HALF2 - 1
    low, high = below[3], below[4]
    groups = (high - low + UNROLL - 1) // UNROLL

    def load(k):
        part = pl.ds(pl.multiple_of((low // UNROLL + k) % (UB // UNROLL) * UNROLL, UNROLL), UNROLL)
        return pltpu.make_async_copy(ld.at[part], ld_here.at[part], sems.at[k])

    def ready(k):
        @pl.when(k + 1 < UB // UNROLL)
        def _():
            load(k + 1).wait()

    def rest_ready(k, carry):
        load(k).wait()
        return carry

    for k in range(UB // UNROLL):
        load(k).start()
    move(ext, TB + 1, rest, 0, inner)
    move(ext, TB + MID, mid, 0, 2 * HALF1)
    move(ext, TB + MID_END, rest, inner, inner)
    ext[at(ZERO), :] = jnp.zeros((BLK, COLS), BF)
    load(0).wait()
    on_ranges([(low, high)], starts, counts, place[3] * TB - TB, ld_here, ext, out, ready)
    lax.fori_loop(groups + 1, UB // UNROLL, rest_ready, 0)


def impute_near(place, starts, counts, below, edge, mid_e, mid_o, ld, before, done, ext, out):
    move(ext, TB, edge, 0, 1)
    move(ext, 2 * TB - 1, edge, 1, 1)
    move(ext, 2 * TB * (1 - place[5]) + MID, mid_e, 0, 2 * HALF1)
    move(ext, 2 * TB * place[5] + MID, mid_o, 0, 2 * HALF1)
    ranges = [(below[k], below[k + 1]) for k in (0, 2, 4, 6)]
    on_ranges(ranges, starts, counts, place[3] * TB - TB, ld, ext, out)


def impute_far(place, starts, counts, below, rest_e, rest_o, edge_e, edge_o, ld, before, done, ext, rows, out, sems):
    inner = HALF2 - 1
    for base, rest, edge in ((2 * TB * (1 - place[5]), rest_e, edge_e), (2 * TB * place[5], rest_o, edge_o)):
        move(ext, base, edge, 0, 1)
        move(ext, base + 1, rest, 0, inner)
        move(ext, base + MID_END, rest, inner, inner)
        move(ext, base + TB - 1, edge, 1, 1)
    ranges = [(0, below[0]), (below[1], below[2]), (below[5], below[6]), (below[7], UB)]
    on_ranges(ranges, starts, counts, place[3] * TB - TB, ld, ext, rows)
    quarter = UB // 4
    parts = [(rows.at[at(k, quarter)], out.at[at(k, quarter)]) for k in range(0, UB, quarter)]
    for copy in copy_all(parts, sems):
        copy.wait()


def call(kernel, outs, ins, args, scratch=(), aliases=None):
    return pl.pallas_call(
        kernel,
        name=kernel.__name__,
        out_shape=tuple(shape for shape, _ in outs),
        in_specs=ins,
        out_specs=tuple(spec for _, spec in outs),
        scratch_shapes=list(scratch),
        input_output_aliases=aliases or {},
        compiler_params=PARAMS,
    )(*args)


def in_vmem(*shapes):
    return [(shape, VM) for shape in shapes]


def on_device(z, band, ld, mix, starts, counts):
    t = lax.axis_index("trait")
    g = lax.axis_index(ROWS)
    owners = lax.axis_size(ROWS)
    lane = lax.iota(jnp.int32, 8)
    place = jnp.zeros((8,), jnp.int32)
    for k, value in enumerate((t, t ^ 1, 3 - t, g, owners, g % 2)):
        place = jnp.where(lane == k, value, place)
    pairs_a = [(i, i ^ 1) for i in range(4)]
    pairs_b = [(i, 3 - i) for i in range(4)]
    pairs_e = [(i, i ^ 1) for i in range(owners)]
    pairs_o = [(i, (i + 1) % owners if i % 2 else (i - 1) % owners) for i in range(owners)]

    def along_trait(x, y, pairs_x, pairs_y):
        return lax.ppermute(x, "trait", pairs_x), lax.ppermute(y, "trait", pairs_y)

    def along_rows(x, y):
        return lax.ppermute(x, ROWS, pairs_e), lax.ppermute(y, ROWS, pairs_o)

    z, band, mix, ld = (pltpu.with_memory_space_constraint(x, pltpu.HBM) for x in (z, band, mix, ld))
    mix_part = jax.ShapeDtypeStruct((2 * COLS, 2 * COLS), BF)
    w1a, w1b, mix_a, mix_b = call(
        whiten_1,
        in_vmem(shaped(HALF1 + 1), shaped(HALF1 + 1), mix_part, mix_part),
        [SMEM, HBM, HBM, HBM],
        (place, z, band, mix),
        [
            pltpu.VMEM(((2 * HALF1 + 2) * BLK, COLS), BF),
            pltpu.VMEM((2 * HALF1, BLK, 3 * BLK), BF),
            pltpu.SemaphoreType.DMA((11 + len(pieces(2 * HALF1)),)),
        ],
    )
    got1a, got1b = along_trait(w1a, w1b, pairs_a, pairs_b)
    z, _ = lax.optimization_barrier((z, w1a))
    w2a, w2b, edge_band = call(
        whiten_2,
        in_vmem(shaped(HALF2), shaped(HALF2), shaped(2)),
        [HBM, HBM],
        (z, band),
        [
            pltpu.VMEM(((2 * HALF2 + 4) * BLK, COLS), BF),
            pltpu.VMEM((2 * HALF2, BLK, 3 * BLK), BF),
            pltpu.SemaphoreType.DMA((2 + 2 * len(pieces(HALF2)),)),
        ],
    )
    got2a, got2b = along_trait(w2a, w2b, pairs_a, pairs_b)

    def mixing(w_a, got_a, w_b, got_b):
        blocks = w_a.shape[0] // BLK
        outs = in_vmem(shaped(blocks), shaped(blocks), shaped(2 * blocks, F32))
        send_a, send_b, own = call(partial, outs, [VM] * 6, (w_a, got_a, w_b, got_b, mix_a, mix_b))
        return (own, *along_trait(send_a, send_b, pairs_b, pairs_a)), send_a

    (own1, far1a, far1b), after = mixing(w1a, got1a, w1b, got1b)
    got2a, got2b, _ = lax.optimization_barrier((got2a, got2b, after))
    (own2, far2a, far2b), after = mixing(w2a, got2a, w2b, got2b)
    far1a, far1b, _ = lax.optimization_barrier((far1a, far1b, after))
    (mixed1,) = call(combine_1, in_vmem(shaped(2 * HALF1 + 2)), [VM] * 3, (own1, far1a, far1b))
    mid_e, mid_o = along_rows(mixed1, mixed1)
    far2a, far2b, _ = lax.optimization_barrier((far2a, far2b, mixed1))
    mixed2, edge_sums = call(
        combine_2, in_vmem(shaped(2 * HALF2 - 2), shaped(2, F32)), [VM] * 3, (own2, far2a, far2b)
    )
    rest_e, rest_o = along_rows(mixed2, mixed2)
    starts_here = starts - (g * TB - TB)
    below = jnp.sum(starts_here[None, :] < jnp.array(LIMITS, jnp.int32)[:, None], axis=1, dtype=jnp.int32)
    plan = (place, starts, counts, below)
    ext, done, ld = call(
        impute_own,
        in_vmem(shaped(EXT), shaped(UB), jax.ShapeDtypeStruct(ld.shape, BF)),
        [SMEM] * 4 + [VM] * 2 + [HBM],
        (*plan, mixed1, mixed2, ld),
        [pltpu.SemaphoreType.DMA((UB // UNROLL,))],
    )
    mid_e, mid_o, ext = lax.optimization_barrier((mid_e, mid_o, ext))
    (mixed3,) = call(
        finish_edge, in_vmem(shaped(2)), [SMEM] + [VM] * 4, (place, edge_sums, edge_band, mid_e, mid_o)
    )
    edge_e, edge_o = along_rows(mixed3, mixed3)
    ext, done = call(
        impute_near,
        in_vmem(shaped(EXT), shaped(UB)),
        [SMEM] * 4 + [VM] * 6,
        (*plan, mixed3, mid_e, mid_o, ld, ext, done),
        (),
        {8: 0, 9: 1},
    )
    _, _, out = call(
        impute_far,
        in_vmem(shaped(EXT), shaped(UB)) + [(shaped(UB), HBM)],
        [SMEM] * 4 + [VM] * 7,
        (*plan, rest_e, rest_o, edge_e, edge_o, ld, ext, done),
        [pltpu.SemaphoreType.DMA((4,))],
        {9: 0, 10: 1},
    )
    return out


def solution(mesh):
    in_specs = (
        P(ROWS, "trait"),
        P(ROWS, None, None),
        P(ROWS, None, None),
        P(),
        P(ROWS),
        P(ROWS),
    )
    return jax.shard_map(on_device, mesh=mesh, in_specs=in_specs, out_specs=P(ROWS, "trait"), check_vma=False)
```

```python
import jax
import jax.numpy as jnp
from jax import lax
from jax.experimental import pallas as pl
from jax.experimental.pallas import tpu as pltpu
from jax.sharding import PartitionSpec as P

BLK = 128
WIN = 4
COLS = 128
TB = 32
UB = 64
ZERO = 3 * TB
EXT = ZERO + 1
UNROLL = 8
BF = jnp.bfloat16
F32 = jnp.float32
ROWS = ("sec", "var")
HBM = pl.BlockSpec(memory_space=pltpu.HBM)
SMEM = pl.BlockSpec(memory_space=pltpu.SMEM)
VM = pl.BlockSpec(memory_space=pltpu.VMEM)
PARAMS = pltpu.CompilerParams(vmem_limit_bytes=16 * 1024 * 1024)
MID = 9
MID_END = TB - MID
HALF1 = (MID_END - MID) // 2
HALF2 = MID


def shaped(blocks, dtype=BF):
    return jax.ShapeDtypeStruct((blocks * BLK, COLS), dtype)


def dot(left, right):
    return jnp.dot(left, right, preferred_element_type=F32)


def at(block, blocks=1):
    start = block * BLK
    return pl.ds(start if isinstance(start, int) else pl.multiple_of(start, BLK), blocks * BLK)


def copy_all(pairs, sems, first=0):
    copies = [pltpu.make_async_copy(a, b, sems.at[first + k]) for k, (a, b) in enumerate(pairs)]
    for copy in copies:
        copy.start()
    return copies


def pieces(blocks):
    return [(k, min(4, blocks - k)) for k in range(0, blocks, 4)]


def whiten_1(place, z, band, mix, w_a, w_b, mix_a, mix_b, zs, bs, sems):
    zcopy = copy_all([(z.at[at(MID - 1, 2 * HALF1 + 2)], zs)], sems)
    cuts = pieces(2 * HALF1)
    bands = copy_all([(band.at[pl.ds(MID + k, n)], bs.at[pl.ds(k, n)]) for k, n in cuts], sems, 1)
    t, a, b = place[0], place[1], place[2]
    pairs = [(z.at[at(0)], w_a.at[at(HALF1)]), (z.at[at(TB - 1)], w_b.at[at(HALF1)])]
    for target, near, far in ((mix_a, a, b), (mix_b, b, a)):
        for i, row in enumerate((t, near)):
            for j, col in enumerate((t, far)):
                pairs.append((mix.at[at(row), at(col)], target.at[at(i), at(j)]))
    others = copy_all(pairs, sems, 1 + len(cuts))
    zcopy[0].wait()
    for (k, n), copy in zip(cuts, bands):
        copy.wait()
        for i in range(k, k + n):
            w = w_a if i < HALF1 else w_b
            w[at(i % HALF1), :] = dot(bs[i], zs[at(i, 3), :]).astype(BF)
    for copy in others:
        copy.wait()


def whiten_2(z, band, w_a, w_b, edge_band, zs, bs, sems):
    zcopies = copy_all(
        [
            (z.at[at(0, HALF2 + 1)], zs.at[at(1, HALF2 + 1)]),
            (z.at[at(MID_END - 1, HALF2 + 1)], zs.at[at(HALF2 + 2, HALF2 + 1)]),
        ],
        sems,
    )
    cuts = [(side, k, n) for side in range(2) for k, n in pieces(HALF2)]
    bands = copy_all(
        [(band.at[pl.ds(side * MID_END + k, n)], bs.at[pl.ds(side * HALF2 + k, n)]) for side, k, n in cuts], sems, 2
    )
    zs[at(0), :] = jnp.zeros((BLK, COLS), BF)
    zs[at(2 * HALF2 + 3), :] = jnp.zeros((BLK, COLS), BF)
    for (side, k, n), copy in zip(cuts, bands):
        if k == 0:
            zcopies[side].wait()
        copy.wait()
        for i in range(k, k + n):
            rows = dot(bs[side * HALF2 + i], zs[at(side * (HALF2 + 2) + i, 3), :])
            (w_a, w_b)[side][at(i), :] = rows.astype(BF)
    edge_band[at(0), :] = bs[0, :, pl.ds(0, BLK)]
    edge_band[at(1), :] = bs[2 * HALF2 - 1, :, pl.ds(2 * BLK, BLK)]


def sums(own_rows, got_rows, mix):
    return dot(own_rows, mix[pl.ds(0, COLS), :]) + dot(got_rows, mix[pl.ds(COLS, COLS), :])


def partial(w_a, got_a, w_b, got_b, mix_a, mix_b, send_a, send_b, own):
    rows = w_a.shape[0]
    for k, (w, got, mix, send) in enumerate(((w_a, got_a, mix_a, send_a), (w_b, got_b, mix_b, send_b))):
        both = sums(w[...], got[...], mix)
        own[pl.ds(k * rows, rows), :] = both[:, :COLS]
        send[...] = both[:, COLS:].astype(BF)


def combine_1(own, far_a, far_b, out):
    for k, far in enumerate((far_a, far_b)):
        rows = (own[at(k * (HALF1 + 1), HALF1 + 1), :] + far[...].astype(F32)).astype(BF)
        out[at(k * HALF1, HALF1), :] = rows[: HALF1 * BLK]
        out[at(2 * HALF1 + k), :] = rows[HALF1 * BLK :]


def combine_2(own, far_a, far_b, out, edge):
    inner = HALF2 - 1
    edge[at(0), :] = own[at(0), :] + far_a[at(0), :].astype(F32)
    out[at(0, inner), :] = (own[at(1, inner), :] + far_a[at(1, inner), :].astype(F32)).astype(BF)
    out[at(inner, inner), :] = (own[at(HALF2, inner), :] + far_b[at(0, inner), :].astype(F32)).astype(BF)
    edge[at(1), :] = own[at(2 * HALF2 - 1), :] + far_b[at(inner), :].astype(F32)


def finish_edge(place, edge, edge_band, got_e, got_o, out):
    odd = place[5] == 1
    nothing = jnp.zeros((BLK, COLS), BF)
    from_left = jnp.where(odd, got_e[at(2 * HALF1 + 1), :], got_o[at(2 * HALF1 + 1), :])
    from_right = jnp.where(odd, got_o[at(2 * HALF1), :], got_e[at(2 * HALF1), :])
    from_left = jnp.where(place[3] == 0, nothing, from_left)
    from_right = jnp.where(place[3] == place[4] - 1, nothing, from_right)
    for k, rows in enumerate((from_left, from_right)):
        out[at(k), :] = (edge[at(k), :] + dot(edge_band[at(k), :], rows)).astype(BF)


def on_ranges(ranges, starts, counts, lowest, ld, ext, out, ready=None, send=None):
    total = 0
    parts = []
    for low, high in ranges:
        parts.append((total, low))
        total = total + high - low

    def window_of(n):
        u = n + parts[0][1]
        for before, low in parts[1:]:
            u = jnp.where(n >= before, n - before + low, u)
        return u

    def several(k, carry):
        if ready is not None:
            ready(k)
        for i in range(UNROLL):
            u = window_of(jnp.minimum(UNROLL * k + i, total - 1))
            first = jnp.clip(starts[u] - lowest, 0, 3 * TB - 1)
            have = counts[u]
            window = [ext[at(jnp.where(s < have, jnp.minimum(first + s, ZERO), ZERO)), :] for s in range(WIN)]
            out[at(u), :] = dot(ld[u], jnp.concatenate(window, axis=0)).astype(BF)
        if send is None:
            return carry
        after = UNROLL * (k + 1)
        complete = jnp.where(after < total, window_of(after), UB) // UNROLL
        lax.fori_loop(carry, complete, send, 0)
        return jnp.maximum(carry, complete)

    return lax.fori_loop(0, (total + UNROLL - 1) // UNROLL, several, 0)


def move(ext, block, source, first, blocks):
    ext[at(block, blocks), :] = source[at(first, blocks), :]


LIMITS = (
    MID,
    MID_END - WIN + 1,
    TB,
    TB + 1,
    2 * TB - WIN,
    2 * TB - WIN + 1,
    2 * TB + MID,
    2 * TB + MID_END - WIN + 1,
)


def impute_own(place, starts, counts, below, mid, rest, ld, ext, out, ld_here, sems):
    inner = HALF2 - 1
    low, high = below[3], below[4]
    groups = (high - low + UNROLL - 1) // UNROLL

    def load(k):
        part = pl.ds(pl.multiple_of((low // UNROLL + k) % (UB // UNROLL) * UNROLL, UNROLL), UNROLL)
        return pltpu.make_async_copy(ld.at[part], ld_here.at[part], sems.at[k])

    def ready(k):
        @pl.when(k + 1 < UB // UNROLL)
        def _():
            load(k + 1).wait()

    def rest_ready(k, carry):
        load(k).wait()
        return carry

    for k in range(UB // UNROLL):
        load(k).start()
    move(ext, TB + 1, rest, 0, inner)
    move(ext, TB + MID, mid, 0, 2 * HALF1)
    move(ext, TB + MID_END, rest, inner, inner)
    ext[at(ZERO), :] = jnp.zeros((BLK, COLS), BF)
    load(0).wait()
    on_ranges([(low, high)], starts, counts, place[3] * TB - TB, ld_here, ext, out, ready)
    lax.fori_loop(groups + 1, UB // UNROLL, rest_ready, 0)


def impute_near(place, starts, counts, below, edge, mid_e, mid_o, ld, before, done, ext, out):
    move(ext, TB, edge, 0, 1)
    move(ext, 2 * TB - 1, edge, 1, 1)
    move(ext, 2 * TB * (1 - place[5]) + MID, mid_e, 0, 2 * HALF1)
    move(ext, 2 * TB * place[5] + MID, mid_o, 0, 2 * HALF1)
    ranges = [(below[k], below[k + 1]) for k in (0, 2, 4, 6)]
    on_ranges(ranges, starts, counts, place[3] * TB - TB, ld, ext, out)


def impute_far(place, starts, counts, below, rest_e, rest_o, edge_e, edge_o, ld, before, done, ext, rows, out, sems):
    inner = HALF2 - 1
    for base, rest, edge in ((2 * TB * (1 - place[5]), rest_e, edge_e), (2 * TB * place[5], rest_o, edge_o)):
        move(ext, base, edge, 0, 1)
        move(ext, base + 1, rest, 0, inner)
        move(ext, base + MID_END, rest, inner, inner)
        move(ext, base + TB - 1, edge, 1, 1)
    ranges = [(0, below[0]), (below[1], below[2]), (below[5], below[6]), (below[7], UB)]

    def leave(k):
        part = at(k * UNROLL, UNROLL)
        return pltpu.make_async_copy(rows.at[part], out.at[part], sems.at[k])

    def send(k, carry):
        leave(k).start()
        return carry

    sent = on_ranges(ranges, starts, counts, place[3] * TB - TB, ld, ext, rows, send=send)
    lax.fori_loop(sent, UB // UNROLL, send, 0)
    for k in range(UB // UNROLL):
        leave(k).wait()


def call(kernel, outs, ins, args, scratch=(), aliases=None):
    return pl.pallas_call(
        kernel,
        name=kernel.__name__,
        out_shape=tuple(shape for shape, _ in outs),
        in_specs=ins,
        out_specs=tuple(spec for _, spec in outs),
        scratch_shapes=list(scratch),
        input_output_aliases=aliases or {},
        compiler_params=PARAMS,
    )(*args)


def in_vmem(*shapes):
    return [(shape, VM) for shape in shapes]


def on_device(z, band, ld, mix, starts, counts):
    t = lax.axis_index("trait")
    g = lax.axis_index(ROWS)
    owners = lax.axis_size(ROWS)
    lane = lax.iota(jnp.int32, 8)
    place = jnp.zeros((8,), jnp.int32)
    for k, value in enumerate((t, t ^ 1, 3 - t, g, owners, g % 2)):
        place = jnp.where(lane == k, value, place)
    pairs_a = [(i, i ^ 1) for i in range(4)]
    pairs_b = [(i, 3 - i) for i in range(4)]
    pairs_e = [(i, i ^ 1) for i in range(owners)]
    pairs_o = [(i, (i + 1) % owners if i % 2 else (i - 1) % owners) for i in range(owners)]

    def along_trait(x, y, pairs_x, pairs_y):
        return lax.ppermute(x, "trait", pairs_x), lax.ppermute(y, "trait", pairs_y)

    def along_rows(x, y):
        return lax.ppermute(x, ROWS, pairs_e), lax.ppermute(y, ROWS, pairs_o)

    z, band, mix, ld = (pltpu.with_memory_space_constraint(x, pltpu.HBM) for x in (z, band, mix, ld))
    mix_part = jax.ShapeDtypeStruct((2 * COLS, 2 * COLS), BF)
    w1a, w1b, mix_a, mix_b = call(
        whiten_1,
        in_vmem(shaped(HALF1 + 1), shaped(HALF1 + 1), mix_part, mix_part),
        [SMEM, HBM, HBM, HBM],
        (place, z, band, mix),
        [
            pltpu.VMEM(((2 * HALF1 + 2) * BLK, COLS), BF),
            pltpu.VMEM((2 * HALF1, BLK, 3 * BLK), BF),
            pltpu.SemaphoreType.DMA((11 + len(pieces(2 * HALF1)),)),
        ],
    )
    got1a, got1b = along_trait(w1a, w1b, pairs_a, pairs_b)
    z, _ = lax.optimization_barrier((z, w1a))
    w2a, w2b, edge_band = call(
        whiten_2,
        in_vmem(shaped(HALF2), shaped(HALF2), shaped(2)),
        [HBM, HBM],
        (z, band),
        [
            pltpu.VMEM(((2 * HALF2 + 4) * BLK, COLS), BF),
            pltpu.VMEM((2 * HALF2, BLK, 3 * BLK), BF),
            pltpu.SemaphoreType.DMA((2 + 2 * len(pieces(HALF2)),)),
        ],
    )
    got2a, got2b = along_trait(w2a, w2b, pairs_a, pairs_b)

    def mixing(w_a, got_a, w_b, got_b):
        blocks = w_a.shape[0] // BLK
        outs = in_vmem(shaped(blocks), shaped(blocks), shaped(2 * blocks, F32))
        send_a, send_b, own = call(partial, outs, [VM] * 6, (w_a, got_a, w_b, got_b, mix_a, mix_b))
        return (own, *along_trait(send_a, send_b, pairs_b, pairs_a)), send_a

    (own1, far1a, far1b), after = mixing(w1a, got1a, w1b, got1b)
    got2a, got2b, _ = lax.optimization_barrier((got2a, got2b, after))
    (own2, far2a, far2b), after = mixing(w2a, got2a, w2b, got2b)
    far1a, far1b, _ = lax.optimization_barrier((far1a, far1b, after))
    (mixed1,) = call(combine_1, in_vmem(shaped(2 * HALF1 + 2)), [VM] * 3, (own1, far1a, far1b))
    mid_e, mid_o = along_rows(mixed1, mixed1)
    far2a, far2b, _ = lax.optimization_barrier((far2a, far2b, mixed1))
    mixed2, edge_sums = call(
        combine_2, in_vmem(shaped(2 * HALF2 - 2), shaped(2, F32)), [VM] * 3, (own2, far2a, far2b)
    )
    rest_e, rest_o = along_rows(mixed2, mixed2)
    starts_here = starts - (g * TB - TB)
    below = jnp.sum(starts_here[None, :] < jnp.array(LIMITS, jnp.int32)[:, None], axis=1, dtype=jnp.int32)
    plan = (place, starts, counts, below)
    ext, done, ld = call(
        impute_own,
        in_vmem(shaped(EXT), shaped(UB), jax.ShapeDtypeStruct(ld.shape, BF)),
        [SMEM] * 4 + [VM] * 2 + [HBM],
        (*plan, mixed1, mixed2, ld),
        [pltpu.SemaphoreType.DMA((UB // UNROLL,))],
    )
    mid_e, mid_o, ext = lax.optimization_barrier((mid_e, mid_o, ext))
    (mixed3,) = call(
        finish_edge, in_vmem(shaped(2)), [SMEM] + [VM] * 4, (place, edge_sums, edge_band, mid_e, mid_o)
    )
    edge_e, edge_o = along_rows(mixed3, mixed3)
    ext, done = call(
        impute_near,
        in_vmem(shaped(EXT), shaped(UB)),
        [SMEM] * 4 + [VM] * 6,
        (*plan, mixed3, mid_e, mid_o, ld, ext, done),
        (),
        {8: 0, 9: 1},
    )
    _, _, out = call(
        impute_far,
        in_vmem(shaped(EXT), shaped(UB)) + [(shaped(UB), HBM)],
        [SMEM] * 4 + [VM] * 7,
        (*plan, rest_e, rest_o, edge_e, edge_o, ld, ext, done),
        [pltpu.SemaphoreType.DMA((UB // UNROLL,))],
        {9: 0, 10: 1},
    )
    return out


def solution(mesh):
    in_specs = (
        P(ROWS, "trait"),
        P(ROWS, None, None),
        P(ROWS, None, None),
        P(),
        P(ROWS),
        P(ROWS),
    )
    return jax.shard_map(on_device, mesh=mesh, in_specs=in_specs, out_specs=P(ROWS, "trait"), check_vma=False)
```

```python
import jax
import jax.numpy as jnp
from jax import lax
from jax.experimental import pallas as pl
from jax.experimental.pallas import tpu as pltpu
from jax.sharding import PartitionSpec as P

BLK = 128
WIN = 4
COLS = 128
TB = 32
UB = 64
ZERO = 3 * TB
EXT = ZERO + 1
UNROLL = 8
BF = jnp.bfloat16
F32 = jnp.float32
ROWS = ("sec", "var")
HBM = pl.BlockSpec(memory_space=pltpu.HBM)
SMEM = pl.BlockSpec(memory_space=pltpu.SMEM)
VM = pl.BlockSpec(memory_space=pltpu.VMEM)
PARAMS = pltpu.CompilerParams(vmem_limit_bytes=16 * 1024 * 1024)
MID = 9
MID_END = TB - MID
HALF1 = (MID_END - MID) // 2
HALF2 = MID


def shaped(blocks, dtype=BF):
    return jax.ShapeDtypeStruct((blocks * BLK, COLS), dtype)


def dot(left, right):
    return jnp.dot(left, right, preferred_element_type=F32)


def at(block, blocks=1):
    start = block * BLK
    return pl.ds(start if isinstance(start, int) else pl.multiple_of(start, BLK), blocks * BLK)


def copy_all(pairs, sems, first=0):
    copies = [pltpu.make_async_copy(a, b, sems.at[first + k]) for k, (a, b) in enumerate(pairs)]
    for copy in copies:
        copy.start()
    return copies


def pieces(blocks):
    return [(k, min(4, blocks - k)) for k in range(0, blocks, 4)]


def whiten_1(place, z, band, mix, w_a, w_b, mix_a, mix_b, zs, bs, sems):
    zcopy = copy_all([(z.at[at(MID - 1, 2 * HALF1 + 2)], zs)], sems)
    cuts = pieces(2 * HALF1)
    bands = copy_all([(band.at[pl.ds(MID + k, n)], bs.at[pl.ds(k, n)]) for k, n in cuts], sems, 1)
    t, a, b = place[0], place[1], place[2]
    pairs = [(z.at[at(0)], w_a.at[at(HALF1)]), (z.at[at(TB - 1)], w_b.at[at(HALF1)])]
    for target, near, far in ((mix_a, a, b), (mix_b, b, a)):
        for i, row in enumerate((t, near)):
            for j, col in enumerate((t, far)):
                pairs.append((mix.at[at(row), at(col)], target.at[at(i), at(j)]))
    others = copy_all(pairs, sems, 1 + len(cuts))
    zcopy[0].wait()
    for (k, n), copy in zip(cuts, bands):
        copy.wait()
        for i in range(k, k + n):
            w = w_a if i < HALF1 else w_b
            w[at(i % HALF1), :] = dot(bs[i], zs[at(i, 3), :]).astype(BF)
    for copy in others:
        copy.wait()


def whiten_2(z, band, w_a, w_b, edge_band, zs, bs, sems):
    zcopies = copy_all(
        [
            (z.at[at(0, HALF2 + 1)], zs.at[at(1, HALF2 + 1)]),
            (z.at[at(MID_END - 1, HALF2 + 1)], zs.at[at(HALF2 + 2, HALF2 + 1)]),
        ],
        sems,
    )
    cuts = [(side, k, n) for side in range(2) for k, n in pieces(HALF2)]
    bands = copy_all(
        [(band.at[pl.ds(side * MID_END + k, n)], bs.at[pl.ds(side * HALF2 + k, n)]) for side, k, n in cuts], sems, 2
    )
    zs[at(0), :] = jnp.zeros((BLK, COLS), BF)
    zs[at(2 * HALF2 + 3), :] = jnp.zeros((BLK, COLS), BF)
    for (side, k, n), copy in zip(cuts, bands):
        if k == 0:
            zcopies[side].wait()
        copy.wait()
        for i in range(k, k + n):
            rows = dot(bs[side * HALF2 + i], zs[at(side * (HALF2 + 2) + i, 3), :])
            (w_a, w_b)[side][at(i), :] = rows.astype(BF)
    edge_band[at(0), :] = bs[0, :, pl.ds(0, BLK)]
    edge_band[at(1), :] = bs[2 * HALF2 - 1, :, pl.ds(2 * BLK, BLK)]


def sums(own_rows, got_rows, mix):
    return dot(own_rows, mix[pl.ds(0, COLS), :]) + dot(got_rows, mix[pl.ds(COLS, COLS), :])


def partial(w_a, got_a, w_b, got_b, mix_a, mix_b, send_a, send_b, own):
    rows = w_a.shape[0]
    for k, (w, got, mix, send) in enumerate(((w_a, got_a, mix_a, send_a), (w_b, got_b, mix_b, send_b))):
        both = sums(w[...], got[...], mix)
        own[pl.ds(k * rows, rows), :] = both[:, :COLS]
        send[...] = both[:, COLS:].astype(BF)


def combine_1(own, far_a, far_b, out):
    for k, far in enumerate((far_a, far_b)):
        rows = (own[at(k * (HALF1 + 1), HALF1 + 1), :] + far[...].astype(F32)).astype(BF)
        out[at(k * HALF1, HALF1), :] = rows[: HALF1 * BLK]
        out[at(2 * HALF1 + k), :] = rows[HALF1 * BLK :]


def combine_2(own, far_a, far_b, out, edge):
    inner = HALF2 - 1
    edge[at(0), :] = own[at(0), :] + far_a[at(0), :].astype(F32)
    out[at(0, inner), :] = (own[at(1, inner), :] + far_a[at(1, inner), :].astype(F32)).astype(BF)
    out[at(inner, inner), :] = (own[at(HALF2, inner), :] + far_b[at(0, inner), :].astype(F32)).astype(BF)
    edge[at(1), :] = own[at(2 * HALF2 - 1), :] + far_b[at(inner), :].astype(F32)


def finish_edge(place, edge, edge_band, got_o, got_e, out):
    odd = place[5] == 1
    nothing = jnp.zeros((BLK, COLS), BF)
    from_left = jnp.where(odd, got_e[at(2 * HALF1 + 1), :], got_o[at(2 * HALF1 + 1), :])
    from_right = jnp.where(odd, got_o[at(2 * HALF1), :], got_e[at(2 * HALF1), :])
    from_left = jnp.where(place[3] == 0, nothing, from_left)
    from_right = jnp.where(place[3] == place[4] - 1, nothing, from_right)
    for k, rows in enumerate((from_left, from_right)):
        out[at(k), :] = (edge[at(k), :] + dot(edge_band[at(k), :], rows)).astype(BF)


def on_ranges(ranges, starts, counts, lowest, ld, ext, out, ready=None, send=None):
    total = 0
    parts = []
    for low, high in ranges:
        parts.append((total, low))
        total = total + high - low

    def window_of(n):
        u = n + parts[0][1]
        for before, low in parts[1:]:
            u = jnp.where(n >= before, n - before + low, u)
        return u

    def several(k, carry):
        if ready is not None:
            ready(k)
        for i in range(UNROLL):
            u = window_of(jnp.minimum(UNROLL * k + i, total - 1))
            first = jnp.clip(starts[u] - lowest, 0, 3 * TB - 1)
            have = counts[u]
            window = [ext[at(jnp.where(s < have, jnp.minimum(first + s, ZERO), ZERO)), :] for s in range(WIN)]
            out[at(u), :] = dot(ld[u], jnp.concatenate(window, axis=0)).astype(BF)
        if send is None:
            return carry
        after = UNROLL * (k + 1)
        complete = jnp.where(after < total, window_of(after), UB) // UNROLL
        lax.fori_loop(carry, complete, send, 0)
        return jnp.maximum(carry, complete)

    return lax.fori_loop(0, (total + UNROLL - 1) // UNROLL, several, 0)


def move(ext, block, source, first, blocks):
    ext[at(block, blocks), :] = source[at(first, blocks), :]


LIMITS = (
    MID,
    MID_END - WIN + 1,
    TB,
    TB + 1,
    2 * TB - WIN,
    2 * TB - WIN + 1,
    2 * TB + MID,
    2 * TB + MID_END - WIN + 1,
)


def impute_own(place, starts, counts, below, mid, rest, ld, ext, out, ld_here, sems):
    inner = HALF2 - 1
    low, high = below[3], below[4]
    groups = (high - low + UNROLL - 1) // UNROLL

    def load(k):
        part = pl.ds(pl.multiple_of((low // UNROLL + k) % (UB // UNROLL) * UNROLL, UNROLL), UNROLL)
        return pltpu.make_async_copy(ld.at[part], ld_here.at[part], sems.at[k])

    def ready(k):
        @pl.when(k + 1 < UB // UNROLL)
        def _():
            load(k + 1).wait()

    def rest_ready(k, carry):
        load(k).wait()
        return carry

    for k in range(UB // UNROLL):
        load(k).start()
    move(ext, TB + 1, rest, 0, inner)
    move(ext, TB + MID, mid, 0, 2 * HALF1)
    move(ext, TB + MID_END, rest, inner, inner)
    ext[at(ZERO), :] = jnp.zeros((BLK, COLS), BF)
    load(0).wait()
    on_ranges([(low, high)], starts, counts, place[3] * TB - TB, ld_here, ext, out, ready)
    lax.fori_loop(groups + 1, UB // UNROLL, rest_ready, 0)


def impute_near(place, starts, counts, below, edge, mid_o, mid_e, ld, before, done, ext, out):
    move(ext, TB, edge, 0, 1)
    move(ext, 2 * TB - 1, edge, 1, 1)
    move(ext, 2 * TB * (1 - place[5]) + MID, mid_e, 0, 2 * HALF1)
    move(ext, 2 * TB * place[5] + MID, mid_o, 0, 2 * HALF1)
    ranges = [(below[k], below[k + 1]) for k in (0, 2, 4, 6)]
    on_ranges(ranges, starts, counts, place[3] * TB - TB, ld, ext, out)


def impute_far(place, starts, counts, below, rest_o, rest_e, edge_o, edge_e, ld, before, done, ext, rows, out, sems):
    inner = HALF2 - 1
    for base, rest, edge in ((2 * TB * (1 - place[5]), rest_e, edge_e), (2 * TB * place[5], rest_o, edge_o)):
        move(ext, base, edge, 0, 1)
        move(ext, base + 1, rest, 0, inner)
        move(ext, base + MID_END, rest, inner, inner)
        move(ext, base + TB - 1, edge, 1, 1)
    ranges = [(0, below[0]), (below[1], below[2]), (below[5], below[6]), (below[7], UB)]

    def leave(k):
        part = at(k * UNROLL, UNROLL)
        return pltpu.make_async_copy(rows.at[part], out.at[part], sems.at[k])

    def send(k, carry):
        leave(k).start()
        return carry

    sent = on_ranges(ranges, starts, counts, place[3] * TB - TB, ld, ext, rows, send=send)
    lax.fori_loop(sent, UB // UNROLL, send, 0)
    for k in range(UB // UNROLL):
        leave(k).wait()


def call(kernel, outs, ins, args, scratch=(), aliases=None):
    return pl.pallas_call(
        kernel,
        name=kernel.__name__,
        out_shape=tuple(shape for shape, _ in outs),
        in_specs=ins,
        out_specs=tuple(spec for _, spec in outs),
        scratch_shapes=list(scratch),
        input_output_aliases=aliases or {},
        compiler_params=PARAMS,
    )(*args)


def in_vmem(*shapes):
    return [(shape, VM) for shape in shapes]


def on_device(z, band, ld, mix, starts, counts):
    t = lax.axis_index("trait")
    g = lax.axis_index(ROWS)
    owners = lax.axis_size(ROWS)
    lane = lax.iota(jnp.int32, 8)
    place = jnp.zeros((8,), jnp.int32)
    for k, value in enumerate((t, t ^ 1, 3 - t, g, owners, g % 2)):
        place = jnp.where(lane == k, value, place)
    pairs_a = [(i, i ^ 1) for i in range(4)]
    pairs_b = [(i, 3 - i) for i in range(4)]
    pairs_e = [(i, i ^ 1) for i in range(owners)]
    pairs_o = [(i, (i + 1) % owners if i % 2 else (i - 1) % owners) for i in range(owners)]

    pairs_open = [(i, min(i + 1, owners - 1) if i % 2 else max(i - 1, 0)) for i in range(owners)]

    def along_trait(x, y, pairs_x, pairs_y):
        return lax.ppermute(x, "trait", pairs_x), lax.ppermute(y, "trait", pairs_y)

    def along_rows(x, pairs):
        other = lax.ppermute(x, ROWS, pairs)
        return lax.ppermute(x, ROWS, pairs_e), other

    z, band, mix, ld = (pltpu.with_memory_space_constraint(x, pltpu.HBM) for x in (z, band, mix, ld))
    mix_part = jax.ShapeDtypeStruct((2 * COLS, 2 * COLS), BF)
    w1a, w1b, mix_a, mix_b = call(
        whiten_1,
        in_vmem(shaped(HALF1 + 1), shaped(HALF1 + 1), mix_part, mix_part),
        [SMEM, HBM, HBM, HBM],
        (place, z, band, mix),
        [
            pltpu.VMEM(((2 * HALF1 + 2) * BLK, COLS), BF),
            pltpu.VMEM((2 * HALF1, BLK, 3 * BLK), BF),
            pltpu.SemaphoreType.DMA((11 + len(pieces(2 * HALF1)),)),
        ],
    )
    got1a, got1b = along_trait(w1a, w1b, pairs_a, pairs_b)
    z, _ = lax.optimization_barrier((z, w1a))
    w2a, w2b, edge_band = call(
        whiten_2,
        in_vmem(shaped(HALF2), shaped(HALF2), shaped(2)),
        [HBM, HBM],
        (z, band),
        [
            pltpu.VMEM(((2 * HALF2 + 4) * BLK, COLS), BF),
            pltpu.VMEM((2 * HALF2, BLK, 3 * BLK), BF),
            pltpu.SemaphoreType.DMA((2 + 2 * len(pieces(HALF2)),)),
        ],
    )
    got2a, got2b = along_trait(w2a, w2b, pairs_a, pairs_b)

    def mixing(w_a, got_a, w_b, got_b):
        blocks = w_a.shape[0] // BLK
        outs = in_vmem(shaped(blocks), shaped(blocks), shaped(2 * blocks, F32))
        send_a, send_b, own = call(partial, outs, [VM] * 6, (w_a, got_a, w_b, got_b, mix_a, mix_b))
        return (own, *along_trait(send_a, send_b, pairs_b, pairs_a)), send_a

    (own1, far1a, far1b), after = mixing(w1a, got1a, w1b, got1b)
    got2a, got2b, _ = lax.optimization_barrier((got2a, got2b, after))
    (own2, far2a, far2b), after = mixing(w2a, got2a, w2b, got2b)
    far1a, far1b, _ = lax.optimization_barrier((far1a, far1b, after))
    (mixed1,) = call(combine_1, in_vmem(shaped(2 * HALF1 + 2)), [VM] * 3, (own1, far1a, far1b))
    mid_e, mid_o = along_rows(mixed1, pairs_o)
    far2a, far2b, _ = lax.optimization_barrier((far2a, far2b, mixed1))
    mixed2, edge_sums = call(
        combine_2, in_vmem(shaped(2 * HALF2 - 2), shaped(2, F32)), [VM] * 3, (own2, far2a, far2b)
    )
    rest_e, rest_o = along_rows(mixed2, pairs_open)
    starts_here = starts - (g * TB - TB)
    below = jnp.sum(starts_here[None, :] < jnp.array(LIMITS, jnp.int32)[:, None], axis=1, dtype=jnp.int32)
    plan = (place, starts, counts, below)
    ext, done, ld = call(
        impute_own,
        in_vmem(shaped(EXT), shaped(UB), jax.ShapeDtypeStruct(ld.shape, BF)),
        [SMEM] * 4 + [VM] * 2 + [HBM],
        (*plan, mixed1, mixed2, ld),
        [pltpu.SemaphoreType.DMA((UB // UNROLL,))],
    )
    mid_o, mid_e, ext = lax.optimization_barrier((mid_o, mid_e, ext))
    (mixed3,) = call(
        finish_edge, in_vmem(shaped(2)), [SMEM] + [VM] * 4, (place, edge_sums, edge_band, mid_o, mid_e)
    )
    edge_e, edge_o = along_rows(mixed3, pairs_o)
    ext, done = call(
        impute_near,
        in_vmem(shaped(EXT), shaped(UB)),
        [SMEM] * 4 + [VM] * 6,
        (*plan, mixed3, mid_o, mid_e, ld, ext, done),
        (),
        {8: 0, 9: 1},
    )
    _, _, out = call(
        impute_far,
        in_vmem(shaped(EXT), shaped(UB)) + [(shaped(UB), HBM)],
        [SMEM] * 4 + [VM] * 7,
        (*plan, rest_o, rest_e, edge_o, edge_e, ld, ext, done),
        [pltpu.SemaphoreType.DMA((UB // UNROLL,))],
        {9: 0, 10: 1},
    )
    return out


def solution(mesh):
    in_specs = (
        P(ROWS, "trait"),
        P(ROWS, None, None),
        P(ROWS, None, None),
        P(),
        P(ROWS),
        P(ROWS),
    )
    return jax.shard_map(on_device, mesh=mesh, in_specs=in_specs, out_specs=P(ROWS, "trait"), check_vma=False)
```

```python
import jax
import jax.numpy as jnp
from jax import lax
from jax.experimental import pallas as pl
from jax.experimental.pallas import tpu as pltpu
from jax.sharding import PartitionSpec as P

BLK = 128
WIN = 4
COLS = 128
TB = 32
UB = 64
ZERO = 3 * TB
EXT = ZERO + 1
UNROLL = 8
BF = jnp.bfloat16
F32 = jnp.float32
ROWS = ("sec", "var")
HBM = pl.BlockSpec(memory_space=pltpu.HBM)
SMEM = pl.BlockSpec(memory_space=pltpu.SMEM)
VM = pl.BlockSpec(memory_space=pltpu.VMEM)
PARAMS = pltpu.CompilerParams(vmem_limit_bytes=16 * 1024 * 1024)
MID = 9
MID_END = TB - MID
HALF1 = (MID_END - MID) // 2
HALF2 = MID


def shaped(blocks, dtype=BF):
    return jax.ShapeDtypeStruct((blocks * BLK, COLS), dtype)


def dot(left, right):
    return jnp.dot(left, right, preferred_element_type=F32)


def at(block, blocks=1):
    start = block * BLK
    return pl.ds(start if isinstance(start, int) else pl.multiple_of(start, BLK), blocks * BLK)


def copy_all(pairs, sems, first=0):
    copies = [pltpu.make_async_copy(a, b, sems.at[first + k]) for k, (a, b) in enumerate(pairs)]
    for copy in copies:
        copy.start()
    return copies


def pieces(blocks):
    return [(k, min(4, blocks - k)) for k in range(0, blocks, 4)]


def whiten_1(place, z, band, mix, w_a, w_b, mix_a, mix_b, zs, bs, sems):
    zcopy = copy_all([(z.at[at(MID - 1, 2 * HALF1 + 2)], zs)], sems)
    cuts = pieces(2 * HALF1)
    bands = copy_all([(band.at[pl.ds(MID + k, n)], bs.at[pl.ds(k, n)]) for k, n in cuts], sems, 1)
    t, a, b = place[0], place[1], place[2]
    pairs = [(z.at[at(0)], w_a.at[at(HALF1)]), (z.at[at(TB - 1)], w_b.at[at(HALF1)])]
    for target, near, far in ((mix_a, a, b), (mix_b, b, a)):
        for i, row in enumerate((t, near)):
            for j, col in enumerate((t, far)):
                pairs.append((mix.at[at(row), at(col)], target.at[at(i), at(j)]))
    others = copy_all(pairs, sems, 1 + len(cuts))
    zcopy[0].wait()
    for (k, n), copy in zip(cuts, bands):
        copy.wait()
        for i in range(k, k + n):
            w = w_a if i < HALF1 else w_b
            w[at(i % HALF1), :] = dot(bs[i], zs[at(i, 3), :]).astype(BF)
    for copy in others:
        copy.wait()


def whiten_2(z, band, w_a, w_b, edge_band, zs, bs, sems):
    zcopies = copy_all(
        [
            (z.at[at(0, HALF2 + 1)], zs.at[at(1, HALF2 + 1)]),
            (z.at[at(MID_END - 1, HALF2 + 1)], zs.at[at(HALF2 + 2, HALF2 + 1)]),
        ],
        sems,
    )
    cuts = [(side, k, n) for side in range(2) for k, n in pieces(HALF2)]
    bands = copy_all(
        [(band.at[pl.ds(side * MID_END + k, n)], bs.at[pl.ds(side * HALF2 + k, n)]) for side, k, n in cuts], sems, 2
    )
    zs[at(0), :] = jnp.zeros((BLK, COLS), BF)
    zs[at(2 * HALF2 + 3), :] = jnp.zeros((BLK, COLS), BF)
    for (side, k, n), copy in zip(cuts, bands):
        if k == 0:
            zcopies[side].wait()
        copy.wait()
        for i in range(k, k + n):
            rows = dot(bs[side * HALF2 + i], zs[at(side * (HALF2 + 2) + i, 3), :])
            (w_a, w_b)[side][at(i), :] = rows.astype(BF)
    edge_band[at(0), :] = bs[0, :, pl.ds(0, BLK)]
    edge_band[at(1), :] = bs[2 * HALF2 - 1, :, pl.ds(2 * BLK, BLK)]


def sums(own_rows, got_rows, mix):
    return dot(own_rows, mix[pl.ds(0, COLS), :]) + dot(got_rows, mix[pl.ds(COLS, COLS), :])


def partial(w_a, got_a, w_b, got_b, mix_a, mix_b, send_a, send_b, own):
    rows = w_a.shape[0]
    for k, (w, got, mix, send) in enumerate(((w_a, got_a, mix_a, send_a), (w_b, got_b, mix_b, send_b))):
        both = sums(w[...], got[...], mix)
        own[pl.ds(k * rows, rows), :] = both[:, :COLS]
        send[...] = both[:, COLS:].astype(BF)


def combine_1(own, far_a, far_b, out):
    for k, far in enumerate((far_a, far_b)):
        rows = (own[at(k * (HALF1 + 1), HALF1 + 1), :] + far[...].astype(F32)).astype(BF)
        out[at(k * HALF1, HALF1), :] = rows[: HALF1 * BLK]
        out[at(2 * HALF1 + k), :] = rows[HALF1 * BLK :]


def combine_2(own, far_a, far_b, out, edge):
    inner = HALF2 - 1
    edge[at(0), :] = own[at(0), :] + far_a[at(0), :].astype(F32)
    out[at(0, inner), :] = (own[at(1, inner), :] + far_a[at(1, inner), :].astype(F32)).astype(BF)
    out[at(inner, inner), :] = (own[at(HALF2, inner), :] + far_b[at(0, inner), :].astype(F32)).astype(BF)
    edge[at(1), :] = own[at(2 * HALF2 - 1), :] + far_b[at(inner), :].astype(F32)


def finish_edge(place, edge, edge_band, got_r, got_l, out):
    nothing = jnp.zeros((BLK, COLS), BF)
    from_left = jnp.where(place[3] == 0, nothing, got_l[at(2 * HALF1 + 1), :])
    from_right = jnp.where(place[3] == place[4] - 1, nothing, got_r[at(2 * HALF1), :])
    for k, rows in enumerate((from_left, from_right)):
        out[at(k), :] = (edge[at(k), :] + dot(edge_band[at(k), :], rows)).astype(BF)


def on_ranges(ranges, starts, counts, lowest, ld, ext, out, ready=None, send=None):
    total = 0
    parts = []
    for low, high in ranges:
        parts.append((total, low))
        total = total + high - low

    def window_of(n):
        u = n + parts[0][1]
        for before, low in parts[1:]:
            u = jnp.where(n >= before, n - before + low, u)
        return u

    def several(k, carry):
        if ready is not None:
            ready(k)
        for i in range(UNROLL):
            u = window_of(jnp.minimum(UNROLL * k + i, total - 1))
            first = jnp.clip(starts[u] - lowest, 0, 3 * TB - 1)
            have = counts[u]
            window = [ext[at(jnp.where(s < have, jnp.minimum(first + s, ZERO), ZERO)), :] for s in range(WIN)]
            out[at(u), :] = dot(ld[u], jnp.concatenate(window, axis=0)).astype(BF)
        if send is None:
            return carry
        after = UNROLL * (k + 1)
        complete = jnp.where(after < total, window_of(after), UB) // UNROLL
        lax.fori_loop(carry, complete, send, 0)
        return jnp.maximum(carry, complete)

    return lax.fori_loop(0, (total + UNROLL - 1) // UNROLL, several, 0)


def move(ext, block, source, first, blocks):
    ext[at(block, blocks), :] = source[at(first, blocks), :]


LIMITS = (
    MID,
    MID_END - WIN + 1,
    TB,
    TB + 1,
    2 * TB - WIN,
    2 * TB - WIN + 1,
    2 * TB + MID,
    2 * TB + MID_END - WIN + 1,
)


def impute_own(place, starts, counts, below, mid, rest, ld, ext, out, ld_here, sems):
    inner = HALF2 - 1
    low, high = below[3], below[4]
    groups = (high - low + UNROLL - 1) // UNROLL

    def load(k):
        part = pl.ds(pl.multiple_of((low // UNROLL + k) % (UB // UNROLL) * UNROLL, UNROLL), UNROLL)
        return pltpu.make_async_copy(ld.at[part], ld_here.at[part], sems.at[k])

    def ready(k):
        @pl.when(k + 1 < UB // UNROLL)
        def _():
            load(k + 1).wait()

    def rest_ready(k, carry):
        load(k).wait()
        return carry

    for k in range(UB // UNROLL):
        load(k).start()
    move(ext, TB + 1, rest, 0, inner)
    move(ext, TB + MID, mid, 0, 2 * HALF1)
    move(ext, TB + MID_END, rest, inner, inner)
    ext[at(ZERO), :] = jnp.zeros((BLK, COLS), BF)
    load(0).wait()
    on_ranges([(low, high)], starts, counts, place[3] * TB - TB, ld_here, ext, out, ready)
    lax.fori_loop(groups + 1, UB // UNROLL, rest_ready, 0)


def impute_near(place, starts, counts, below, edge, mid_r, mid_l, ld, before, done, ext, out):
    move(ext, TB, edge, 0, 1)
    move(ext, 2 * TB - 1, edge, 1, 1)
    move(ext, MID, mid_l, 0, 2 * HALF1)
    move(ext, 2 * TB + MID, mid_r, 0, 2 * HALF1)
    ranges = [(below[k], below[k + 1]) for k in (0, 2, 4, 6)]
    on_ranges(ranges, starts, counts, place[3] * TB - TB, ld, ext, out)


def impute_far(place, starts, counts, below, rest_r, rest_l, edge_r, edge_l, ld, before, done, ext, rows, out, sems):
    inner = HALF2 - 1
    for base, rest, edge in ((0, rest_l, edge_l), (2 * TB, rest_r, edge_r)):
        move(ext, base, edge, 0, 1)
        move(ext, base + 1, rest, 0, inner)
        move(ext, base + MID_END, rest, inner, inner)
        move(ext, base + TB - 1, edge, 1, 1)
    ranges = [(0, below[0]), (below[1], below[2]), (below[5], below[6]), (below[7], UB)]

    def leave(k):
        part = at(k * UNROLL, UNROLL)
        return pltpu.make_async_copy(rows.at[part], out.at[part], sems.at[k])

    def send(k, carry):
        leave(k).start()
        return carry

    sent = on_ranges(ranges, starts, counts, place[3] * TB - TB, ld, ext, rows, send=send)
    lax.fori_loop(sent, UB // UNROLL, send, 0)
    for k in range(UB // UNROLL):
        leave(k).wait()


def call(kernel, outs, ins, args, scratch=(), aliases=None):
    return pl.pallas_call(
        kernel,
        name=kernel.__name__,
        out_shape=tuple(shape for shape, _ in outs),
        in_specs=ins,
        out_specs=tuple(spec for _, spec in outs),
        scratch_shapes=list(scratch),
        input_output_aliases=aliases or {},
        compiler_params=PARAMS,
    )(*args)


def in_vmem(*shapes):
    return [(shape, VM) for shape in shapes]


def on_device(z, band, ld, mix, starts, counts):
    t = lax.axis_index("trait")
    g = lax.axis_index(ROWS)
    owners = lax.axis_size(ROWS)
    lane = lax.iota(jnp.int32, 8)
    place = jnp.zeros((8,), jnp.int32)
    for k, value in enumerate((t, t ^ 1, 3 - t, g, owners)):
        place = jnp.where(lane == k, value, place)
    pairs_a = [(i, i ^ 1) for i in range(4)]
    pairs_b = [(i, 3 - i) for i in range(4)]
    open_right = [(i, i + 1) for i in range(owners - 1)]
    open_left = [(i + 1, i) for i in range(owners - 1)]
    right = open_right + [(owners - 1, 0)]
    left = open_left + [(0, owners - 1)]

    def along_trait(x, y, pairs_x, pairs_y):
        return lax.ppermute(x, "trait", pairs_x), lax.ppermute(y, "trait", pairs_y)

    def along_rows(x, to_right, to_left):
        from_right = lax.ppermute(x, ROWS, to_left)
        return from_right, lax.ppermute(x, ROWS, to_right)

    z, band, mix, ld = (pltpu.with_memory_space_constraint(x, pltpu.HBM) for x in (z, band, mix, ld))
    mix_part = jax.ShapeDtypeStruct((2 * COLS, 2 * COLS), BF)
    w1a, w1b, mix_a, mix_b = call(
        whiten_1,
        in_vmem(shaped(HALF1 + 1), shaped(HALF1 + 1), mix_part, mix_part),
        [SMEM, HBM, HBM, HBM],
        (place, z, band, mix),
        [
            pltpu.VMEM(((2 * HALF1 + 2) * BLK, COLS), BF),
            pltpu.VMEM((2 * HALF1, BLK, 3 * BLK), BF),
            pltpu.SemaphoreType.DMA((11 + len(pieces(2 * HALF1)),)),
        ],
    )
    got1a, got1b = along_trait(w1a, w1b, pairs_a, pairs_b)
    z, _ = lax.optimization_barrier((z, w1a))
    w2a, w2b, edge_band = call(
        whiten_2,
        in_vmem(shaped(HALF2), shaped(HALF2), shaped(2)),
        [HBM, HBM],
        (z, band),
        [
            pltpu.VMEM(((2 * HALF2 + 4) * BLK, COLS), BF),
            pltpu.VMEM((2 * HALF2, BLK, 3 * BLK), BF),
            pltpu.SemaphoreType.DMA((2 + 2 * len(pieces(HALF2)),)),
        ],
    )
    got2a, got2b = along_trait(w2a, w2b, pairs_a, pairs_b)

    def mixing(w_a, got_a, w_b, got_b):
        blocks = w_a.shape[0] // BLK
        outs = in_vmem(shaped(blocks), shaped(blocks), shaped(2 * blocks, F32))
        send_a, send_b, own = call(partial, outs, [VM] * 6, (w_a, got_a, w_b, got_b, mix_a, mix_b))
        return (own, *along_trait(send_a, send_b, pairs_b, pairs_a)), send_a

    (own1, far1a, far1b), after = mixing(w1a, got1a, w1b, got1b)
    got2a, got2b, _ = lax.optimization_barrier((got2a, got2b, after))
    (own2, far2a, far2b), after = mixing(w2a, got2a, w2b, got2b)
    far1a, far1b, _ = lax.optimization_barrier((far1a, far1b, after))
    (mixed1,) = call(combine_1, in_vmem(shaped(2 * HALF1 + 2)), [VM] * 3, (own1, far1a, far1b))
    mid_r, mid_l = along_rows(mixed1, right, left)
    far2a, far2b, _ = lax.optimization_barrier((far2a, far2b, mixed1))
    mixed2, edge_sums = call(
        combine_2, in_vmem(shaped(2 * HALF2 - 2), shaped(2, F32)), [VM] * 3, (own2, far2a, far2b)
    )
    rest_r, rest_l = along_rows(mixed2, open_right, open_left)
    starts_here = starts - (g * TB - TB)
    below = jnp.sum(starts_here[None, :] < jnp.array(LIMITS, jnp.int32)[:, None], axis=1, dtype=jnp.int32)
    plan = (place, starts, counts, below)
    ext, done, ld = call(
        impute_own,
        in_vmem(shaped(EXT), shaped(UB), jax.ShapeDtypeStruct(ld.shape, BF)),
        [SMEM] * 4 + [VM] * 2 + [HBM],
        (*plan, mixed1, mixed2, ld),
        [pltpu.SemaphoreType.DMA((UB // UNROLL,))],
    )
    mid_r, mid_l, ext = lax.optimization_barrier((mid_r, mid_l, ext))
    (mixed3,) = call(
        finish_edge, in_vmem(shaped(2)), [SMEM] + [VM] * 4, (place, edge_sums, edge_band, mid_r, mid_l)
    )
    edge_r, edge_l = along_rows(mixed3, right, left)
    ext, done = call(
        impute_near,
        in_vmem(shaped(EXT), shaped(UB)),
        [SMEM] * 4 + [VM] * 6,
        (*plan, mixed3, mid_r, mid_l, ld, ext, done),
        (),
        {8: 0, 9: 1},
    )
    _, _, out = call(
        impute_far,
        in_vmem(shaped(EXT), shaped(UB)) + [(shaped(UB), HBM)],
        [SMEM] * 4 + [VM] * 7,
        (*plan, rest_r, rest_l, edge_r, edge_l, ld, ext, done),
        [pltpu.SemaphoreType.DMA((UB // UNROLL,))],
        {9: 0, 10: 1},
    )
    return out


def solution(mesh):
    in_specs = (
        P(ROWS, "trait"),
        P(ROWS, None, None),
        P(ROWS, None, None),
        P(),
        P(ROWS),
        P(ROWS),
    )
    return jax.shard_map(on_device, mesh=mesh, in_specs=in_specs, out_specs=P(ROWS, "trait"), check_vma=False)
```

```python
import jax
import jax.numpy as jnp
from jax import lax
from jax.experimental import pallas as pl
from jax.experimental.pallas import tpu as pltpu
from jax.sharding import PartitionSpec as P

BLK = 128
WIN = 4
COLS = 128
TB = 32
UB = 64
ZERO = 3 * TB
EXT = ZERO + 1
UNROLL = 8
BF = jnp.bfloat16
F32 = jnp.float32
ROWS = ("sec", "var")
HBM = pl.BlockSpec(memory_space=pltpu.HBM)
SMEM = pl.BlockSpec(memory_space=pltpu.SMEM)
VM = pl.BlockSpec(memory_space=pltpu.VMEM)
PARAMS = pltpu.CompilerParams(vmem_limit_bytes=16 * 1024 * 1024)
MID = 9
MID_END = TB - MID
HALF1 = (MID_END - MID) // 2
HALF2 = MID


def shaped(blocks, dtype=BF):
    return jax.ShapeDtypeStruct((blocks * BLK, COLS), dtype)


def dot(left, right):
    return jnp.dot(left, right, preferred_element_type=F32)


def at(block, blocks=1):
    start = block * BLK
    return pl.ds(start if isinstance(start, int) else pl.multiple_of(start, BLK), blocks * BLK)


def copy_all(pairs, sems, first=0):
    copies = [pltpu.make_async_copy(a, b, sems.at[first + k]) for k, (a, b) in enumerate(pairs)]
    for copy in copies:
        copy.start()
    return copies


def pieces(blocks):
    return [(k, min(4, blocks - k)) for k in range(0, blocks, 4)]


def whiten_1(place, z, band, mix, w_a, w_b, mix_a, mix_b, zs, bs, sems):
    zcopy = copy_all([(z.at[at(MID - 1, 2 * HALF1 + 2)], zs)], sems)
    cuts = pieces(2 * HALF1)
    bands = copy_all([(band.at[pl.ds(MID + k, n)], bs.at[pl.ds(k, n)]) for k, n in cuts], sems, 1)
    t, a, b = place[0], place[1], place[2]
    pairs = [(z.at[at(0)], w_a.at[at(HALF1)]), (z.at[at(TB - 1)], w_b.at[at(HALF1)])]
    for target, near, far in ((mix_a, a, b), (mix_b, b, a)):
        for i, row in enumerate((t, near)):
            for j, col in enumerate((t, far)):
                pairs.append((mix.at[at(row), at(col)], target.at[at(i), at(j)]))
    others = copy_all(pairs, sems, 1 + len(cuts))
    zcopy[0].wait()
    for (k, n), copy in zip(cuts, bands):
        copy.wait()
        for i in range(k, k + n):
            w = w_a if i < HALF1 else w_b
            w[at(i % HALF1), :] = dot(bs[i], zs[at(i, 3), :]).astype(BF)
    for copy in others:
        copy.wait()


def whiten_2(z, band, w_a, w_b, edge_band, zs, bs, sems):
    zcopies = copy_all(
        [
            (z.at[at(0, HALF2 + 1)], zs.at[at(1, HALF2 + 1)]),
            (z.at[at(MID_END - 1, HALF2 + 1)], zs.at[at(HALF2 + 2, HALF2 + 1)]),
        ],
        sems,
    )
    cuts = [(side, k, n) for side in range(2) for k, n in pieces(HALF2)]
    bands = copy_all(
        [(band.at[pl.ds(side * MID_END + k, n)], bs.at[pl.ds(side * HALF2 + k, n)]) for side, k, n in cuts], sems, 2
    )
    zs[at(0), :] = jnp.zeros((BLK, COLS), BF)
    zs[at(2 * HALF2 + 3), :] = jnp.zeros((BLK, COLS), BF)
    for (side, k, n), copy in zip(cuts, bands):
        if k == 0:
            zcopies[side].wait()
        copy.wait()
        for i in range(k, k + n):
            rows = dot(bs[side * HALF2 + i], zs[at(side * (HALF2 + 2) + i, 3), :])
            (w_a, w_b)[side][at(i), :] = rows.astype(BF)
    edge_band[at(0), :] = bs[0, :, pl.ds(0, BLK)]
    edge_band[at(1), :] = bs[2 * HALF2 - 1, :, pl.ds(2 * BLK, BLK)]


def sums(own_rows, got_rows, mix):
    return dot(own_rows, mix[pl.ds(0, COLS), :]) + dot(got_rows, mix[pl.ds(COLS, COLS), :])


def partial(w_a, got_a, w_b, got_b, mix_a, mix_b, send_a, send_b, own):
    rows = w_a.shape[0]
    for k, (w, got, mix, send) in enumerate(((w_a, got_a, mix_a, send_a), (w_b, got_b, mix_b, send_b))):
        both = sums(w[...], got[...], mix)
        own[pl.ds(k * rows, rows), :] = both[:, :COLS]
        send[...] = both[:, COLS:].astype(BF)


def combine_1(own, far_a, far_b, out):
    for k, far in enumerate((far_a, far_b)):
        rows = (own[at(k * (HALF1 + 1), HALF1 + 1), :] + far[...].astype(F32)).astype(BF)
        out[at(k * HALF1, HALF1), :] = rows[: HALF1 * BLK]
        out[at(2 * HALF1 + k), :] = rows[HALF1 * BLK :]


def combine_2(own, far_a, far_b, out, edge):
    inner = HALF2 - 1
    edge[at(0), :] = own[at(0), :] + far_a[at(0), :].astype(F32)
    out[at(0, inner), :] = (own[at(1, inner), :] + far_a[at(1, inner), :].astype(F32)).astype(BF)
    out[at(inner, inner), :] = (own[at(HALF2, inner), :] + far_b[at(0, inner), :].astype(F32)).astype(BF)
    edge[at(1), :] = own[at(2 * HALF2 - 1), :] + far_b[at(inner), :].astype(F32)


def finish_edge(place, edge, edge_band, got_r, got_l, out):
    nothing = jnp.zeros((BLK, COLS), BF)
    from_left = jnp.where(place[3] == 0, nothing, got_l[at(2 * HALF1 + 1), :])
    from_right = jnp.where(place[3] == place[4] - 1, nothing, got_r[at(2 * HALF1), :])
    for k, rows in enumerate((from_left, from_right)):
        out[at(k), :] = (edge[at(k), :] + dot(edge_band[at(k), :], rows)).astype(BF)


def on_ranges(ranges, starts, counts, lowest, ld, ext, out, ready=None, send=None):
    total = 0
    parts = []
    for low, high in ranges:
        parts.append((total, low))
        total = total + high - low

    def window_of(n):
        u = n + parts[0][1]
        for before, low in parts[1:]:
            u = jnp.where(n >= before, n - before + low, u)
        return u

    def several(k, carry):
        if ready is not None:
            ready(k)
        for i in range(UNROLL):
            u = window_of(jnp.minimum(UNROLL * k + i, total - 1))
            first = jnp.clip(starts[u] - lowest, 0, 3 * TB - 1)
            have = counts[u]
            window = [ext[at(jnp.where(s < have, jnp.minimum(first + s, ZERO), ZERO)), :] for s in range(WIN)]
            out[at(u), :] = dot(ld[u], jnp.concatenate(window, axis=0)).astype(BF)
        if send is None:
            return carry
        after = UNROLL * (k + 1)
        complete = jnp.where(after < total, window_of(after), UB) // UNROLL
        lax.fori_loop(carry, complete, send, 0)
        return jnp.maximum(carry, complete)

    return lax.fori_loop(0, (total + UNROLL - 1) // UNROLL, several, 0)


def move(ext, block, source, first, blocks):
    ext[at(block, blocks), :] = source[at(first, blocks), :]


LIMITS = (
    MID,
    MID_END - WIN + 1,
    TB,
    TB + 1,
    2 * TB - WIN,
    2 * TB - WIN + 1,
    2 * TB + MID,
    2 * TB + MID_END - WIN + 1,
)


def impute_own(place, starts, counts, below, mid, rest, ld, ext, out, ld_here, sems):
    inner = HALF2 - 1
    low, high = below[3], below[4]
    groups = (high - low + UNROLL - 1) // UNROLL

    def load(k):
        part = pl.ds(pl.multiple_of((low // UNROLL + k) % (UB // UNROLL) * UNROLL, UNROLL), UNROLL)
        return pltpu.make_async_copy(ld.at[part], ld_here.at[part], sems.at[k])

    def ready(k):
        @pl.when(k + 1 < UB // UNROLL)
        def _():
            load(k + 1).wait()

    def rest_ready(k, carry):
        load(k).wait()
        return carry

    for k in range(UB // UNROLL):
        load(k).start()
    move(ext, TB + 1, rest, 0, inner)
    move(ext, TB + MID, mid, 0, 2 * HALF1)
    move(ext, TB + MID_END, rest, inner, inner)
    ext[at(ZERO), :] = jnp.zeros((BLK, COLS), BF)
    load(0).wait()
    on_ranges([(low, high)], starts, counts, place[3] * TB - TB, ld_here, ext, out, ready)
    lax.fori_loop(groups + 1, UB // UNROLL, rest_ready, 0)


def impute_near(place, starts, counts, below, edge, mid_r, mid_l, ld, before, done, ext, out):
    move(ext, TB, edge, 0, 1)
    move(ext, 2 * TB - 1, edge, 1, 1)
    move(ext, MID, mid_l, 0, 2 * HALF1)
    move(ext, 2 * TB + MID, mid_r, 0, 2 * HALF1)
    ranges = [(below[k], below[k + 1]) for k in (0, 2, 4, 6)]
    on_ranges(ranges, starts, counts, place[3] * TB - TB, ld, ext, out)


def impute_far(place, starts, counts, below, rest_r, rest_l, edge_r, edge_l, ld, before, done, ext, rows, out, sems):
    inner = HALF2 - 1
    for base, rest, edge in ((0, rest_l, edge_l), (2 * TB, rest_r, edge_r)):
        move(ext, base, edge, 0, 1)
        move(ext, base + 1, rest, 0, inner)
        move(ext, base + MID_END, rest, inner, inner)
        move(ext, base + TB - 1, edge, 1, 1)
    ranges = [(0, below[0]), (below[1], below[2]), (below[5], below[6]), (below[7], UB)]

    def leave(k):
        part = at(k * UNROLL, UNROLL)
        return pltpu.make_async_copy(rows.at[part], out.at[part], sems.at[k])

    def send(k, carry):
        leave(k).start()
        return carry

    sent = on_ranges(ranges, starts, counts, place[3] * TB - TB, ld, ext, rows, send=send)
    lax.fori_loop(sent, UB // UNROLL, send, 0)
    for k in range(UB // UNROLL):
        leave(k).wait()


def call(kernel, outs, ins, args, scratch=(), aliases=None):
    return pl.pallas_call(
        kernel,
        name=kernel.__name__,
        out_shape=tuple(shape for shape, _ in outs),
        in_specs=ins,
        out_specs=tuple(spec for _, spec in outs),
        scratch_shapes=list(scratch),
        input_output_aliases=aliases or {},
        compiler_params=PARAMS,
    )(*args)


def in_vmem(*shapes):
    return [(shape, VM) for shape in shapes]


def on_device(z, band, ld, mix, starts, counts):
    t = lax.axis_index("trait")
    g = lax.axis_index(ROWS)
    owners = lax.axis_size(ROWS)
    lane = lax.iota(jnp.int32, 8)
    place = jnp.zeros((8,), jnp.int32)
    for k, value in enumerate((t, t ^ 1, 3 - t, g, owners)):
        place = jnp.where(lane == k, value, place)
    pairs_a = [(i, i ^ 1) for i in range(4)]
    pairs_b = [(i, 3 - i) for i in range(4)]
    open_right = [(i, i + 1) for i in range(owners - 1)]
    right = open_right + [(owners - 1, 0)]
    left = [(target, source) for source, target in right]

    def along_trait(x, y, pairs_x, pairs_y):
        return lax.ppermute(x, "trait", pairs_x), lax.ppermute(y, "trait", pairs_y)

    def along_rows(x, to_right, to_left):
        from_right = lax.ppermute(x, ROWS, to_left)
        return from_right, lax.ppermute(x, ROWS, to_right)

    z, band, mix, ld = (pltpu.with_memory_space_constraint(x, pltpu.HBM) for x in (z, band, mix, ld))
    mix_part = jax.ShapeDtypeStruct((2 * COLS, 2 * COLS), BF)
    w1a, w1b, mix_a, mix_b = call(
        whiten_1,
        in_vmem(shaped(HALF1 + 1), shaped(HALF1 + 1), mix_part, mix_part),
        [SMEM, HBM, HBM, HBM],
        (place, z, band, mix),
        [
            pltpu.VMEM(((2 * HALF1 + 2) * BLK, COLS), BF),
            pltpu.VMEM((2 * HALF1, BLK, 3 * BLK), BF),
            pltpu.SemaphoreType.DMA((11 + len(pieces(2 * HALF1)),)),
        ],
    )
    got1a, got1b = along_trait(w1a, w1b, pairs_a, pairs_b)
    z, _ = lax.optimization_barrier((z, w1a))
    w2a, w2b, edge_band = call(
        whiten_2,
        in_vmem(shaped(HALF2), shaped(HALF2), shaped(2)),
        [HBM, HBM],
        (z, band),
        [
            pltpu.VMEM(((2 * HALF2 + 4) * BLK, COLS), BF),
            pltpu.VMEM((2 * HALF2, BLK, 3 * BLK), BF),
            pltpu.SemaphoreType.DMA((2 + 2 * len(pieces(HALF2)),)),
        ],
    )
    got2a, got2b = along_trait(w2a, w2b, pairs_a, pairs_b)

    def mixing(w_a, got_a, w_b, got_b):
        blocks = w_a.shape[0] // BLK
        outs = in_vmem(shaped(blocks), shaped(blocks), shaped(2 * blocks, F32))
        send_a, send_b, own = call(partial, outs, [VM] * 6, (w_a, got_a, w_b, got_b, mix_a, mix_b))
        return (own, *along_trait(send_a, send_b, pairs_b, pairs_a)), send_a

    (own1, far1a, far1b), after = mixing(w1a, got1a, w1b, got1b)
    got2a, got2b, _ = lax.optimization_barrier((got2a, got2b, after))
    (own2, far2a, far2b), after = mixing(w2a, got2a, w2b, got2b)
    far1a, far1b, _ = lax.optimization_barrier((far1a, far1b, after))
    (mixed1,) = call(combine_1, in_vmem(shaped(2 * HALF1 + 2)), [VM] * 3, (own1, far1a, far1b))
    mid_r, mid_l = along_rows(mixed1, right, left)
    far2a, far2b, _ = lax.optimization_barrier((far2a, far2b, mixed1))
    mixed2, edge_sums = call(
        combine_2, in_vmem(shaped(2 * HALF2 - 2), shaped(2, F32)), [VM] * 3, (own2, far2a, far2b)
    )
    rest_r, rest_l = along_rows(mixed2, open_right, left)
    starts_here = starts - (g * TB - TB)
    below = jnp.sum(starts_here[None, :] < jnp.array(LIMITS, jnp.int32)[:, None], axis=1, dtype=jnp.int32)
    plan = (place, starts, counts, below)
    ext, done, ld = call(
        impute_own,
        in_vmem(shaped(EXT), shaped(UB), jax.ShapeDtypeStruct(ld.shape, BF)),
        [SMEM] * 4 + [VM] * 2 + [HBM],
        (*plan, mixed1, mixed2, ld),
        [pltpu.SemaphoreType.DMA((UB // UNROLL,))],
    )
    mid_r, mid_l, ext = lax.optimization_barrier((mid_r, mid_l, ext))
    (mixed3,) = call(
        finish_edge, in_vmem(shaped(2)), [SMEM] + [VM] * 4, (place, edge_sums, edge_band, mid_r, mid_l)
    )
    edge_r, edge_l = along_rows(mixed3, right, left)
    ext, done = call(
        impute_near,
        in_vmem(shaped(EXT), shaped(UB)),
        [SMEM] * 4 + [VM] * 6,
        (*plan, mixed3, mid_r, mid_l, ld, ext, done),
        (),
        {8: 0, 9: 1},
    )
    _, _, out = call(
        impute_far,
        in_vmem(shaped(EXT), shaped(UB)) + [(shaped(UB), HBM)],
        [SMEM] * 4 + [VM] * 7,
        (*plan, rest_r, rest_l, edge_r, edge_l, ld, ext, done),
        [pltpu.SemaphoreType.DMA((UB // UNROLL,))],
        {9: 0, 10: 1},
    )
    return out


def solution(mesh):
    in_specs = (
        P(ROWS, "trait"),
        P(ROWS, None, None),
        P(ROWS, None, None),
        P(),
        P(ROWS),
        P(ROWS),
    )
    return jax.shard_map(on_device, mesh=mesh, in_specs=in_specs, out_specs=P(ROWS, "trait"), check_vma=False)
```

```python
import jax
import jax.numpy as jnp
from jax import lax
from jax.experimental import pallas as pl
from jax.experimental.pallas import tpu as pltpu
from jax.sharding import PartitionSpec as P

BLK = 128
WIN = 4
COLS = 128
TB = 32
UB = 64
ZERO = 3 * TB
EXT = ZERO + 1
UNROLL = 8
BF = jnp.bfloat16
F32 = jnp.float32
ROWS = ("sec", "var")
HBM = pl.BlockSpec(memory_space=pltpu.HBM)
SMEM = pl.BlockSpec(memory_space=pltpu.SMEM)
VM = pl.BlockSpec(memory_space=pltpu.VMEM)
PARAMS = pltpu.CompilerParams(vmem_limit_bytes=16 * 1024 * 1024)
MID = 9
MID_END = TB - MID
HALF1 = (MID_END - MID) // 2
HALF2 = MID


def shaped(blocks, dtype=BF):
    return jax.ShapeDtypeStruct((blocks * BLK, COLS), dtype)


def dot(left, right):
    return jnp.dot(left, right, preferred_element_type=F32)


def at(block, blocks=1):
    start = block * BLK
    return pl.ds(start if isinstance(start, int) else pl.multiple_of(start, BLK), blocks * BLK)


def copy_all(pairs, sems, first=0):
    copies = [pltpu.make_async_copy(a, b, sems.at[first + k]) for k, (a, b) in enumerate(pairs)]
    for copy in copies:
        copy.start()
    return copies


def pieces(blocks):
    return [(k, min(4, blocks - k)) for k in range(0, blocks, 4)]


def whiten_1(place, z, band, mix, w_a, w_b, mix_a, mix_b, zs, bs, sems):
    zcopy = copy_all([(z.at[at(MID - 1, 2 * HALF1 + 2)], zs)], sems)
    cuts = pieces(2 * HALF1)
    bands = copy_all([(band.at[pl.ds(MID + k, n)], bs.at[pl.ds(k, n)]) for k, n in cuts], sems, 1)
    t, a, b = place[0], place[1], place[2]
    pairs = [(z.at[at(0)], w_a.at[at(HALF1)]), (z.at[at(TB - 1)], w_b.at[at(HALF1)])]
    for target, near, far in ((mix_a, a, b), (mix_b, b, a)):
        for i, row in enumerate((t, near)):
            for j, col in enumerate((t, far)):
                pairs.append((mix.at[at(row), at(col)], target.at[at(i), at(j)]))
    others = copy_all(pairs, sems, 1 + len(cuts))
    zcopy[0].wait()
    for (k, n), copy in zip(cuts, bands):
        copy.wait()
        for i in range(k, k + n):
            w = w_a if i < HALF1 else w_b
            w[at(i % HALF1), :] = dot(bs[i], zs[at(i, 3), :]).astype(BF)
    for copy in others:
        copy.wait()


def whiten_2(z, band, w_a, w_b, edge_band, zs, bs, sems):
    zcopies = copy_all(
        [
            (z.at[at(0, HALF2 + 1)], zs.at[at(1, HALF2 + 1)]),
            (z.at[at(MID_END - 1, HALF2 + 1)], zs.at[at(HALF2 + 2, HALF2 + 1)]),
        ],
        sems,
    )
    cuts = [(side, k, n) for side in range(2) for k, n in pieces(HALF2)]
    bands = copy_all(
        [(band.at[pl.ds(side * MID_END + k, n)], bs.at[pl.ds(side * HALF2 + k, n)]) for side, k, n in cuts], sems, 2
    )
    zs[at(0), :] = jnp.zeros((BLK, COLS), BF)
    zs[at(2 * HALF2 + 3), :] = jnp.zeros((BLK, COLS), BF)
    for (side, k, n), copy in zip(cuts, bands):
        if k == 0:
            zcopies[side].wait()
        copy.wait()
        for i in range(k, k + n):
            rows = dot(bs[side * HALF2 + i], zs[at(side * (HALF2 + 2) + i, 3), :])
            (w_a, w_b)[side][at(i), :] = rows.astype(BF)
    edge_band[at(0), :] = bs[0, :, pl.ds(0, BLK)]
    edge_band[at(1), :] = bs[2 * HALF2 - 1, :, pl.ds(2 * BLK, BLK)]


def sums(own_rows, got_rows, mix):
    return dot(own_rows, mix[pl.ds(0, COLS), :]) + dot(got_rows, mix[pl.ds(COLS, COLS), :])


def partial(w_a, got_a, w_b, got_b, mix_a, mix_b, send_a, send_b, own):
    rows = w_a.shape[0]
    for k, (w, got, mix, send) in enumerate(((w_a, got_a, mix_a, send_a), (w_b, got_b, mix_b, send_b))):
        both = sums(w[...], got[...], mix)
        own[pl.ds(k * rows, rows), :] = both[:, :COLS]
        send[...] = both[:, COLS:].astype(BF)


def combine_1(own, far_a, far_b, out):
    for k, far in enumerate((far_a, far_b)):
        rows = (own[at(k * (HALF1 + 1), HALF1 + 1), :] + far[...].astype(F32)).astype(BF)
        out[at(k * HALF1, HALF1), :] = rows[: HALF1 * BLK]
        out[at(2 * HALF1 + k), :] = rows[HALF1 * BLK :]


def combine_2(own, far_a, far_b, out, edge):
    inner = HALF2 - 1
    edge[at(0), :] = own[at(0), :] + far_a[at(0), :].astype(F32)
    out[at(0, inner), :] = (own[at(1, inner), :] + far_a[at(1, inner), :].astype(F32)).astype(BF)
    out[at(inner, inner), :] = (own[at(HALF2, inner), :] + far_b[at(0, inner), :].astype(F32)).astype(BF)
    edge[at(1), :] = own[at(2 * HALF2 - 1), :] + far_b[at(inner), :].astype(F32)


def finish_edge(place, edge, edge_band, got_r, got_l, out):
    nothing = jnp.zeros((BLK, COLS), BF)
    from_left = jnp.where(place[3] == 0, nothing, got_l[at(2 * HALF1 + 1), :])
    from_right = jnp.where(place[3] == place[4] - 1, nothing, got_r[at(2 * HALF1), :])
    for k, rows in enumerate((from_left, from_right)):
        out[at(k), :] = (edge[at(k), :] + dot(edge_band[at(k), :], rows)).astype(BF)


def on_ranges(ranges, starts, counts, lowest, ld, ext, out, ready=None, send=None):
    total = 0
    parts = []
    for low, high in ranges:
        parts.append((total, low))
        total = total + high - low

    def window_of(n):
        u = n + parts[0][1]
        for before, low in parts[1:]:
            u = jnp.where(n >= before, n - before + low, u)
        return u

    def several(k, carry):
        if ready is not None:
            ready(k)
        for i in range(UNROLL):
            u = window_of(jnp.minimum(UNROLL * k + i, total - 1))
            first = jnp.clip(starts[u] - lowest, 0, 3 * TB - 1)
            have = counts[u]
            window = [ext[at(jnp.where(s < have, jnp.minimum(first + s, ZERO), ZERO)), :] for s in range(WIN)]
            out[at(u), :] = dot(ld[u], jnp.concatenate(window, axis=0)).astype(BF)
        if send is None:
            return carry
        after = UNROLL * (k + 1)
        complete = jnp.where(after < total, window_of(after), UB) // UNROLL
        lax.fori_loop(carry, complete, send, 0)
        return jnp.maximum(carry, complete)

    return lax.fori_loop(0, (total + UNROLL - 1) // UNROLL, several, 0)


def move(ext, block, source, first, blocks):
    ext[at(block, blocks), :] = source[at(first, blocks), :]


LIMITS = (
    MID,
    MID_END - WIN + 1,
    TB,
    TB + 1,
    2 * TB - WIN,
    2 * TB - WIN + 1,
    2 * TB + MID,
    2 * TB + MID_END - WIN + 1,
)


def impute_own(place, starts, counts, below, mid, rest, ld, ext, out, ld_here, sems):
    inner = HALF2 - 1
    low, high = below[3], below[4]
    groups = (high - low + UNROLL - 1) // UNROLL

    def load(k):
        part = pl.ds(pl.multiple_of((low // UNROLL + k) % (UB // UNROLL) * UNROLL, UNROLL), UNROLL)
        return pltpu.make_async_copy(ld.at[part], ld_here.at[part], sems.at[k])

    def ready(k):
        @pl.when(k + 1 < UB // UNROLL)
        def _():
            load(k + 1).wait()

    def rest_ready(k, carry):
        load(k).wait()
        return carry

    for k in range(UB // UNROLL):
        load(k).start()
    move(ext, TB + 1, rest, 0, inner)
    move(ext, TB + MID, mid, 0, 2 * HALF1)
    move(ext, TB + MID_END, rest, inner, inner)
    ext[at(ZERO), :] = jnp.zeros((BLK, COLS), BF)
    load(0).wait()
    on_ranges([(low, high)], starts, counts, place[3] * TB - TB, ld_here, ext, out, ready)
    lax.fori_loop(groups + 1, UB // UNROLL, rest_ready, 0)


def impute_near(place, starts, counts, below, edge, mid_r, mid_l, ld, before, done, ext, out):
    move(ext, TB, edge, 0, 1)
    move(ext, 2 * TB - 1, edge, 1, 1)
    move(ext, MID, mid_l, 0, 2 * HALF1)
    move(ext, 2 * TB + MID, mid_r, 0, 2 * HALF1)
    ranges = [(below[k], below[k + 1]) for k in (0, 2, 4, 6)]
    on_ranges(ranges, starts, counts, place[3] * TB - TB, ld, ext, out)


def impute_far(place, starts, counts, below, rest_r, rest_l, edge_r, edge_l, ld, before, done, ext, rows, out, sems):
    inner = HALF2 - 1
    for base, rest, edge in ((0, rest_l, edge_l), (2 * TB, rest_r, edge_r)):
        move(ext, base, edge, 0, 1)
        move(ext, base + 1, rest, 0, inner)
        move(ext, base + MID_END, rest, inner, inner)
        move(ext, base + TB - 1, edge, 1, 1)
    ranges = [(0, below[0]), (below[1], below[2]), (below[5], below[6]), (below[7], UB)]

    def leave(k):
        part = at(k * UNROLL, UNROLL)
        return pltpu.make_async_copy(rows.at[part], out.at[part], sems.at[k])

    def send(k, carry):
        leave(k).start()
        return carry

    sent = on_ranges(ranges, starts, counts, place[3] * TB - TB, ld, ext, rows, send=send)
    lax.fori_loop(sent, UB // UNROLL, send, 0)
    for k in range(UB // UNROLL):
        leave(k).wait()


def call(kernel, outs, ins, args, scratch=(), aliases=None):
    return pl.pallas_call(
        kernel,
        name=kernel.__name__,
        out_shape=tuple(shape for shape, _ in outs),
        in_specs=ins,
        out_specs=tuple(spec for _, spec in outs),
        scratch_shapes=list(scratch),
        input_output_aliases=aliases or {},
        compiler_params=PARAMS,
    )(*args)


def in_vmem(*shapes):
    return [(shape, VM) for shape in shapes]


def on_device(z, band, ld, mix, starts, counts):
    t = lax.axis_index("trait")
    g = lax.axis_index(ROWS)
    owners = lax.axis_size(ROWS)
    lane = lax.iota(jnp.int32, 8)
    place = jnp.zeros((8,), jnp.int32)
    for k, value in enumerate((t, t ^ 1, 3 - t, g, owners)):
        place = jnp.where(lane == k, value, place)
    pairs_a = [(i, i ^ 1) for i in range(4)]
    pairs_b = [(i, 3 - i) for i in range(4)]
    open_right = [(i, i + 1) for i in range(owners - 1)]
    right = open_right + [(owners - 1, 0)]
    left = [(target, source) for source, target in right]
    open_left = left[:-1]

    def along_trait(x, y, pairs_x, pairs_y):
        return lax.ppermute(x, "trait", pairs_x), lax.ppermute(y, "trait", pairs_y)

    def along_rows(x, to_right, to_left):
        from_right = lax.ppermute(x, ROWS, to_left)
        return from_right, lax.ppermute(x, ROWS, to_right)

    z, band, mix, ld = (pltpu.with_memory_space_constraint(x, pltpu.HBM) for x in (z, band, mix, ld))
    mix_part = jax.ShapeDtypeStruct((2 * COLS, 2 * COLS), BF)
    w1a, w1b, mix_a, mix_b = call(
        whiten_1,
        in_vmem(shaped(HALF1 + 1), shaped(HALF1 + 1), mix_part, mix_part),
        [SMEM, HBM, HBM, HBM],
        (place, z, band, mix),
        [
            pltpu.VMEM(((2 * HALF1 + 2) * BLK, COLS), BF),
            pltpu.VMEM((2 * HALF1, BLK, 3 * BLK), BF),
            pltpu.SemaphoreType.DMA((11 + len(pieces(2 * HALF1)),)),
        ],
    )
    got1a, got1b = along_trait(w1a, w1b, pairs_a, pairs_b)
    z, _ = lax.optimization_barrier((z, w1a))
    w2a, w2b, edge_band = call(
        whiten_2,
        in_vmem(shaped(HALF2), shaped(HALF2), shaped(2)),
        [HBM, HBM],
        (z, band),
        [
            pltpu.VMEM(((2 * HALF2 + 4) * BLK, COLS), BF),
            pltpu.VMEM((2 * HALF2, BLK, 3 * BLK), BF),
            pltpu.SemaphoreType.DMA((2 + 2 * len(pieces(HALF2)),)),
        ],
    )
    got2a, got2b = along_trait(w2a, w2b, pairs_a, pairs_b)

    def mixing(w_a, got_a, w_b, got_b):
        blocks = w_a.shape[0] // BLK
        outs = in_vmem(shaped(blocks), shaped(blocks), shaped(2 * blocks, F32))
        send_a, send_b, own = call(partial, outs, [VM] * 6, (w_a, got_a, w_b, got_b, mix_a, mix_b))
        return (own, *along_trait(send_a, send_b, pairs_b, pairs_a)), send_a

    (own1, far1a, far1b), after = mixing(w1a, got1a, w1b, got1b)
    got2a, got2b, _ = lax.optimization_barrier((got2a, got2b, after))
    (own2, far2a, far2b), after = mixing(w2a, got2a, w2b, got2b)
    far1a, far1b, _ = lax.optimization_barrier((far1a, far1b, after))
    (mixed1,) = call(combine_1, in_vmem(shaped(2 * HALF1 + 2)), [VM] * 3, (own1, far1a, far1b))
    mid_r, mid_l = along_rows(mixed1, right, open_left)
    far2a, far2b, _ = lax.optimization_barrier((far2a, far2b, mixed1))
    mixed2, edge_sums = call(
        combine_2, in_vmem(shaped(2 * HALF2 - 2), shaped(2, F32)), [VM] * 3, (own2, far2a, far2b)
    )
    rest_r, rest_l = along_rows(mixed2, open_right, left)
    starts_here = starts - (g * TB - TB)
    below = jnp.sum(starts_here[None, :] < jnp.array(LIMITS, jnp.int32)[:, None], axis=1, dtype=jnp.int32)
    plan = (place, starts, counts, below)
    ext, done, ld = call(
        impute_own,
        in_vmem(shaped(EXT), shaped(UB), jax.ShapeDtypeStruct(ld.shape, BF)),
        [SMEM] * 4 + [VM] * 2 + [HBM],
        (*plan, mixed1, mixed2, ld),
        [pltpu.SemaphoreType.DMA((UB // UNROLL,))],
    )
    mid_r, mid_l, ext = lax.optimization_barrier((mid_r, mid_l, ext))
    (mixed3,) = call(
        finish_edge, in_vmem(shaped(2)), [SMEM] + [VM] * 4, (place, edge_sums, edge_band, mid_r, mid_l)
    )
    edge_r, edge_l = along_rows(mixed3, right, left)
    ext, done = call(
        impute_near,
        in_vmem(shaped(EXT), shaped(UB)),
        [SMEM] * 4 + [VM] * 6,
        (*plan, mixed3, mid_r, mid_l, ld, ext, done),
        (),
        {8: 0, 9: 1},
    )
    _, _, out = call(
        impute_far,
        in_vmem(shaped(EXT), shaped(UB)) + [(shaped(UB), HBM)],
        [SMEM] * 4 + [VM] * 7,
        (*plan, rest_r, rest_l, edge_r, edge_l, ld, ext, done),
        [pltpu.SemaphoreType.DMA((UB // UNROLL,))],
        {9: 0, 10: 1},
    )
    return out


def solution(mesh):
    in_specs = (
        P(ROWS, "trait"),
        P(ROWS, None, None),
        P(ROWS, None, None),
        P(),
        P(ROWS),
        P(ROWS),
    )
    return jax.shard_map(on_device, mesh=mesh, in_specs=in_specs, out_specs=P(ROWS, "trait"), check_vma=False)
```

```python
import jax
import jax.numpy as jnp
from jax import lax
from jax.experimental import pallas as pl
from jax.experimental.pallas import tpu as pltpu
from jax.sharding import PartitionSpec as P

BLK = 128
WIN = 4
COLS = 128
TB = 32
UB = 64
ZERO = 3 * TB
EXT = ZERO + 1
UNROLL = 8
BF = jnp.bfloat16
F32 = jnp.float32
ROWS = ("sec", "var")
HBM = pl.BlockSpec(memory_space=pltpu.HBM)
SMEM = pl.BlockSpec(memory_space=pltpu.SMEM)
VM = pl.BlockSpec(memory_space=pltpu.VMEM)
PARAMS = pltpu.CompilerParams(vmem_limit_bytes=16 * 1024 * 1024)
MID = 9
MID_END = TB - MID
HALF1 = (MID_END - MID) // 2
HALF2 = MID


def shaped(blocks, dtype=BF):
    return jax.ShapeDtypeStruct((blocks * BLK, COLS), dtype)


def dot(left, right):
    return jnp.dot(left, right, preferred_element_type=F32)


def at(block, blocks=1):
    start = block * BLK
    return pl.ds(start if isinstance(start, int) else pl.multiple_of(start, BLK), blocks * BLK)


def copy_all(pairs, sems, first=0):
    copies = [pltpu.make_async_copy(a, b, sems.at[first + k]) for k, (a, b) in enumerate(pairs)]
    for copy in copies:
        copy.start()
    return copies


def pieces(blocks, most):
    return [(k, min(most, blocks - k)) for k in range(0, blocks, most)]


CUTS1 = pieces(2 * HALF1, 2)
CUTS2 = [(side, k, n) for side in range(2) for k, n in pieces(HALF2, 4)]


def whiten_1(z, band, w_a, w_b, zs, bs, sems):
    zcopy = copy_all([(z.at[at(MID - 1, 2 * HALF1 + 2)], zs)], sems)
    bands = copy_all([(band.at[pl.ds(MID + k, n)], bs.at[pl.ds(k, n)]) for k, n in CUTS1], sems, 1)
    edges = [(z.at[at(0)], w_a.at[at(HALF1)]), (z.at[at(TB - 1)], w_b.at[at(HALF1)])]
    edges = copy_all(edges, sems, 1 + len(CUTS1))
    zcopy[0].wait()
    for (k, n), copy in zip(CUTS1, bands):
        copy.wait()
        for i in range(k, k + n):
            w = w_a if i < HALF1 else w_b
            w[at(i % HALF1), :] = dot(bs[i], zs[at(i, 3), :]).astype(BF)
    for copy in edges:
        copy.wait()


def whiten_2(place, z, band, mix, w_a, w_b, edge_band, mix_a, mix_b, zs, bs, sems):
    zcopies = copy_all(
        [
            (z.at[at(0, HALF2 + 1)], zs.at[at(1, HALF2 + 1)]),
            (z.at[at(MID_END - 1, HALF2 + 1)], zs.at[at(HALF2 + 2, HALF2 + 1)]),
        ],
        sems,
    )
    bands = copy_all(
        [(band.at[pl.ds(side * MID_END + k, n)], bs.at[pl.ds(side * HALF2 + k, n)]) for side, k, n in CUTS2], sems, 2
    )
    t, a, b = place[0], place[1], place[2]
    pairs = []
    for target, near, far in ((mix_a, a, b), (mix_b, b, a)):
        for i, row in enumerate((t, near)):
            for j, col in enumerate((t, far)):
                pairs.append((mix.at[at(row), at(col)], target.at[at(i), at(j)]))
    parts = copy_all(pairs, sems, 2 + len(CUTS2))
    zs[at(0), :] = jnp.zeros((BLK, COLS), BF)
    zs[at(2 * HALF2 + 3), :] = jnp.zeros((BLK, COLS), BF)
    for (side, k, n), copy in zip(CUTS2, bands):
        if k == 0:
            zcopies[side].wait()
        copy.wait()
        for i in range(k, k + n):
            rows = dot(bs[side * HALF2 + i], zs[at(side * (HALF2 + 2) + i, 3), :])
            (w_a, w_b)[side][at(i), :] = rows.astype(BF)
    edge_band[at(0), :] = bs[0, :, pl.ds(0, BLK)]
    edge_band[at(1), :] = bs[2 * HALF2 - 1, :, pl.ds(2 * BLK, BLK)]
    for copy in parts:
        copy.wait()


def sums(own_rows, got_rows, mix):
    return dot(own_rows, mix[pl.ds(0, COLS), :]) + dot(got_rows, mix[pl.ds(COLS, COLS), :])


def partial(w_a, got_a, w_b, got_b, mix_a, mix_b, send_a, send_b, own):
    rows = w_a.shape[0]
    for k, (w, got, mix, send) in enumerate(((w_a, got_a, mix_a, send_a), (w_b, got_b, mix_b, send_b))):
        both = sums(w[...], got[...], mix)
        own[pl.ds(k * rows, rows), :] = both[:, :COLS]
        send[...] = both[:, COLS:].astype(BF)


def combine_1(own, far_a, far_b, out):
    for k, far in enumerate((far_a, far_b)):
        rows = (own[at(k * (HALF1 + 1), HALF1 + 1), :] + far[...].astype(F32)).astype(BF)
        out[at(k * HALF1, HALF1), :] = rows[: HALF1 * BLK]
        out[at(2 * HALF1 + k), :] = rows[HALF1 * BLK :]


def combine_2(own, far_a, far_b, out, edge):
    inner = HALF2 - 1
    edge[at(0), :] = own[at(0), :] + far_a[at(0), :].astype(F32)
    out[at(0, inner), :] = (own[at(1, inner), :] + far_a[at(1, inner), :].astype(F32)).astype(BF)
    out[at(inner, inner), :] = (own[at(HALF2, inner), :] + far_b[at(0, inner), :].astype(F32)).astype(BF)
    edge[at(1), :] = own[at(2 * HALF2 - 1), :] + far_b[at(inner), :].astype(F32)


def finish_edge(place, edge, edge_band, got_o, got_e, out):
    odd = place[5] == 1
    nothing = jnp.zeros((BLK, COLS), BF)
    from_left = jnp.where(odd, got_e[at(2 * HALF1 + 1), :], got_o[at(2 * HALF1 + 1), :])
    from_right = jnp.where(odd, got_o[at(2 * HALF1), :], got_e[at(2 * HALF1), :])
    from_left = jnp.where(place[3] == 0, nothing, from_left)
    from_right = jnp.where(place[3] == place[4] - 1, nothing, from_right)
    for k, rows in enumerate((from_left, from_right)):
        out[at(k), :] = (edge[at(k), :] + dot(edge_band[at(k), :], rows)).astype(BF)


def on_ranges(ranges, starts, counts, lowest, ld, ext, out, ready=None, send=None):
    total = 0
    parts = []
    for low, high in ranges:
        parts.append((total, low))
        total = total + high - low

    def window_of(n):
        u = n + parts[0][1]
        for before, low in parts[1:]:
            u = jnp.where(n >= before, n - before + low, u)
        return u

    def several(k, carry):
        if ready is not None:
            ready(k)
        for i in range(UNROLL):
            u = window_of(jnp.minimum(UNROLL * k + i, total - 1))
            first = jnp.clip(starts[u] - lowest, 0, 3 * TB - 1)
            have = counts[u]
            window = [ext[at(jnp.where(s < have, jnp.minimum(first + s, ZERO), ZERO)), :] for s in range(WIN)]
            out[at(u), :] = dot(ld[u], jnp.concatenate(window, axis=0)).astype(BF)
        if send is None:
            return carry
        after = UNROLL * (k + 1)
        complete = jnp.where(after < total, window_of(after), UB) // UNROLL
        lax.fori_loop(carry, complete, send, 0)
        return jnp.maximum(carry, complete)

    return lax.fori_loop(0, (total + UNROLL - 1) // UNROLL, several, 0)


def move(ext, block, source, first, blocks):
    ext[at(block, blocks), :] = source[at(first, blocks), :]


LIMITS = (
    MID,
    MID_END - WIN + 1,
    TB,
    TB + 1,
    2 * TB - WIN,
    2 * TB - WIN + 1,
    2 * TB + MID,
    2 * TB + MID_END - WIN + 1,
)


def impute_own(place, starts, counts, below, mid, rest, ld, ext, out, ld_here, sems):
    inner = HALF2 - 1
    low, high = below[3], below[4]
    groups = (high - low + UNROLL - 1) // UNROLL

    def load(k):
        part = pl.ds(pl.multiple_of((low // UNROLL + k) % (UB // UNROLL) * UNROLL, UNROLL), UNROLL)
        return pltpu.make_async_copy(ld.at[part], ld_here.at[part], sems.at[k])

    def ready(k):
        @pl.when(k + 1 < UB // UNROLL)
        def _():
            load(k + 1).wait()

    def rest_ready(k, carry):
        load(k).wait()
        return carry

    for k in range(UB // UNROLL):
        load(k).start()
    move(ext, TB + 1, rest, 0, inner)
    move(ext, TB + MID, mid, 0, 2 * HALF1)
    move(ext, TB + MID_END, rest, inner, inner)
    ext[at(ZERO), :] = jnp.zeros((BLK, COLS), BF)
    load(0).wait()
    on_ranges([(low, high)], starts, counts, place[3] * TB - TB, ld_here, ext, out, ready)
    lax.fori_loop(groups + 1, UB // UNROLL, rest_ready, 0)


def impute_near(place, starts, counts, below, edge, mid_o, mid_e, ld, before, done, ext, out):
    move(ext, TB, edge, 0, 1)
    move(ext, 2 * TB - 1, edge, 1, 1)
    move(ext, 2 * TB * (1 - place[5]) + MID, mid_e, 0, 2 * HALF1)
    move(ext, 2 * TB * place[5] + MID, mid_o, 0, 2 * HALF1)
    ranges = [(below[k], below[k + 1]) for k in (0, 2, 4, 6)]
    on_ranges(ranges, starts, counts, place[3] * TB - TB, ld, ext, out)


def impute_far(place, starts, counts, below, rest_o, rest_e, edge_o, edge_e, ld, before, done, ext, rows, out, sems):
    inner = HALF2 - 1
    for base, rest, edge in ((2 * TB * (1 - place[5]), rest_e, edge_e), (2 * TB * place[5], rest_o, edge_o)):
        move(ext, base, edge, 0, 1)
        move(ext, base + 1, rest, 0, inner)
        move(ext, base + MID_END, rest, inner, inner)
        move(ext, base + TB - 1, edge, 1, 1)
    ranges = [(0, below[0]), (below[1], below[2]), (below[5], below[6]), (below[7], UB)]

    def leave(k):
        part = at(k * UNROLL, UNROLL)
        return pltpu.make_async_copy(rows.at[part], out.at[part], sems.at[k])

    def send(k, carry):
        leave(k).start()
        return carry

    sent = on_ranges(ranges, starts, counts, place[3] * TB - TB, ld, ext, rows, send=send)
    lax.fori_loop(sent, UB // UNROLL, send, 0)
    for k in range(UB // UNROLL):
        leave(k).wait()


def call(kernel, outs, ins, args, scratch=(), aliases=None):
    return pl.pallas_call(
        kernel,
        name=kernel.__name__,
        out_shape=tuple(shape for shape, _ in outs),
        in_specs=ins,
        out_specs=tuple(spec for _, spec in outs),
        scratch_shapes=list(scratch),
        input_output_aliases=aliases or {},
        compiler_params=PARAMS,
    )(*args)


def in_vmem(*shapes):
    return [(shape, VM) for shape in shapes]


def on_device(z, band, ld, mix, starts, counts):
    t = lax.axis_index("trait")
    g = lax.axis_index(ROWS)
    owners = lax.axis_size(ROWS)
    lane = lax.iota(jnp.int32, 8)
    place = jnp.zeros((8,), jnp.int32)
    for k, value in enumerate((t, t ^ 1, 3 - t, g, owners, g % 2)):
        place = jnp.where(lane == k, value, place)
    pairs_a = [(i, i ^ 1) for i in range(4)]
    pairs_b = [(i, 3 - i) for i in range(4)]
    pairs_e = [(i, i ^ 1) for i in range(owners)]
    pairs_o = [(i, (i + 1) % owners if i % 2 else (i - 1) % owners) for i in range(owners)]

    pairs_open = [(i, min(i + 1, owners - 1) if i % 2 else max(i - 1, 0)) for i in range(owners)]

    def along_trait(x, y, pairs_x, pairs_y):
        return lax.ppermute(x, "trait", pairs_x), lax.ppermute(y, "trait", pairs_y)

    def along_rows(x, pairs):
        other = lax.ppermute(x, ROWS, pairs)
        return lax.ppermute(x, ROWS, pairs_e), other

    z, band, mix, ld = (pltpu.with_memory_space_constraint(x, pltpu.HBM) for x in (z, band, mix, ld))
    mix_part = jax.ShapeDtypeStruct((2 * COLS, 2 * COLS), BF)
    w1a, w1b = call(
        whiten_1,
        in_vmem(shaped(HALF1 + 1), shaped(HALF1 + 1)),
        [HBM, HBM],
        (z, band),
        [
            pltpu.VMEM(((2 * HALF1 + 2) * BLK, COLS), BF),
            pltpu.VMEM((2 * HALF1, BLK, 3 * BLK), BF),
            pltpu.SemaphoreType.DMA((3 + len(CUTS1),)),
        ],
    )
    got1a, got1b = along_trait(w1a, w1b, pairs_a, pairs_b)
    z, _ = lax.optimization_barrier((z, w1a))
    w2a, w2b, edge_band, mix_a, mix_b = call(
        whiten_2,
        in_vmem(shaped(HALF2), shaped(HALF2), shaped(2), mix_part, mix_part),
        [SMEM, HBM, HBM, HBM],
        (place, z, band, mix),
        [
            pltpu.VMEM(((2 * HALF2 + 4) * BLK, COLS), BF),
            pltpu.VMEM((2 * HALF2, BLK, 3 * BLK), BF),
            pltpu.SemaphoreType.DMA((10 + len(CUTS2),)),
        ],
    )
    got2a, got2b = along_trait(w2a, w2b, pairs_a, pairs_b)

    def mixing(w_a, got_a, w_b, got_b):
        blocks = w_a.shape[0] // BLK
        outs = in_vmem(shaped(blocks), shaped(blocks), shaped(2 * blocks, F32))
        send_a, send_b, own = call(partial, outs, [VM] * 6, (w_a, got_a, w_b, got_b, mix_a, mix_b))
        return (own, *along_trait(send_a, send_b, pairs_b, pairs_a)), send_a

    (own1, far1a, far1b), after = mixing(w1a, got1a, w1b, got1b)
    got2a, got2b, _ = lax.optimization_barrier((got2a, got2b, after))
    (own2, far2a, far2b), after = mixing(w2a, got2a, w2b, got2b)
    far1a, far1b, _ = lax.optimization_barrier((far1a, far1b, after))
    (mixed1,) = call(combine_1, in_vmem(shaped(2 * HALF1 + 2)), [VM] * 3, (own1, far1a, far1b))
    mid_e, mid_o = along_rows(mixed1, pairs_o)
    far2a, far2b, _ = lax.optimization_barrier((far2a, far2b, mixed1))
    mixed2, edge_sums = call(
        combine_2, in_vmem(shaped(2 * HALF2 - 2), shaped(2, F32)), [VM] * 3, (own2, far2a, far2b)
    )
    rest_e, rest_o = along_rows(mixed2, pairs_open)
    starts_here = starts - (g * TB - TB)
    below = jnp.sum(starts_here[None, :] < jnp.array(LIMITS, jnp.int32)[:, None], axis=1, dtype=jnp.int32)
    plan = (place, starts, counts, below)
    ext, done, ld = call(
        impute_own,
        in_vmem(shaped(EXT), shaped(UB), jax.ShapeDtypeStruct(ld.shape, BF)),
        [SMEM] * 4 + [VM] * 2 + [HBM],
        (*plan, mixed1, mixed2, ld),
        [pltpu.SemaphoreType.DMA((UB // UNROLL,))],
    )
    mid_o, mid_e, ext = lax.optimization_barrier((mid_o, mid_e, ext))
    (mixed3,) = call(
        finish_edge, in_vmem(shaped(2)), [SMEM] + [VM] * 4, (place, edge_sums, edge_band, mid_o, mid_e)
    )
    edge_e, edge_o = along_rows(mixed3, pairs_o)
    ext, done = call(
        impute_near,
        in_vmem(shaped(EXT), shaped(UB)),
        [SMEM] * 4 + [VM] * 6,
        (*plan, mixed3, mid_o, mid_e, ld, ext, done),
        (),
        {8: 0, 9: 1},
    )
    _, _, out = call(
        impute_far,
        in_vmem(shaped(EXT), shaped(UB)) + [(shaped(UB), HBM)],
        [SMEM] * 4 + [VM] * 7,
        (*plan, rest_o, rest_e, edge_o, edge_e, ld, ext, done),
        [pltpu.SemaphoreType.DMA((UB // UNROLL,))],
        {9: 0, 10: 1},
    )
    return out


def solution(mesh):
    in_specs = (
        P(ROWS, "trait"),
        P(ROWS, None, None),
        P(ROWS, None, None),
        P(),
        P(ROWS),
        P(ROWS),
    )
    return jax.shard_map(on_device, mesh=mesh, in_specs=in_specs, out_specs=P(ROWS, "trait"), check_vma=False)
```

```python
import jax
import jax.numpy as jnp
from jax import lax
from jax.experimental import pallas as pl
from jax.experimental.pallas import tpu as pltpu
from jax.sharding import PartitionSpec as P

BLK = 128
WIN = 4
COLS = 128
TB = 32
UB = 64
ZERO = 3 * TB
EXT = ZERO + 1
UNROLL = 8
BF = jnp.bfloat16
F32 = jnp.float32
ROWS = ("sec", "var")
HBM = pl.BlockSpec(memory_space=pltpu.HBM)
SMEM = pl.BlockSpec(memory_space=pltpu.SMEM)
VM = pl.BlockSpec(memory_space=pltpu.VMEM)
PARAMS = pltpu.CompilerParams(vmem_limit_bytes=16 * 1024 * 1024)
MID = 9
MID_END = TB - MID
HALF1 = (MID_END - MID) // 2
HALF2 = MID


def shaped(blocks, dtype=BF):
    return jax.ShapeDtypeStruct((blocks * BLK, COLS), dtype)


def dot(left, right):
    return jnp.dot(left, right, preferred_element_type=F32)


def at(block, blocks=1):
    start = block * BLK
    return pl.ds(start if isinstance(start, int) else pl.multiple_of(start, BLK), blocks * BLK)


def copy_all(pairs, sems, first=0):
    copies = [pltpu.make_async_copy(a, b, sems.at[first + k]) for k, (a, b) in enumerate(pairs)]
    for copy in copies:
        copy.start()
    return copies


def pieces(blocks, most):
    return [(k, min(most, blocks - k)) for k in range(0, blocks, most)]


CUTS1 = pieces(2 * HALF1, 4)
CUTS2 = [(side, k, n) for side in range(2) for k, n in pieces(HALF2, 4)]


def whiten_1(z, band, w_a, w_b, zs, bs, sems):
    zcopy = copy_all([(z.at[at(MID - 1, 2 * HALF1 + 2)], zs)], sems)
    bands = copy_all([(band.at[pl.ds(MID + k, n)], bs.at[pl.ds(k, n)]) for k, n in CUTS1], sems, 1)
    edges = [(z.at[at(0)], w_a.at[at(HALF1)]), (z.at[at(TB - 1)], w_b.at[at(HALF1)])]
    edges = copy_all(edges, sems, 1 + len(CUTS1))
    zcopy[0].wait()
    for (k, n), copy in zip(CUTS1, bands):
        copy.wait()
        for i in range(k, k + n):
            w = w_a if i < HALF1 else w_b
            w[at(i % HALF1), :] = dot(bs[i], zs[at(i, 3), :]).astype(BF)
    for copy in edges:
        copy.wait()


def whiten_2(place, z, band, mix, w_a, w_b, edge_band, mix_rows, zs, bs, sems):
    zcopies = copy_all(
        [
            (z.at[at(0, HALF2 + 1)], zs.at[at(1, HALF2 + 1)]),
            (z.at[at(MID_END - 1, HALF2 + 1)], zs.at[at(HALF2 + 2, HALF2 + 1)]),
        ],
        sems,
    )
    bands = copy_all(
        [(band.at[pl.ds(side * MID_END + k, n)], bs.at[pl.ds(side * HALF2 + k, n)]) for side, k, n in CUTS2], sems, 2
    )
    parts = copy_all([(mix.at[at(place[k])], mix_rows.at[at(k)]) for k in range(3)], sems, 2 + len(CUTS2))
    zs[at(0), :] = jnp.zeros((BLK, COLS), BF)
    zs[at(2 * HALF2 + 3), :] = jnp.zeros((BLK, COLS), BF)
    for (side, k, n), copy in zip(CUTS2, bands):
        if k == 0:
            zcopies[side].wait()
        copy.wait()
        for i in range(k, k + n):
            rows = dot(bs[side * HALF2 + i], zs[at(side * (HALF2 + 2) + i, 3), :])
            (w_a, w_b)[side][at(i), :] = rows.astype(BF)
    edge_band[at(0), :] = bs[0, :, pl.ds(0, BLK)]
    edge_band[at(1), :] = bs[2 * HALF2 - 1, :, pl.ds(2 * BLK, BLK)]
    for copy in parts:
        copy.wait()


def partial(place, w_a, got_a, w_b, got_b, mix_rows, send_a, send_b, own):
    rows = w_a.shape[0]
    for k, (w, got, send) in enumerate(((w_a, got_a, send_a), (w_b, got_b, send_b))):
        columns = (at(place[0]), at(place[2 - k]))
        weights = [
            jnp.concatenate([mix_rows[at(row), column] for column in columns], axis=1) for row in (0, 1 + k)
        ]
        both = dot(w[...], weights[0]) + dot(got[...], weights[1])
        own[pl.ds(k * rows, rows), :] = both[:, :COLS]
        send[...] = both[:, COLS:].astype(BF)


def combine_1(own, far_a, far_b, out):
    for k, far in enumerate((far_a, far_b)):
        rows = (own[at(k * (HALF1 + 1), HALF1 + 1), :] + far[...].astype(F32)).astype(BF)
        out[at(k * HALF1, HALF1), :] = rows[: HALF1 * BLK]
        out[at(2 * HALF1 + k), :] = rows[HALF1 * BLK :]


def combine_2(own, far_a, far_b, out, edge):
    inner = HALF2 - 1
    edge[at(0), :] = own[at(0), :] + far_a[at(0), :].astype(F32)
    out[at(0, inner), :] = (own[at(1, inner), :] + far_a[at(1, inner), :].astype(F32)).astype(BF)
    out[at(inner, inner), :] = (own[at(HALF2, inner), :] + far_b[at(0, inner), :].astype(F32)).astype(BF)
    edge[at(1), :] = own[at(2 * HALF2 - 1), :] + far_b[at(inner), :].astype(F32)


def finish_edge(place, edge, edge_band, got_o, got_e, out):
    odd = place[5] == 1
    nothing = jnp.zeros((BLK, COLS), BF)
    from_left = jnp.where(odd, got_e[at(2 * HALF1 + 1), :], got_o[at(2 * HALF1 + 1), :])
    from_right = jnp.where(odd, got_o[at(2 * HALF1), :], got_e[at(2 * HALF1), :])
    from_left = jnp.where(place[3] == 0, nothing, from_left)
    from_right = jnp.where(place[3] == place[4] - 1, nothing, from_right)
    for k, rows in enumerate((from_left, from_right)):
        out[at(k), :] = (edge[at(k), :] + dot(edge_band[at(k), :], rows)).astype(BF)


def on_ranges(ranges, starts, counts, lowest, ld, ext, out, ready=None, send=None):
    total = 0
    parts = []
    for low, high in ranges:
        parts.append((total, low))
        total = total + high - low

    def window_of(n):
        u = n + parts[0][1]
        for before, low in parts[1:]:
            u = jnp.where(n >= before, n - before + low, u)
        return u

    def several(k, carry):
        if ready is not None:
            ready(k)
        for i in range(UNROLL):
            u = window_of(jnp.minimum(UNROLL * k + i, total - 1))
            first = jnp.clip(starts[u] - lowest, 0, 3 * TB - 1)
            have = counts[u]
            window = [ext[at(jnp.where(s < have, jnp.minimum(first + s, ZERO), ZERO)), :] for s in range(WIN)]
            out[at(u), :] = dot(ld[u], jnp.concatenate(window, axis=0)).astype(BF)
        if send is None:
            return carry
        after = UNROLL * (k + 1)
        complete = jnp.where(after < total, window_of(after), UB) // UNROLL
        lax.fori_loop(carry, complete, send, 0)
        return jnp.maximum(carry, complete)

    return lax.fori_loop(0, (total + UNROLL - 1) // UNROLL, several, 0)


def move(ext, block, source, first, blocks):
    ext[at(block, blocks), :] = source[at(first, blocks), :]


LIMITS = (
    MID,
    MID_END - WIN + 1,
    TB,
    TB + 1,
    2 * TB - WIN,
    2 * TB - WIN + 1,
    2 * TB + MID,
    2 * TB + MID_END - WIN + 1,
)


def impute_own(place, starts, counts, below, mid, rest, ld, ext, out, ld_here, sems):
    inner = HALF2 - 1
    low, high = below[3], below[4]
    groups = (high - low + UNROLL - 1) // UNROLL

    def load(k):
        part = pl.ds(pl.multiple_of((low // UNROLL + k) % (UB // UNROLL) * UNROLL, UNROLL), UNROLL)
        return pltpu.make_async_copy(ld.at[part], ld_here.at[part], sems.at[k])

    def ready(k):
        @pl.when(k + 1 < UB // UNROLL)
        def _():
            load(k + 1).wait()

    def rest_ready(k, carry):
        load(k).wait()
        return carry

    for k in range(UB // UNROLL):
        load(k).start()
    move(ext, TB + 1, rest, 0, inner)
    move(ext, TB + MID, mid, 0, 2 * HALF1)
    move(ext, TB + MID_END, rest, inner, inner)
    ext[at(ZERO), :] = jnp.zeros((BLK, COLS), BF)
    load(0).wait()
    on_ranges([(low, high)], starts, counts, place[3] * TB - TB, ld_here, ext, out, ready)
    lax.fori_loop(groups + 1, UB // UNROLL, rest_ready, 0)


def impute_near(place, starts, counts, below, edge, mid_o, mid_e, ld, before, done, ext, out):
    move(ext, TB, edge, 0, 1)
    move(ext, 2 * TB - 1, edge, 1, 1)
    move(ext, 2 * TB * (1 - place[5]) + MID, mid_e, 0, 2 * HALF1)
    move(ext, 2 * TB * place[5] + MID, mid_o, 0, 2 * HALF1)
    ranges = [(below[k], below[k + 1]) for k in (0, 2, 4, 6)]
    on_ranges(ranges, starts, counts, place[3] * TB - TB, ld, ext, out)


def impute_far(place, starts, counts, below, rest_o, rest_e, edge_o, edge_e, ld, before, done, ext, rows, out, sems):
    inner = HALF2 - 1
    for base, rest, edge in ((2 * TB * (1 - place[5]), rest_e, edge_e), (2 * TB * place[5], rest_o, edge_o)):
        move(ext, base, edge, 0, 1)
        move(ext, base + 1, rest, 0, inner)
        move(ext, base + MID_END, rest, inner, inner)
        move(ext, base + TB - 1, edge, 1, 1)
    ranges = [(0, below[0]), (below[1], below[2]), (below[5], below[6]), (below[7], UB)]

    def leave(k):
        part = at(k * UNROLL, UNROLL)
        return pltpu.make_async_copy(rows.at[part], out.at[part], sems.at[k])

    def send(k, carry):
        leave(k).start()
        return carry

    sent = on_ranges(ranges, starts, counts, place[3] * TB - TB, ld, ext, rows, send=send)
    lax.fori_loop(sent, UB // UNROLL, send, 0)
    for k in range(UB // UNROLL):
        leave(k).wait()


def call(kernel, outs, ins, args, scratch=(), aliases=None):
    return pl.pallas_call(
        kernel,
        name=kernel.__name__,
        out_shape=tuple(shape for shape, _ in outs),
        in_specs=ins,
        out_specs=tuple(spec for _, spec in outs),
        scratch_shapes=list(scratch),
        input_output_aliases=aliases or {},
        compiler_params=PARAMS,
    )(*args)


def in_vmem(*shapes):
    return [(shape, VM) for shape in shapes]


def on_device(z, band, ld, mix, starts, counts):
    t = lax.axis_index("trait")
    g = lax.axis_index(ROWS)
    owners = lax.axis_size(ROWS)
    lane = lax.iota(jnp.int32, 8)
    place = jnp.zeros((8,), jnp.int32)
    for k, value in enumerate((t, t ^ 1, 3 - t, g, owners, g % 2)):
        place = jnp.where(lane == k, value, place)
    pairs_a = [(i, i ^ 1) for i in range(4)]
    pairs_b = [(i, 3 - i) for i in range(4)]
    pairs_e = [(i, i ^ 1) for i in range(owners)]
    pairs_o = [(i, (i + 1) % owners if i % 2 else (i - 1) % owners) for i in range(owners)]

    pairs_open = [(i, min(i + 1, owners - 1) if i % 2 else max(i - 1, 0)) for i in range(owners)]

    def along_trait(x, y, pairs_x, pairs_y):
        return lax.ppermute(x, "trait", pairs_x), lax.ppermute(y, "trait", pairs_y)

    def along_rows(x, pairs):
        other = lax.ppermute(x, ROWS, pairs)
        return lax.ppermute(x, ROWS, pairs_e), other

    z, band, mix, ld = (pltpu.with_memory_space_constraint(x, pltpu.HBM) for x in (z, band, mix, ld))
    w1a, w1b = call(
        whiten_1,
        in_vmem(shaped(HALF1 + 1), shaped(HALF1 + 1)),
        [HBM, HBM],
        (z, band),
        [
            pltpu.VMEM(((2 * HALF1 + 2) * BLK, COLS), BF),
            pltpu.VMEM((2 * HALF1, BLK, 3 * BLK), BF),
            pltpu.SemaphoreType.DMA((3 + len(CUTS1),)),
        ],
    )
    got1a, got1b = along_trait(w1a, w1b, pairs_a, pairs_b)
    z, _ = lax.optimization_barrier((z, w1a))
    w2a, w2b, edge_band, mix_rows = call(
        whiten_2,
        in_vmem(shaped(HALF2), shaped(HALF2), shaped(2), jax.ShapeDtypeStruct((3 * COLS, mix.shape[1]), BF)),
        [SMEM, HBM, HBM, HBM],
        (place, z, band, mix),
        [
            pltpu.VMEM(((2 * HALF2 + 4) * BLK, COLS), BF),
            pltpu.VMEM((2 * HALF2, BLK, 3 * BLK), BF),
            pltpu.SemaphoreType.DMA((5 + len(CUTS2),)),
        ],
    )
    got2a, got2b = along_trait(w2a, w2b, pairs_a, pairs_b)

    def mixing(w_a, got_a, w_b, got_b):
        blocks = w_a.shape[0] // BLK
        outs = in_vmem(shaped(blocks), shaped(blocks), shaped(2 * blocks, F32))
        send_a, send_b, own = call(
            partial, outs, [SMEM] + [VM] * 5, (place, w_a, got_a, w_b, got_b, mix_rows)
        )
        return (own, *along_trait(send_a, send_b, pairs_b, pairs_a)), send_a

    (own1, far1a, far1b), after = mixing(w1a, got1a, w1b, got1b)
    got2a, got2b, _ = lax.optimization_barrier((got2a, got2b, after))
    (own2, far2a, far2b), after = mixing(w2a, got2a, w2b, got2b)
    far1a, far1b, _ = lax.optimization_barrier((far1a, far1b, after))
    (mixed1,) = call(combine_1, in_vmem(shaped(2 * HALF1 + 2)), [VM] * 3, (own1, far1a, far1b))
    mid_e, mid_o = along_rows(mixed1, pairs_o)
    far2a, far2b, _ = lax.optimization_barrier((far2a, far2b, mixed1))
    mixed2, edge_sums = call(
        combine_2, in_vmem(shaped(2 * HALF2 - 2), shaped(2, F32)), [VM] * 3, (own2, far2a, far2b)
    )
    rest_e, rest_o = along_rows(mixed2, pairs_open)
    starts_here = starts - (g * TB - TB)
    below = jnp.sum(starts_here[None, :] < jnp.array(LIMITS, jnp.int32)[:, None], axis=1, dtype=jnp.int32)
    plan = (place, starts, counts, below)
    ext, done, ld = call(
        impute_own,
        in_vmem(shaped(EXT), shaped(UB), jax.ShapeDtypeStruct(ld.shape, BF)),
        [SMEM] * 4 + [VM] * 2 + [HBM],
        (*plan, mixed1, mixed2, ld),
        [pltpu.SemaphoreType.DMA((UB // UNROLL,))],
    )
    mid_o, mid_e, ext = lax.optimization_barrier((mid_o, mid_e, ext))
    (mixed3,) = call(
        finish_edge, in_vmem(shaped(2)), [SMEM] + [VM] * 4, (place, edge_sums, edge_band, mid_o, mid_e)
    )
    edge_e, edge_o = along_rows(mixed3, pairs_o)
    ext, done = call(
        impute_near,
        in_vmem(shaped(EXT), shaped(UB)),
        [SMEM] * 4 + [VM] * 6,
        (*plan, mixed3, mid_o, mid_e, ld, ext, done),
        (),
        {8: 0, 9: 1},
    )
    _, _, out = call(
        impute_far,
        in_vmem(shaped(EXT), shaped(UB)) + [(shaped(UB), HBM)],
        [SMEM] * 4 + [VM] * 7,
        (*plan, rest_o, rest_e, edge_o, edge_e, ld, ext, done),
        [pltpu.SemaphoreType.DMA((UB // UNROLL,))],
        {9: 0, 10: 1},
    )
    return out


def solution(mesh):
    in_specs = (
        P(ROWS, "trait"),
        P(ROWS, None, None),
        P(ROWS, None, None),
        P(),
        P(ROWS),
        P(ROWS),
    )
    return jax.shard_map(on_device, mesh=mesh, in_specs=in_specs, out_specs=P(ROWS, "trait"), check_vma=False)
```

```python
import jax
import jax.numpy as jnp
from jax import lax
from jax.experimental import pallas as pl
from jax.experimental.pallas import tpu as pltpu
from jax.sharding import PartitionSpec as P

BLK = 128
WIN = 4
COLS = 128
TB = 32
UB = 64
ZERO = 3 * TB
EXT = ZERO + 1
UNROLL = 8
BF = jnp.bfloat16
F32 = jnp.float32
ROWS = ("sec", "var")
HBM = pl.BlockSpec(memory_space=pltpu.HBM)
SMEM = pl.BlockSpec(memory_space=pltpu.SMEM)
VM = pl.BlockSpec(memory_space=pltpu.VMEM)
PARAMS = pltpu.CompilerParams(vmem_limit_bytes=16 * 1024 * 1024)
MID = 9
MID_END = TB - MID
HALF1 = (MID_END - MID) // 2
HALF2 = MID


def shaped(blocks, dtype=BF):
    return jax.ShapeDtypeStruct((blocks * BLK, COLS), dtype)


def dot(left, right):
    return jnp.dot(left, right, preferred_element_type=F32)


def at(block, blocks=1):
    start = block * BLK
    return pl.ds(start if isinstance(start, int) else pl.multiple_of(start, BLK), blocks * BLK)


def copy_all(pairs, sems, first=0):
    copies = [pltpu.make_async_copy(a, b, sems.at[first + k]) for k, (a, b) in enumerate(pairs)]
    for copy in copies:
        copy.start()
    return copies


def pieces(blocks, most):
    return [(k, min(most, blocks - k)) for k in range(0, blocks, most)]


CUTS1 = pieces(2 * HALF1, 4)
CUTS2 = [(side, k, n) for side in range(2) for k, n in pieces(HALF2, 4)]


def place():
    t = lax.axis_index("trait")
    return t, t ^ 1, 3 - t


def whiten_1(z, band, w_a, w_b, zs, bs, sems):
    zcopy = copy_all([(z.at[at(MID - 1, 2 * HALF1 + 2)], zs)], sems)
    bands = copy_all([(band.at[pl.ds(MID + k, n)], bs.at[pl.ds(k, n)]) for k, n in CUTS1], sems, 1)
    edges = [(z.at[at(0)], w_a.at[at(HALF1)]), (z.at[at(TB - 1)], w_b.at[at(HALF1)])]
    edges = copy_all(edges, sems, 1 + len(CUTS1))
    zcopy[0].wait()
    for (k, n), copy in zip(CUTS1, bands):
        copy.wait()
        for i in range(k, k + n):
            w = w_a if i < HALF1 else w_b
            w[at(i % HALF1), :] = dot(bs[i], zs[at(i, 3), :]).astype(BF)
    for copy in edges:
        copy.wait()


def whiten_2(z, band, mix, w_a, w_b, edge_band, mix_rows, zs, bs, sems):
    zcopies = copy_all(
        [
            (z.at[at(0, HALF2 + 1)], zs.at[at(1, HALF2 + 1)]),
            (z.at[at(MID_END - 1, HALF2 + 1)], zs.at[at(HALF2 + 2, HALF2 + 1)]),
        ],
        sems,
    )
    bands = copy_all(
        [(band.at[pl.ds(side * MID_END + k, n)], bs.at[pl.ds(side * HALF2 + k, n)]) for side, k, n in CUTS2], sems, 2
    )
    parts = copy_all([(mix.at[at(row)], mix_rows.at[at(k)]) for k, row in enumerate(place())], sems, 2 + len(CUTS2))
    zs[at(0), :] = jnp.zeros((BLK, COLS), BF)
    zs[at(2 * HALF2 + 3), :] = jnp.zeros((BLK, COLS), BF)
    for (side, k, n), copy in zip(CUTS2, bands):
        if k == 0:
            zcopies[side].wait()
        copy.wait()
        for i in range(k, k + n):
            rows = dot(bs[side * HALF2 + i], zs[at(side * (HALF2 + 2) + i, 3), :])
            (w_a, w_b)[side][at(i), :] = rows.astype(BF)
    edge_band[at(0), :] = bs[0, :, pl.ds(0, BLK)]
    edge_band[at(1), :] = bs[2 * HALF2 - 1, :, pl.ds(2 * BLK, BLK)]
    for copy in parts:
        copy.wait()


def partial(w_a, got_a, w_b, got_b, mix_rows, send_a, send_b, own):
    here = place()
    rows = w_a.shape[0]
    for k, (w, got, send) in enumerate(((w_a, got_a, send_a), (w_b, got_b, send_b))):
        columns = (at(here[0]), at(here[2 - k]))
        weights = [
            jnp.concatenate([mix_rows[at(row), column] for column in columns], axis=1) for row in (0, 1 + k)
        ]
        both = dot(w[...], weights[0]) + dot(got[...], weights[1])
        own[pl.ds(k * rows, rows), :] = both[:, :COLS]
        send[...] = both[:, COLS:].astype(BF)


def combine_1(own, far_a, far_b, out):
    for k, far in enumerate((far_a, far_b)):
        rows = (own[at(k * (HALF1 + 1), HALF1 + 1), :] + far[...].astype(F32)).astype(BF)
        out[at(k * HALF1, HALF1), :] = rows[: HALF1 * BLK]
        out[at(2 * HALF1 + k), :] = rows[HALF1 * BLK :]


def combine_2(own, far_a, far_b, out, edge):
    inner = HALF2 - 1
    edge[at(0), :] = own[at(0), :] + far_a[at(0), :].astype(F32)
    out[at(0, inner), :] = (own[at(1, inner), :] + far_a[at(1, inner), :].astype(F32)).astype(BF)
    out[at(inner, inner), :] = (own[at(HALF2, inner), :] + far_b[at(0, inner), :].astype(F32)).astype(BF)
    edge[at(1), :] = own[at(2 * HALF2 - 1), :] + far_b[at(inner), :].astype(F32)


def finish_edge(edge, edge_band, got_o, got_e, out):
    g = lax.axis_index(ROWS)
    odd = g % 2 == 1
    nothing = jnp.zeros((BLK, COLS), BF)
    from_left = jnp.where(odd, got_e[at(2 * HALF1 + 1), :], got_o[at(2 * HALF1 + 1), :])
    from_right = jnp.where(odd, got_o[at(2 * HALF1), :], got_e[at(2 * HALF1), :])
    from_left = jnp.where(g == 0, nothing, from_left)
    from_right = jnp.where(g == lax.axis_size(ROWS) - 1, nothing, from_right)
    for k, rows in enumerate((from_left, from_right)):
        out[at(k), :] = (edge[at(k), :] + dot(edge_band[at(k), :], rows)).astype(BF)


def on_ranges(ranges, plan, ld, ext, out, ready=None, send=None):
    total = 0
    parts = []
    for low, high in ranges:
        parts.append((total, low))
        total = total + high - low

    def window_of(n):
        u = n + parts[0][1]
        for before, low in parts[1:]:
            u = jnp.where(n >= before, n - before + low, u)
        return u

    def several(k, carry):
        if ready is not None:
            ready(k)
        for i in range(UNROLL):
            u = window_of(jnp.minimum(UNROLL * k + i, total - 1))
            first = jnp.clip(plan[u], 0, 3 * TB - 1)
            have = plan[UB + u]
            window = [ext[at(jnp.where(s < have, jnp.minimum(first + s, ZERO), ZERO)), :] for s in range(WIN)]
            out[at(u), :] = dot(ld[u], jnp.concatenate(window, axis=0)).astype(BF)
        if send is None:
            return carry
        after = UNROLL * (k + 1)
        complete = jnp.where(after < total, window_of(after), UB) // UNROLL
        lax.fori_loop(carry, complete, send, 0)
        return jnp.maximum(carry, complete)

    return lax.fori_loop(0, (total + UNROLL - 1) // UNROLL, several, 0)


def move(ext, block, source, first, blocks):
    ext[at(block, blocks), :] = source[at(first, blocks), :]


LIMITS = (
    MID,
    MID_END - WIN + 1,
    TB,
    TB + 1,
    2 * TB - WIN,
    2 * TB - WIN + 1,
    2 * TB + MID,
    2 * TB + MID_END - WIN + 1,
)


def impute_own(plan, mid, rest, ld, ext, out, ld_here, sems):
    inner = HALF2 - 1
    low, high = plan[2 * UB + 3], plan[2 * UB + 4]
    groups = (high - low + UNROLL - 1) // UNROLL

    def load(k):
        part = pl.ds(pl.multiple_of((low // UNROLL + k) % (UB // UNROLL) * UNROLL, UNROLL), UNROLL)
        return pltpu.make_async_copy(ld.at[part], ld_here.at[part], sems.at[k])

    def ready(k):
        @pl.when(k + 1 < UB // UNROLL)
        def _():
            load(k + 1).wait()

    def rest_ready(k, carry):
        load(k).wait()
        return carry

    for k in range(UB // UNROLL):
        load(k).start()
    move(ext, TB + 1, rest, 0, inner)
    move(ext, TB + MID, mid, 0, 2 * HALF1)
    move(ext, TB + MID_END, rest, inner, inner)
    ext[at(ZERO), :] = jnp.zeros((BLK, COLS), BF)
    load(0).wait()
    on_ranges([(low, high)], plan, ld_here, ext, out, ready)
    lax.fori_loop(groups + 1, UB // UNROLL, rest_ready, 0)


def impute_near(plan, edge, mid_o, mid_e, ld, before, done, ext, out):
    move(ext, TB, edge, 0, 1)
    move(ext, 2 * TB - 1, edge, 1, 1)
    move(ext, 2 * TB * (1 - lax.axis_index(ROWS) % 2) + MID, mid_e, 0, 2 * HALF1)
    move(ext, 2 * TB * (lax.axis_index(ROWS) % 2) + MID, mid_o, 0, 2 * HALF1)
    ranges = [(plan[2 * UB + k], plan[2 * UB + k + 1]) for k in (0, 2, 4, 6)]
    on_ranges(ranges, plan, ld, ext, out)


def impute_far(plan, rest_o, rest_e, edge_o, edge_e, ld, before, done, ext, rows, out, sems):
    inner = HALF2 - 1
    for base, rest, edge in ((2 * TB * (1 - lax.axis_index(ROWS) % 2), rest_e, edge_e), (2 * TB * (lax.axis_index(ROWS) % 2), rest_o, edge_o)):
        move(ext, base, edge, 0, 1)
        move(ext, base + 1, rest, 0, inner)
        move(ext, base + MID_END, rest, inner, inner)
        move(ext, base + TB - 1, edge, 1, 1)
    ranges = [(0, plan[2 * UB + 0]), (plan[2 * UB + 1], plan[2 * UB + 2]), (plan[2 * UB + 5], plan[2 * UB + 6]), (plan[2 * UB + 7], UB)]

    def leave(k):
        part = at(k * UNROLL, UNROLL)
        return pltpu.make_async_copy(rows.at[part], out.at[part], sems.at[k])

    def send(k, carry):
        leave(k).start()
        return carry

    sent = on_ranges(ranges, plan, ld, ext, rows, send=send)
    lax.fori_loop(sent, UB // UNROLL, send, 0)
    for k in range(UB // UNROLL):
        leave(k).wait()


def call(kernel, outs, ins, args, scratch=(), aliases=None):
    return pl.pallas_call(
        kernel,
        name=kernel.__name__,
        out_shape=tuple(shape for shape, _ in outs),
        in_specs=ins,
        out_specs=tuple(spec for _, spec in outs),
        scratch_shapes=list(scratch),
        input_output_aliases=aliases or {},
        compiler_params=PARAMS,
    )(*args)


def in_vmem(*shapes):
    return [(shape, VM) for shape in shapes]


def on_device(z, band, ld, mix, starts, counts):
    g = lax.axis_index(ROWS)
    owners = lax.axis_size(ROWS)
    pairs_a = [(i, i ^ 1) for i in range(4)]
    pairs_b = [(i, 3 - i) for i in range(4)]
    pairs_e = [(i, i ^ 1) for i in range(owners)]
    pairs_o = [(i, (i + 1) % owners if i % 2 else (i - 1) % owners) for i in range(owners)]

    pairs_open = [(i, min(i + 1, owners - 1) if i % 2 else max(i - 1, 0)) for i in range(owners)]

    def along_trait(x, y, pairs_x, pairs_y):
        return lax.ppermute(x, "trait", pairs_x), lax.ppermute(y, "trait", pairs_y)

    def along_rows(x, pairs):
        other = lax.ppermute(x, ROWS, pairs)
        return lax.ppermute(x, ROWS, pairs_e), other

    z, band, mix, ld = (pltpu.with_memory_space_constraint(x, pltpu.HBM) for x in (z, band, mix, ld))
    w1a, w1b = call(
        whiten_1,
        in_vmem(shaped(HALF1 + 1), shaped(HALF1 + 1)),
        [HBM, HBM],
        (z, band),
        [
            pltpu.VMEM(((2 * HALF1 + 2) * BLK, COLS), BF),
            pltpu.VMEM((2 * HALF1, BLK, 3 * BLK), BF),
            pltpu.SemaphoreType.DMA((3 + len(CUTS1),)),
        ],
    )
    got1a, got1b = along_trait(w1a, w1b, pairs_a, pairs_b)
    z, _ = lax.optimization_barrier((z, w1a))
    w2a, w2b, edge_band, mix_rows = call(
        whiten_2,
        in_vmem(shaped(HALF2), shaped(HALF2), shaped(2), jax.ShapeDtypeStruct((3 * COLS, mix.shape[1]), BF)),
        [HBM, HBM, HBM],
        (z, band, mix),
        [
            pltpu.VMEM(((2 * HALF2 + 4) * BLK, COLS), BF),
            pltpu.VMEM((2 * HALF2, BLK, 3 * BLK), BF),
            pltpu.SemaphoreType.DMA((5 + len(CUTS2),)),
        ],
    )
    got2a, got2b = along_trait(w2a, w2b, pairs_a, pairs_b)

    def mixing(w_a, got_a, w_b, got_b):
        blocks = w_a.shape[0] // BLK
        outs = in_vmem(shaped(blocks), shaped(blocks), shaped(2 * blocks, F32))
        send_a, send_b, own = call(partial, outs, [VM] * 5, (w_a, got_a, w_b, got_b, mix_rows))
        return (own, *along_trait(send_a, send_b, pairs_b, pairs_a)), send_a

    (own1, far1a, far1b), after = mixing(w1a, got1a, w1b, got1b)
    got2a, got2b, _ = lax.optimization_barrier((got2a, got2b, after))
    (own2, far2a, far2b), after = mixing(w2a, got2a, w2b, got2b)
    far1a, far1b, _ = lax.optimization_barrier((far1a, far1b, after))
    (mixed1,) = call(combine_1, in_vmem(shaped(2 * HALF1 + 2)), [VM] * 3, (own1, far1a, far1b))
    mid_e, mid_o = along_rows(mixed1, pairs_o)
    far2a, far2b, _ = lax.optimization_barrier((far2a, far2b, mixed1))
    mixed2, edge_sums = call(
        combine_2, in_vmem(shaped(2 * HALF2 - 2), shaped(2, F32)), [VM] * 3, (own2, far2a, far2b)
    )
    rest_e, rest_o = along_rows(mixed2, pairs_open)
    starts_here = starts - (g * TB - TB)
    below = jnp.sum(starts_here[None, :] < jnp.array(LIMITS, jnp.int32)[:, None], axis=1, dtype=jnp.int32)
    plan = jnp.concatenate([starts_here, counts, below])
    ext, done, ld = call(
        impute_own,
        in_vmem(shaped(EXT), shaped(UB), jax.ShapeDtypeStruct(ld.shape, BF)),
        [SMEM] + [VM] * 2 + [HBM],
        (plan, mixed1, mixed2, ld),
        [pltpu.SemaphoreType.DMA((UB // UNROLL,))],
    )
    mid_o, mid_e, ext = lax.optimization_barrier((mid_o, mid_e, ext))
    (mixed3,) = call(
        finish_edge, in_vmem(shaped(2)), [VM] * 4, (edge_sums, edge_band, mid_o, mid_e)
    )
    edge_e, edge_o = along_rows(mixed3, pairs_o)
    ext, done = call(
        impute_near,
        in_vmem(shaped(EXT), shaped(UB)),
        [SMEM] + [VM] * 6,
        (plan, mixed3, mid_o, mid_e, ld, ext, done),
        (),
        {5: 0, 6: 1},
    )
    _, _, out = call(
        impute_far,
        in_vmem(shaped(EXT), shaped(UB)) + [(shaped(UB), HBM)],
        [SMEM] + [VM] * 7,
        (plan, rest_o, rest_e, edge_o, edge_e, ld, ext, done),
        [pltpu.SemaphoreType.DMA((UB // UNROLL,))],
        {6: 0, 7: 1},
    )
    return out


def solution(mesh):
    in_specs = (
        P(ROWS, "trait"),
        P(ROWS, None, None),
        P(ROWS, None, None),
        P(),
        P(ROWS),
        P(ROWS),
    )
    return jax.shard_map(on_device, mesh=mesh, in_specs=in_specs, out_specs=P(ROWS, "trait"), check_vma=False)
```

```python
import jax
import jax.numpy as jnp
from jax import lax
from jax.experimental import pallas as pl
from jax.experimental.pallas import tpu as pltpu
from jax.sharding import PartitionSpec as P

BLK = 128
WIN = 4
COLS = 128
TB = 32
UB = 64
ZERO = 3 * TB
EXT = ZERO + 1
UNROLL = 8
BF = jnp.bfloat16
F32 = jnp.float32
ROWS = ("sec", "var")
HBM = pl.BlockSpec(memory_space=pltpu.HBM)
SMEM = pl.BlockSpec(memory_space=pltpu.SMEM)
VM = pl.BlockSpec(memory_space=pltpu.VMEM)
PARAMS = pltpu.CompilerParams(vmem_limit_bytes=16 * 1024 * 1024)
MID = 9
MID_END = TB - MID
HALF1 = (MID_END - MID) // 2
HALF2 = MID


def shaped(blocks, dtype=BF):
    return jax.ShapeDtypeStruct((blocks * BLK, COLS), dtype)


def dot(left, right):
    return jnp.dot(left, right, preferred_element_type=F32)


def at(block, blocks=1):
    start = block * BLK
    return pl.ds(start if isinstance(start, int) else pl.multiple_of(start, BLK), blocks * BLK)


def copy_all(pairs, sems, first=0):
    copies = [pltpu.make_async_copy(a, b, sems.at[first + k]) for k, (a, b) in enumerate(pairs)]
    for copy in copies:
        copy.start()
    return copies


def pieces(blocks, most):
    return [(k, min(most, blocks - k)) for k in range(0, blocks, most)]


CUTS1 = pieces(2 * HALF1, 7)
CUTS2 = [(side, k, n) for side in range(2) for k, n in pieces(HALF2, 5)]


def place():
    t = lax.axis_index("trait")
    return t, t ^ 1, 3 - t


def whiten_1(z, band, w_a, w_b, zs, bs, sems):
    zcopy = copy_all([(z.at[at(MID - 1, 2 * HALF1 + 2)], zs)], sems)
    bands = copy_all([(band.at[pl.ds(MID + k, n)], bs.at[pl.ds(k, n)]) for k, n in CUTS1], sems, 1)
    edges = [(z.at[at(0)], w_a.at[at(HALF1)]), (z.at[at(TB - 1)], w_b.at[at(HALF1)])]
    edges = copy_all(edges, sems, 1 + len(CUTS1))
    zcopy[0].wait()
    for (k, n), copy in zip(CUTS1, bands):
        copy.wait()
        for i in range(k, k + n):
            w = w_a if i < HALF1 else w_b
            w[at(i % HALF1), :] = dot(bs[i], zs[at(i, 3), :]).astype(BF)
    for copy in edges:
        copy.wait()


def whiten_2(z, band, mix, w_a, w_b, edge_band, mix_rows, zs, bs, sems):
    zcopies = copy_all(
        [
            (z.at[at(0, HALF2 + 1)], zs.at[at(1, HALF2 + 1)]),
            (z.at[at(MID_END - 1, HALF2 + 1)], zs.at[at(HALF2 + 2, HALF2 + 1)]),
        ],
        sems,
    )
    bands = copy_all(
        [(band.at[pl.ds(side * MID_END + k, n)], bs.at[pl.ds(side * HALF2 + k, n)]) for side, k, n in CUTS2], sems, 2
    )
    parts = copy_all([(mix.at[at(row)], mix_rows.at[at(k)]) for k, row in enumerate(place())], sems, 2 + len(CUTS2))
    zs[at(0), :] = jnp.zeros((BLK, COLS), BF)
    zs[at(2 * HALF2 + 3), :] = jnp.zeros((BLK, COLS), BF)
    for (side, k, n), copy in zip(CUTS2, bands):
        if k == 0:
            zcopies[side].wait()
        copy.wait()
        for i in range(k, k + n):
            rows = dot(bs[side * HALF2 + i], zs[at(side * (HALF2 + 2) + i, 3), :])
            (w_a, w_b)[side][at(i), :] = rows.astype(BF)
    edge_band[at(0), :] = bs[0, :, pl.ds(0, BLK)]
    edge_band[at(1), :] = bs[2 * HALF2 - 1, :, pl.ds(2 * BLK, BLK)]
    for copy in parts:
        copy.wait()


def partial(w_a, got_a, w_b, got_b, mix_rows, send_a, send_b, own):
    here = place()
    rows = w_a.shape[0]
    for k, (w, got, send) in enumerate(((w_a, got_a, send_a), (w_b, got_b, send_b))):
        columns = (at(here[0]), at(here[2 - k]))
        weights = [
            jnp.concatenate([mix_rows[at(row), column] for column in columns], axis=1) for row in (0, 1 + k)
        ]
        both = dot(w[...], weights[0]) + dot(got[...], weights[1])
        own[pl.ds(k * rows, rows), :] = both[:, :COLS]
        send[...] = both[:, COLS:].astype(BF)


def combine_1(own, far_a, far_b, out):
    for k, far in enumerate((far_a, far_b)):
        rows = (own[at(k * (HALF1 + 1), HALF1 + 1), :] + far[...].astype(F32)).astype(BF)
        out[at(k * HALF1, HALF1), :] = rows[: HALF1 * BLK]
        out[at(2 * HALF1 + k), :] = rows[HALF1 * BLK :]


def combine_2(own, far_a, far_b, out, edge):
    inner = HALF2 - 1
    edge[at(0), :] = own[at(0), :] + far_a[at(0), :].astype(F32)
    out[at(0, inner), :] = (own[at(1, inner), :] + far_a[at(1, inner), :].astype(F32)).astype(BF)
    out[at(inner, inner), :] = (own[at(HALF2, inner), :] + far_b[at(0, inner), :].astype(F32)).astype(BF)
    edge[at(1), :] = own[at(2 * HALF2 - 1), :] + far_b[at(inner), :].astype(F32)


def finish_edge(edge, edge_band, got_o, got_e, out):
    g = lax.axis_index(ROWS)
    odd = g % 2 == 1
    nothing = jnp.zeros((BLK, COLS), BF)
    from_left = jnp.where(odd, got_e[at(2 * HALF1 + 1), :], got_o[at(2 * HALF1 + 1), :])
    from_right = jnp.where(odd, got_o[at(2 * HALF1), :], got_e[at(2 * HALF1), :])
    from_left = jnp.where(g == 0, nothing, from_left)
    from_right = jnp.where(g == lax.axis_size(ROWS) - 1, nothing, from_right)
    for k, rows in enumerate((from_left, from_right)):
        out[at(k), :] = (edge[at(k), :] + dot(edge_band[at(k), :], rows)).astype(BF)


def on_ranges(ranges, plan, ld, ext, out, ready=None, send=None):
    total = 0
    parts = []
    for low, high in ranges:
        parts.append((total, low))
        total = total + high - low

    def window_of(n):
        u = n + parts[0][1]
        for before, low in parts[1:]:
            u = jnp.where(n >= before, n - before + low, u)
        return u

    def several(k, carry):
        if ready is not None:
            ready(k)
        for i in range(UNROLL):
            u = window_of(jnp.minimum(UNROLL * k + i, total - 1))
            first = jnp.clip(plan[u], 0, 3 * TB - 1)
            have = plan[UB + u]
            window = [ext[at(jnp.where(s < have, jnp.minimum(first + s, ZERO), ZERO)), :] for s in range(WIN)]
            out[at(u), :] = dot(ld[u], jnp.concatenate(window, axis=0)).astype(BF)
        if send is None:
            return carry
        after = UNROLL * (k + 1)
        complete = jnp.where(after < total, window_of(after), UB) // UNROLL
        lax.fori_loop(carry, complete, send, 0)
        return jnp.maximum(carry, complete)

    return lax.fori_loop(0, (total + UNROLL - 1) // UNROLL, several, 0)


def move(ext, block, source, first, blocks):
    ext[at(block, blocks), :] = source[at(first, blocks), :]


LIMITS = (
    MID,
    MID_END - WIN + 1,
    TB,
    TB + 1,
    2 * TB - WIN,
    2 * TB - WIN + 1,
    2 * TB + MID,
    2 * TB + MID_END - WIN + 1,
)


def impute_own(plan, mid, rest, ld, ext, out, ld_here, sems):
    inner = HALF2 - 1
    low, high = plan[2 * UB + 3], plan[2 * UB + 4]
    groups = (high - low + UNROLL - 1) // UNROLL

    def load(k):
        part = pl.ds(pl.multiple_of((low // UNROLL + k) % (UB // UNROLL) * UNROLL, UNROLL), UNROLL)
        return pltpu.make_async_copy(ld.at[part], ld_here.at[part], sems.at[k])

    def ready(k):
        @pl.when(k + 1 < UB // UNROLL)
        def _():
            load(k + 1).wait()

    def rest_ready(k, carry):
        load(k).wait()
        return carry

    for k in range(UB // UNROLL):
        load(k).start()
    move(ext, TB + 1, rest, 0, inner)
    move(ext, TB + MID, mid, 0, 2 * HALF1)
    move(ext, TB + MID_END, rest, inner, inner)
    ext[at(ZERO), :] = jnp.zeros((BLK, COLS), BF)
    load(0).wait()
    on_ranges([(low, high)], plan, ld_here, ext, out, ready)
    lax.fori_loop(groups + 1, UB // UNROLL, rest_ready, 0)


def impute_near(plan, edge, mid_o, mid_e, ld, before, done, ext, out):
    move(ext, TB, edge, 0, 1)
    move(ext, 2 * TB - 1, edge, 1, 1)
    move(ext, 2 * TB * (1 - lax.axis_index(ROWS) % 2) + MID, mid_e, 0, 2 * HALF1)
    move(ext, 2 * TB * (lax.axis_index(ROWS) % 2) + MID, mid_o, 0, 2 * HALF1)
    ranges = [(plan[2 * UB + k], plan[2 * UB + k + 1]) for k in (0, 2, 4, 6)]
    on_ranges(ranges, plan, ld, ext, out)


def impute_far(plan, rest_o, rest_e, edge_o, edge_e, ld, before, done, ext, rows, out, sems):
    inner = HALF2 - 1
    for base, rest, edge in ((2 * TB * (1 - lax.axis_index(ROWS) % 2), rest_e, edge_e), (2 * TB * (lax.axis_index(ROWS) % 2), rest_o, edge_o)):
        move(ext, base, edge, 0, 1)
        move(ext, base + 1, rest, 0, inner)
        move(ext, base + MID_END, rest, inner, inner)
        move(ext, base + TB - 1, edge, 1, 1)
    ranges = [(0, plan[2 * UB + 0]), (plan[2 * UB + 1], plan[2 * UB + 2]), (plan[2 * UB + 5], plan[2 * UB + 6]), (plan[2 * UB + 7], UB)]

    def leave(k):
        part = at(k * UNROLL, UNROLL)
        return pltpu.make_async_copy(rows.at[part], out.at[part], sems.at[k])

    def send(k, carry):
        leave(k).start()
        return carry

    sent = on_ranges(ranges, plan, ld, ext, rows, send=send)
    lax.fori_loop(sent, UB // UNROLL, send, 0)
    for k in range(UB // UNROLL):
        leave(k).wait()


def call(kernel, outs, ins, args, scratch=(), aliases=None):
    return pl.pallas_call(
        kernel,
        name=kernel.__name__,
        out_shape=tuple(shape for shape, _ in outs),
        in_specs=ins,
        out_specs=tuple(spec for _, spec in outs),
        scratch_shapes=list(scratch),
        input_output_aliases=aliases or {},
        compiler_params=PARAMS,
    )(*args)


def in_vmem(*shapes):
    return [(shape, VM) for shape in shapes]


def on_device(z, band, ld, mix, starts, counts):
    g = lax.axis_index(ROWS)
    owners = lax.axis_size(ROWS)
    pairs_a = [(i, i ^ 1) for i in range(4)]
    pairs_b = [(i, 3 - i) for i in range(4)]
    pairs_e = [(i, i ^ 1) for i in range(owners)]
    pairs_o = [(i, (i + 1) % owners if i % 2 else (i - 1) % owners) for i in range(owners)]

    pairs_open = [(i, min(i + 1, owners - 1) if i % 2 else max(i - 1, 0)) for i in range(owners)]

    def along_trait(x, y, pairs_x, pairs_y):
        return lax.ppermute(x, "trait", pairs_x), lax.ppermute(y, "trait", pairs_y)

    def along_rows(x, pairs):
        other = lax.ppermute(x, ROWS, pairs)
        return lax.ppermute(x, ROWS, pairs_e), other

    z, band, mix, ld = (pltpu.with_memory_space_constraint(x, pltpu.HBM) for x in (z, band, mix, ld))
    w1a, w1b = call(
        whiten_1,
        in_vmem(shaped(HALF1 + 1), shaped(HALF1 + 1)),
        [HBM, HBM],
        (z, band),
        [
            pltpu.VMEM(((2 * HALF1 + 2) * BLK, COLS), BF),
            pltpu.VMEM((2 * HALF1, BLK, 3 * BLK), BF),
            pltpu.SemaphoreType.DMA((3 + len(CUTS1),)),
        ],
    )
    got1a, got1b = along_trait(w1a, w1b, pairs_a, pairs_b)
    z, _ = lax.optimization_barrier((z, w1a))
    w2a, w2b, edge_band, mix_rows = call(
        whiten_2,
        in_vmem(shaped(HALF2), shaped(HALF2), shaped(2), jax.ShapeDtypeStruct((3 * COLS, mix.shape[1]), BF)),
        [HBM, HBM, HBM],
        (z, band, mix),
        [
            pltpu.VMEM(((2 * HALF2 + 4) * BLK, COLS), BF),
            pltpu.VMEM((2 * HALF2, BLK, 3 * BLK), BF),
            pltpu.SemaphoreType.DMA((5 + len(CUTS2),)),
        ],
    )
    got2a, got2b = along_trait(w2a, w2b, pairs_a, pairs_b)

    def mixing(w_a, got_a, w_b, got_b):
        blocks = w_a.shape[0] // BLK
        outs = in_vmem(shaped(blocks), shaped(blocks), shaped(2 * blocks, F32))
        send_a, send_b, own = call(partial, outs, [VM] * 5, (w_a, got_a, w_b, got_b, mix_rows))
        return (own, *along_trait(send_a, send_b, pairs_b, pairs_a)), send_a

    (own1, far1a, far1b), after = mixing(w1a, got1a, w1b, got1b)
    got2a, got2b, _ = lax.optimization_barrier((got2a, got2b, after))
    (own2, far2a, far2b), after = mixing(w2a, got2a, w2b, got2b)
    far1a, far1b, _ = lax.optimization_barrier((far1a, far1b, after))
    (mixed1,) = call(combine_1, in_vmem(shaped(2 * HALF1 + 2)), [VM] * 3, (own1, far1a, far1b))
    mid_e, mid_o = along_rows(mixed1, pairs_o)
    far2a, far2b, _ = lax.optimization_barrier((far2a, far2b, mixed1))
    mixed2, edge_sums = call(
        combine_2, in_vmem(shaped(2 * HALF2 - 2), shaped(2, F32)), [VM] * 3, (own2, far2a, far2b)
    )
    rest_e, rest_o = along_rows(mixed2, pairs_open)
    starts_here = starts - (g * TB - TB)
    below = jnp.sum(starts_here[None, :] < jnp.array(LIMITS, jnp.int32)[:, None], axis=1, dtype=jnp.int32)
    plan = jnp.concatenate([starts_here, counts, below])
    ext, done, ld = call(
        impute_own,
        in_vmem(shaped(EXT), shaped(UB), jax.ShapeDtypeStruct(ld.shape, BF)),
        [SMEM] + [VM] * 2 + [HBM],
        (plan, mixed1, mixed2, ld),
        [pltpu.SemaphoreType.DMA((UB // UNROLL,))],
    )
    mid_o, mid_e, ext = lax.optimization_barrier((mid_o, mid_e, ext))
    (mixed3,) = call(
        finish_edge, in_vmem(shaped(2)), [VM] * 4, (edge_sums, edge_band, mid_o, mid_e)
    )
    edge_e, edge_o = along_rows(mixed3, pairs_o)
    ext, done = call(
        impute_near,
        in_vmem(shaped(EXT), shaped(UB)),
        [SMEM] + [VM] * 6,
        (plan, mixed3, mid_o, mid_e, ld, ext, done),
        (),
        {5: 0, 6: 1},
    )
    _, _, out = call(
        impute_far,
        in_vmem(shaped(EXT), shaped(UB)) + [(shaped(UB), HBM)],
        [SMEM] + [VM] * 7,
        (plan, rest_o, rest_e, edge_o, edge_e, ld, ext, done),
        [pltpu.SemaphoreType.DMA((UB // UNROLL,))],
        {6: 0, 7: 1},
    )
    return out


def solution(mesh):
    in_specs = (
        P(ROWS, "trait"),
        P(ROWS, None, None),
        P(ROWS, None, None),
        P(),
        P(ROWS),
        P(ROWS),
    )
    return jax.shard_map(on_device, mesh=mesh, in_specs=in_specs, out_specs=P(ROWS, "trait"), check_vma=False)
```
